32 devices in a mesh: grp: 2 (over x), gx: 8 (over z, y), gy: 2 (over core).
Axes of the slice: x: 2, y: 2, z: 4, core: 2. Of those that a mesh axis runs over, the one named last changes fastest.
Arguments:
- loaded_fields: bfloat16 [2, 32, 16, 128], P(None, ('grp', 'gx'), 'gy'), parts along dimension 1, may hold values from -6 to 6
- brick_home: int32 [16], P('grp'), parts along dimension 0, may hold values from 0 to 7, each once
- liquid_mask: int32 [32, 16, 128], P(('grp', 'gx'), 'gy'), parts along dimension 0, may hold values 0 or 1
- density_class: int32 [32, 16, 128], P(('grp', 'gx'), 'gy'), parts along dimension 0, may hold values from 0 to 3
- inverse_density: float32 [4], replicated, may hold values from 0.25 to 4
- conv_a: bfloat16 [27, 64, 3], replicated, may hold values from -0.625 to 0.625
- bias_a: float32 [64], replicated, may hold values from -3 to 3
- conv_b: bfloat16 [27, 64, 64], replicated, may hold values from -0.15625 to 0.15625
- bias_b: float32 [64], replicated, may hold values from -3 to 3
- conv_c: bfloat16 [27, 64, 64], replicated, may hold values from -0.15625 to 0.15625
- bias_c: float32 [64], replicated, may hold values from -3 to 3
- head_weight: bfloat16 [64], replicated, may hold values from -0.75 to 0.75
- head_bias: float32 [1], replicated, may hold values from -3 to 3
Outputs:
- pressure: float32 [32, 16, 128], P(('grp', 'gx'), 'gy'), parts along dimension 0
- loss: float32 [2], P('grp'), parts along dimension 0
- grad_conv_a: float32 [54, 64, 3], P('grp'), parts along dimension 0
- grad_bias_a: float32 [128], P('grp'), parts along dimension 0
- grad_conv_b: float32 [54, 64, 64], P('grp'), parts along dimension 0
- grad_bias_b: float32 [128], P('grp'), parts along dimension 0
- grad_conv_c: float32 [54, 64, 64], P('grp'), parts along dimension 0
- grad_bias_c: float32 [128], P('grp'), parts along dimension 0
- grad_head_weight: float32 [128], P('grp'), parts along dimension 0
The draws below stay inside these ranges and needn't reach their ends.
There are 2 independent parts, one for each index of `grp`. The reference program is written for one: setup_inputs(seed, part) draws one part's arguments, and reference() takes and returns one part's arrays. A program takes and returns all parts, laid end to end along the dimension named above; an argument that names none is the same for every part. Nothing has to cross between parts.
Inputs may be any that keep to these rules, and one draw needn't show every extreme that they name: `brick_home`: a permutation of 0 to 7.
All inputs are finite; a program needn't handle non-finite values. No bound on the sum of `liquid_mask` on one device may be relied on, other than what follows from the above.
Results may differ from the reference program's by a relative error of at most 0.0041.
The reference program's roundings to bfloat16 on the way count: a program that leaves them out, or rounds other values in their place, can miss the bound.
Values may be sent and summed in bfloat16 or wider, within the bound.
No kernel may reach another device: no remote copies, remote signals or barrier semaphores. Data moves between devices by JAX's collectives and lax.ppermute only.
A program may use at most 64 MiB of HBM per device.

```python
import math
import jax
import jax.numpy as jnp
from jax import lax

HID = 64
CIN = 3
NCLASS = 4
CX = 2
NZ = 128
NX = 16
NY = 16
N_GX = 8


def place_ends(entries, key, least, largest):
    spot = [jax.random.randint(jax.random.fold_in(key, axis), (), 0, length) for axis, length in enumerate(entries.shape)]
    main_axis = entries.shape.index(max(entries.shape))
    beside = spot[:main_axis] + [(spot[main_axis] + 1) % entries.shape[main_axis]] + spot[main_axis + 1:]
    return entries.at[tuple(spot)].set(least).at[tuple(beside)].set(largest)


def levels(key, shape, cuts, least, largest):
    def one(axis_at, parts):
        draws = jax.random.uniform(jax.random.fold_in(jax.random.fold_in(key, 6), axis_at), (parts,), jnp.float32, least / len(cuts), largest / len(cuts))
        return jnp.repeat(jnp.exp(draws), shape[axis_at] // parts).reshape((-1,) + (1,) * (len(shape) - axis_at - 1))

    gain = one(*cuts[0])
    for cut in cuts[1:]:
        gain = gain * one(*cut)
    return gain


def bell_draw(own_key, extent, deviation, reach, cuts=(), kind=jnp.bfloat16):
    level = levels(own_key, extent, cuts, -0.22, 0.18) if cuts else 1.0
    drawn = jax.random.normal(own_key, extent, jnp.float32) * deviation * level
    return jnp.minimum(jnp.maximum(drawn, -reach), reach).astype(kind)


def setup_inputs(seed: int = 0, part: int = 0) -> dict:
    key_of = jax.random.split(jax.random.key(seed), 14)
    own_keys = jax.random.split(jax.random.fold_in(key_of[13], part), 14)
    loaded_fields = bell_draw(own_keys[0], (2, NX, NY, NZ), 1.0, 6.0, ((1, 8), (2, 2)))
    brick_home = jax.random.permutation(own_keys[1], N_GX).astype(jnp.int32)
    liquid_mask = place_ends((jax.random.randint(own_keys[2], (NX, NY, NZ), 0, 4) < 3).astype(jnp.int32), jax.random.fold_in(own_keys[2], 1), 0, 1)
    density_class = place_ends(jax.random.randint(own_keys[3], (NX, NY, NZ), 0, NCLASS), jax.random.fold_in(own_keys[3], 1), 0, NCLASS - 1).astype(jnp.int32)
    inverse_density = jnp.clip(jnp.exp(jax.random.uniform(key_of[4], (NCLASS,), jnp.float32, math.log(0.25), math.log(4.0))), 0.25, 4.0)
    conv_a = bell_draw(key_of[5], (27, HID, CIN), (27 * CIN) ** -0.5, 0.625)
    bias_a = bell_draw(key_of[6], (HID,), 0.5, 3.0, (), jnp.float32)
    conv_b = bell_draw(key_of[7], (27, HID, HID), (27 * HID) ** -0.5, 0.15625)
    bias_b = bell_draw(key_of[8], (HID,), 0.5, 3.0, (), jnp.float32)
    conv_c = bell_draw(key_of[9], (27, HID, HID), (27 * HID) ** -0.5, 0.15625)
    bias_c = bell_draw(key_of[10], (HID,), 0.5, 3.0, (), jnp.float32)
    head_weight = bell_draw(key_of[11], (HID,), HID ** -0.5, 0.75)
    head_bias = bell_draw(key_of[12], (1,), 0.5, 3.0, (), jnp.float32)
    return {"loaded_fields": loaded_fields, "brick_home": brick_home, "liquid_mask": liquid_mask, "density_class": density_class, "inverse_density": inverse_density, "conv_a": conv_a, "bias_a": bias_a, "conv_b": conv_b, "bias_b": bias_b, "conv_c": conv_c, "bias_c": bias_c, "head_weight": head_weight, "head_bias": head_bias}


PRECISE = lax.Precision.HIGHEST
TAP_LIST = [(first, second, third) for first in range(3) for second in range(3) for third in range(3)]
NEIGHBOUR_LIST = [(2, 1, 1), (0, 1, 1), (1, 2, 1), (1, 0, 1), (1, 1, 2), (1, 1, 0)]

def pad_space(values):
    widths = [(0, 0)] * (values.ndim - 3) + [(1, 1)] * 3
    return jnp.pad(values, widths)

def conv_forward(inputs, weights):
    padded = pad_space(inputs)
    size_x, size_y, size_z = inputs.shape[1:]
    total = jnp.zeros((weights.shape[1], size_x, size_y, size_z), inputs.dtype)
    for tap_index, (first, second, third) in enumerate(TAP_LIST):
        window = padded[:, first:first + size_x, second:second + size_y, third:third + size_z]
        total = total + jnp.einsum('oi,ixyz->oxyz', weights[tap_index], window, precision=PRECISE)
    return total

def conv_weight_grad(inputs, grads):
    padded = pad_space(inputs)
    size_x, size_y, size_z = inputs.shape[1:]
    parts_list = []
    for first, second, third in TAP_LIST:
        window = padded[:, first:first + size_x, second:second + size_y, third:third + size_z]
        parts_list.append(jnp.einsum('oxyz,ixyz->oi', grads, window, precision=PRECISE))
    return jnp.stack(parts_list)

def conv_input_grad(grads, weights):
    padded = pad_space(grads)
    size_x, size_y, size_z = grads.shape[1:]
    total = jnp.zeros((weights.shape[2], size_x, size_y, size_z), grads.dtype)
    for tap_index, (first, second, third) in enumerate(TAP_LIST):
        window = padded[:, 2 - first:2 - first + size_x, 2 - second:2 - second + size_y, 2 - third:2 - third + size_z]
        total = total + jnp.einsum('oi,oxyz->ixyz', weights[tap_index], window, precision=PRECISE)
    return total

def silu_slope(values):
    sigma = jax.nn.sigmoid(values)
    return sigma * (1.0 + values * (1.0 - sigma))

def face_coefs(scaled, liquid):
    padded_scaled = pad_space(scaled)
    padded_liquid = pad_space(liquid)
    size_x, size_y, size_z = scaled.shape
    result = []
    for first, second, third in NEIGHBOUR_LIST:
        near_scaled = padded_scaled[first:first + size_x, second:second + size_y, third:third + size_z]
        near_liquid = padded_liquid[first:first + size_x, second:second + size_y, third:third + size_z]
        result.append(0.5 * (scaled * near_liquid + near_scaled * liquid))
    return result

def apply_operator(values, coefs):
    padded = pad_space(values)
    size_x, size_y, size_z = values.shape
    total = jnp.zeros_like(values)
    for coef, (first, second, third) in zip(coefs, NEIGHBOUR_LIST):
        near = padded[first:first + size_x, second:second + size_y, third:third + size_z]
        total = total + coef * (near - values)
    return total

def reference(loaded_fields, brick_home, liquid_mask, density_class, inverse_density, conv_a, bias_a, conv_b, bias_b, conv_c, bias_c, head_weight, head_bias):
    slots = jnp.arange(N_GX, dtype=jnp.int32)
    inverse = lax.optimization_barrier(jnp.sum(jnp.where(brick_home[None, :] == slots[:, None], slots[None, :], 0), axis=1)).astype(jnp.int32)
    fields = loaded_fields.reshape(2, N_GX, CX, NY, NZ)[:, inverse].reshape(2, NX, NY, NZ)
    liquid = liquid_mask.astype(jnp.float32)
    classes = jnp.arange(NCLASS, dtype=jnp.int32)
    scale = lax.optimization_barrier(jnp.sum(jnp.where(density_class[None] == classes[:, None, None, None], inverse_density[:, None, None, None], 0.0), axis=0))
    inputs = jnp.concatenate([fields, liquid.astype(jnp.bfloat16)[None]], axis=0)
    pre_one = conv_forward(inputs.astype(jnp.float32), conv_a.astype(jnp.float32)) + bias_a[:, None, None, None]
    act_one = (jax.nn.silu(pre_one) * liquid).astype(jnp.bfloat16)
    pre_two = conv_forward(act_one.astype(jnp.float32), conv_b.astype(jnp.float32)) + bias_b[:, None, None, None]
    act_two = (jax.nn.silu(pre_two) * liquid).astype(jnp.bfloat16)
    pre_three = conv_forward(act_two.astype(jnp.float32), conv_c.astype(jnp.float32)) + bias_c[:, None, None, None]
    act_three = (jax.nn.silu(pre_three) * liquid).astype(jnp.bfloat16)
    head_float = head_weight.astype(jnp.float32)
    pressure = liquid * (jnp.einsum('o,oxyz->xyz', head_float, act_three.astype(jnp.float32), precision=PRECISE) + head_bias[0])
    coefs = face_coefs(scale * liquid, liquid)
    residual = apply_operator(pressure, coefs) - liquid * fields[1].astype(jnp.float32)
    cells = NX * NY * NZ
    loss = jnp.sum(residual * residual) / cells
    grad_score = liquid * apply_operator(2.0 * residual / cells, coefs)
    grad_head_weight = jnp.einsum('xyz,oxyz->o', grad_score, act_three.astype(jnp.float32), precision=PRECISE)
    grad_three = (grad_score[None] * head_float[:, None, None, None] * liquid * silu_slope(pre_three)).astype(jnp.bfloat16)
    grad_three_f = grad_three.astype(jnp.float32)
    grad_conv_c = conv_weight_grad(act_two.astype(jnp.float32), grad_three_f)
    grad_bias_c = lax.optimization_barrier(jnp.sum(grad_three_f, axis=(1, 2, 3)))
    back_two = conv_input_grad(grad_three_f, conv_c.astype(jnp.float32))
    grad_two = (back_two * liquid * silu_slope(pre_two)).astype(jnp.bfloat16)
    grad_two_f = grad_two.astype(jnp.float32)
    grad_conv_b = conv_weight_grad(act_one.astype(jnp.float32), grad_two_f)
    grad_bias_b = lax.optimization_barrier(jnp.sum(grad_two_f, axis=(1, 2, 3)))
    back_one = conv_input_grad(grad_two_f, conv_b.astype(jnp.float32))
    grad_one = (back_one * liquid * silu_slope(pre_one)).astype(jnp.bfloat16)
    grad_one_f = grad_one.astype(jnp.float32)
    grad_conv_a = conv_weight_grad(inputs.astype(jnp.float32), grad_one_f)
    grad_bias_a = lax.optimization_barrier(jnp.sum(grad_one_f, axis=(1, 2, 3)))
    return (pressure, loss.reshape(1), grad_conv_a, grad_bias_a, grad_conv_b, grad_bias_b, grad_conv_c, grad_bias_c, grad_head_weight)
```

```python
import functools

import jax
import jax.numpy as jnp
from jax import lax
from jax.experimental import pallas as pl
from jax.experimental.pallas import tpu as pltpu
from jax.sharding import PartitionSpec as P

F32 = jnp.float32
BF16 = jnp.bfloat16
AXES = ("gx", "gy")
HID = 64
NZ = 128
NY = 16
PLANES = 16
MID = 7
WROWS = 864
ROWS = 896


def shift_right(v):
    lane = lax.broadcasted_iota(jnp.int32, v.shape, v.ndim - 1)
    return jnp.where(lane == 0, 0.0, pltpu.roll(v, 1, v.ndim - 1))


def shift_left(v):
    lane = lax.broadcasted_iota(jnp.int32, v.shape, v.ndim - 1)
    return jnp.where(lane == NZ - 1, 0.0, pltpu.roll(v, NZ - 1, v.ndim - 1))


def dot_nn(a, b):
    return jnp.dot(a, b, preferred_element_type=F32)


def dot_nt(a, b):
    return lax.dot_general(a, b, (((1,), (1,)), ((), ())), preferred_element_type=F32)


def step_kernel(
    pos_ref,
    home_ref,
    invd_ref,
    hb_ref,
    gath_ref,
    wa_ref,
    wb_ref,
    wc_ref,
    wbt_ref,
    wct_ref,
    ba_ref,
    bb_ref,
    bc_ref,
    hw_ref,
    p_out,
    keep_ref,
    send_ref,
    inv_ref,
    x0s,
    liq,
    scl,
    f1,
    h1,
    h2,
    h3o,
    s1,
    s2,
    s3,
    pf,
    rs,
    gs,
    g3,
    g2,
    g1,
    gcat,
    hcat,
    acc,
    *,
    n_slots,
    cells,
):
    gx = pos_ref[0]
    gy = pos_ref[1]
    for s in range(n_slots):
        inv_ref[home_ref[s]] = s

    def zero_rims(ref):
        z = jnp.zeros(ref.shape[2:], ref.dtype)

        def body(i, c):
            ref[i, 0] = z
            ref[i, NY + 1] = z
            return c

        lax.fori_loop(0, ref.shape[0], body, 0)

    for ref in (x0s, h1, h2, g3, g2):
        zero_rims(ref)
    for ref in (liq, scl, pf, rs, f1):
        ref[...] = jnp.zeros(ref.shape, F32)

    def load_plane(X, c):
        xg = 2 * gx - MID + X
        ok = jnp.where((xg >= 0) & (xg < 2 * n_slots), 1.0, 0.0).astype(F32)
        xc = jnp.clip(xg, 0, 2 * n_slots - 1)
        home = xc // 2
        half = xc - 2 * home
        slot = inv_ref[home]
        for y in range(NY):
            fb = gath_ref[2 * slot + y // 8, half, y % 8].astype(F32) * ok
            mb = gath_ref[2 * home + y // 8, half, y % 8].astype(F32)
            lq = mb[2:3] * ok
            cl = mb[3:4]
            sc = jnp.zeros((1, NZ), F32)
            for k in range(4):
                sc = jnp.where(cl == k, invd_ref[k], sc)
            row4 = lax.broadcasted_iota(jnp.int32, (4, NZ), 0)
            base = jnp.where(row4 < 2, fb, jnp.where(row4 == 2, mb * ok, 0.0))
            k12 = jnp.concatenate(
                [shift_right(base), base, shift_left(base), jnp.zeros((4, NZ), F32)], axis=0
            )
            x0s[X, y + 1] = k12.astype(BF16)
            liq[X, y + 1 : y + 2, :] = lq
            scl[X, y + 1 : y + 2, :] = sc * lq
            f1[X, y + 1 : y + 2, :] = fb[1:2]
        return c

    lax.fori_loop(0, PLANES, load_plane, 0)

    def taps(src, X, y):
        out = []
        for a in range(3):
            for b in range(3):
                out.append(
                    jnp.concatenate([src[X + a - 1, y + b - 1], src[X + a - 1, y + b]], axis=1)
                )
        return jnp.concatenate(out, axis=0)

    def lane_taps(Y):
        res = []
        for k in range(2):
            part = Y[:, k * NZ : (k + 1) * NZ]
            res.append(
                part[HID : 2 * HID]
                + shift_right(part[:HID])
                + shift_left(part[2 * HID :])
            )
        return res

    def sweep(x_lo, x_n, ry, body):
        y_lo = gy * (8 - ry) + 1

        def plane(i, c):
            def pair(j, c2):
                body(x_lo + i, y_lo + 2 * j)
                return c2

            return lax.fori_loop(0, (8 + ry) // 2, pair, c)

        lax.fori_loop(0, x_n, plane, 0)

    def activate(z):
        sig = 0.5 * jnp.tanh(0.5 * z) + 0.5
        return z * sig, sig

    def slope_of(z, sig):
        return sig * (1.0 + z * (1.0 - sig))

    def layer1(X, y):
        Y = dot_nn(wa_ref[...], taps(x0s, X, y))
        for k in range(2):
            z = Y[:, k * NZ : (k + 1) * NZ] + ba_ref[...]
            m = liq[X, pl.ds(y + k, 1), :]
            act, sig = activate(z)
            h1[X, y + k] = (act * m).astype(BF16)

            @pl.when((X >= MID) & (X < MID + 2))
            def _():
                s1[X - MID, y + k] = slope_of(z, sig) * m

    sweep(MID - 6, 14, 6, layer1)

    def layer2(X, y):
        zs = lane_taps(dot_nn(wb_ref[...], taps(h1, X, y)))
        for k in range(2):
            z = zs[k] + bb_ref[...]
            m = liq[X, pl.ds(y + k, 1), :]
            act, sig = activate(z)
            h2[X, y + k] = (act * m).astype(BF16)

            @pl.when((X >= MID - 1) & (X < MID + 3))
            def _():
                s2[X - MID + 1, y + k] = slope_of(z, sig) * m

    sweep(MID - 5, 12, 6, layer2)

    def layer3(X, y):
        zs = lane_taps(dot_nn(wc_ref[...], taps(h2, X, y)))
        for k in range(2):
            z = zs[k] + bc_ref[...]
            m = liq[X, pl.ds(y + k, 1), :]
            act, sig = activate(z)
            h3 = (act * m).astype(BF16)
            score = jnp.sum(hw_ref[...] * h3.astype(F32), axis=0, keepdims=True)
            pf[X, pl.ds(y + k, 1), :] = m * (score + hb_ref[0])

            @pl.when((X >= MID - 2) & (X < MID + 4))
            def _():
                s3[X - MID + 2, y + k] = slope_of(z, sig) * m

            @pl.when((X >= MID) & (X < MID + 2))
            def _():
                h3o[X - MID, y + k] = h3

    sweep(MID - 4, 10, 4, layer3)

    def operator(val, X):
        v = val[X, 1 : NY + 1, :]
        s = scl[X, 1 : NY + 1, :]
        q = liq[X, 1 : NY + 1, :]

        def term(nv, ns, nq):
            return 0.5 * (s * nq + ns * q) * (nv - v)

        total = term(val[X + 1, 1 : NY + 1, :], scl[X + 1, 1 : NY + 1, :], liq[X + 1, 1 : NY + 1, :])
        total += term(val[X - 1, 1 : NY + 1, :], scl[X - 1, 1 : NY + 1, :], liq[X - 1, 1 : NY + 1, :])
        total += term(val[X, 2 : NY + 2, :], scl[X, 2 : NY + 2, :], liq[X, 2 : NY + 2, :])
        total += term(val[X, 0:NY, :], scl[X, 0:NY, :], liq[X, 0:NY, :])
        total += term(shift_left(v), shift_left(s), shift_left(q))
        total += term(shift_right(v), shift_right(s), shift_right(q))
        return total

    for X in range(MID - 3, MID + 5):
        rs[X, 1 : NY + 1, :] = (
            operator(pf, X) - liq[X, 1 : NY + 1, :] * f1[X, 1 : NY + 1, :]
        )
    own_y = pl.ds(pl.multiple_of(gy * 8, 8) + 1, 8)
    loss = jnp.zeros((8, NZ), F32)
    for k in range(2):
        p_out[k] = pf[MID + k, own_y, :]
        r = rs[MID + k, own_y, :]
        loss += r * r
    loss = jnp.sum(jnp.sum(loss, axis=0, keepdims=True), axis=1, keepdims=True) / cells
    for X in range(PLANES):
        rs[X] = rs[X] * (2.0 / cells)
    for X in range(MID - 2, MID + 4):
        gs[X - MID + 2, 1 : NY + 1, :] = liq[X, 1 : NY + 1, :] * operator(rs, X)

    def back3(X, y):
        for k in range(2):
            g = gs[X - MID + 2, pl.ds(y + k, 1), :]
            g3[X - MID + 2, y + k] = (g * hw_ref[...] * s3[X - MID + 2, y + k]).astype(BF16)

    sweep(MID - 2, 6, 2, back3)

    acc[...] = jnp.zeros(acc.shape, F32)
    y_own = gy * 8 + 1

    def head_grad(i, hacc):
        X = i // 8
        y = y_own + i - 8 * X
        return hacc + gs[X + 2, pl.ds(y, 1), :] * h3o[X, y].astype(F32)

    head = lax.fori_loop(0, 16, head_grad, jnp.zeros((HID, NZ), F32))

    def weight_grad(g_ref, g_off, h_ref, which):
        for i in range(16):
            X, dy = i // 8, i % 8
            y = y_own + dy
            g = g_ref[g_off + X, y].astype(F32)
            cols = slice(i * NZ, (i + 1) * NZ)
            gcat[0:HID, cols] = shift_left(g).astype(BF16)
            gcat[HID : 2 * HID, cols] = g.astype(BF16)
            gcat[2 * HID : 3 * HID, cols] = shift_right(g).astype(BF16)
            for a in range(3):
                for b in range(3):
                    k = 3 * a + b
                    hcat[k * HID : (k + 1) * HID, cols] = h_ref[MID + X + a - 1, y + b - 1]
        W = dot_nt(gcat[...], hcat[...])
        for a in range(3):
            for b in range(3):
                for e in range(3):
                    t = 9 * a + 3 * b + e
                    k = 3 * a + b
                    blk = W[e * HID : (e + 1) * HID, k * HID : (k + 1) * HID]
                    acc[which, t * 32 : (t + 1) * 32, 0:HID] = blk[:32]
                    acc[which, t * 32 : (t + 1) * 32, HID:NZ] = blk[32:]

    def lane_sum(g_ref, g_off):
        def body(i, c):
            X = i // 8
            return c + g_ref[g_off + X, y_own + i - 8 * X].astype(F32)

        return lax.fori_loop(0, 16, body, jnp.zeros((HID, NZ), F32))

    weight_grad(g3, 2, h2, 1)
    bias_c = lane_sum(g3, 2)

    def back2(X, y):
        bs = lane_taps(dot_nn(wct_ref[...], taps(g3, X - MID + 2, y)))
        for k in range(2):
            g2[X - MID + 1, y + k] = (bs[k] * s2[X - MID + 1, y + k]).astype(BF16)

    sweep(MID - 1, 4, 2, back2)
    weight_grad(g2, 1, h1, 0)
    bias_b = lane_sum(g2, 1)

    def back1(X, y):
        bs = lane_taps(dot_nn(wbt_ref[...], taps(g2, X - MID + 1, y)))
        for k in range(2):
            g1[X - MID, y + k] = (bs[k] * s1[X - MID, y + k]).astype(BF16)

    sweep(MID, 2, 0, back1)
    bias_a = lane_sum(g1, 0)

    for i in range(16):
        X, dy = i // 8, i % 8
        y = y_own + dy
        cols = slice(i * NZ, (i + 1) * NZ)
        gcat[0:HID, cols] = g1[X, y]
        for a in range(3):
            for b in range(3):
                k = 3 * a + b
                hcat[k * 16 : (k + 1) * 16, cols] = x0s[MID + X + a - 1, y + b - 1]
    A = dot_nt(hcat[0:144, :], gcat[0:HID, :])
    for k in range(8):
        blk = A[16 * k : 16 * k + 12]
        which, spot = k // 4, k % 4
        r0 = WROWS + 12 * (spot % 2)
        c0 = HID * (spot // 2)
        acc[which, r0 : r0 + 12, c0 : c0 + HID] = blk
    acc[1, WROWS + 24 : WROWS + 32, 0:HID] = A[128:136]
    acc[1, WROWS + 24 : WROWS + 28, HID:NZ] = A[136:140]
    sums = [
        jnp.sum(v, axis=1, keepdims=True).reshape(1, HID) for v in (bias_a, bias_b, bias_c, head)
    ]
    for j in range(2):
        pair = jnp.concatenate([sums[2 * j], sums[2 * j + 1]], axis=1)
        acc[0, WROWS + 24 + j : WROWS + 25 + j, :] = pair
    acc[0, WROWS + 26 : WROWS + 27, :] = jnp.broadcast_to(loss, (1, NZ))
    keep_ref[...] = acc[gy]
    send_ref[...] = acc[1 - gy]


def forward_lhs(w):
    w = w.reshape(3, 3, 3, HID, HID)
    return w.transpose(2, 3, 0, 1, 4).reshape(3 * HID, 9 * HID)


def backward_lhs(w):
    w = w.reshape(3, 3, 3, HID, HID)[::-1, ::-1, ::-1]
    return w.transpose(2, 4, 0, 1, 3).reshape(3 * HID, 9 * HID)


def first_lhs(w):
    w = w.reshape(9, 3, HID, 3)
    w = jnp.pad(w, ((0, 0), (0, 1), (0, 0), (0, 1)))
    w = w.transpose(2, 0, 1, 3).reshape(HID, 9, 16)
    return w.reshape(HID, 144)


def partner(value, bit, count):
    return lax.ppermute(value, AXES, [(i, i ^ bit) for i in range(count)])


def gather_all(block, me, count):
    value = block[None]
    bit = 1
    while bit < count:
        other = partner(value, bit, count)
        upper = (me & bit) != 0
        value = jnp.where(
            upper, jnp.concatenate([other, value]), jnp.concatenate([value, other])
        )
        bit *= 2
    return value


def on_device(
    loaded_fields,
    brick_home,
    liquid_mask,
    density_class,
    inverse_density,
    conv_a,
    bias_a,
    conv_b,
    bias_b,
    conv_c,
    bias_c,
    head_weight,
    head_bias,
):
    n_slots = lax.axis_size("gx")
    count = n_slots * lax.axis_size("gy")
    gx = lax.axis_index("gx")
    gy = lax.axis_index("gy")
    me = gx * 2 + gy
    block = jnp.stack(
        [
            loaded_fields[0],
            loaded_fields[1],
            liquid_mask.astype(BF16),
            density_class.astype(BF16),
        ],
        axis=2,
    )
    gath = gather_all(block, me, count)
    cells = 2 * n_slots * NY * NZ

    def wide(v):
        return jnp.broadcast_to(v.astype(F32)[:, None], (HID, NZ))

    smem = pl.BlockSpec(memory_space=pltpu.SMEM)
    vmem = pl.BlockSpec(memory_space=pltpu.VMEM)
    yy = NY + 2
    pressure, keep, send = pl.pallas_call(
        functools.partial(step_kernel, n_slots=n_slots, cells=cells),
        out_shape=(
            jax.ShapeDtypeStruct((2, 8, NZ), F32),
            jax.ShapeDtypeStruct((ROWS, NZ), F32),
            jax.ShapeDtypeStruct((ROWS, NZ), F32),
        ),
        in_specs=[smem] * 4 + [vmem] * 10,
        out_specs=(vmem, vmem, vmem),
        scratch_shapes=[
            pltpu.SMEM((n_slots,), jnp.int32),
            pltpu.VMEM((PLANES, yy, 16, NZ), BF16),
            pltpu.VMEM((PLANES, yy, NZ), F32),
            pltpu.VMEM((PLANES, yy, NZ), F32),
            pltpu.VMEM((PLANES, yy, NZ), F32),
            pltpu.VMEM((PLANES, yy, HID, NZ), BF16),
            pltpu.VMEM((PLANES, yy, HID, NZ), BF16),
            pltpu.VMEM((2, yy, HID, NZ), BF16),
            pltpu.VMEM((2, yy, HID, NZ), F32),
            pltpu.VMEM((4, yy, HID, NZ), F32),
            pltpu.VMEM((6, yy, HID, NZ), F32),
            pltpu.VMEM((PLANES, yy, NZ), F32),
            pltpu.VMEM((PLANES, yy, NZ), F32),
            pltpu.VMEM((6, yy, NZ), F32),
            pltpu.VMEM((6, yy, HID, NZ), BF16),
            pltpu.VMEM((4, yy, HID, NZ), BF16),
            pltpu.VMEM((2, yy, HID, NZ), BF16),
            pltpu.VMEM((3 * HID, 16 * NZ), BF16),
            pltpu.VMEM((9 * HID, 16 * NZ), BF16),
            pltpu.VMEM((2, ROWS, NZ), F32),
        ],
        compiler_params=pltpu.CompilerParams(vmem_limit_bytes=56 * 1024 * 1024),
        name="step",
    )(
        jnp.stack([gx, gy]).astype(jnp.int32),
        brick_home,
        inverse_density,
        head_bias,
        gath,
        first_lhs(conv_a),
        forward_lhs(conv_b),
        forward_lhs(conv_c),
        backward_lhs(conv_b),
        backward_lhs(conv_c),
        wide(bias_a),
        wide(bias_b),
        wide(bias_c),
        wide(head_weight),
    )

    def pack(v):
        return v

    del pack
    total = keep + partner(send, 1, count)
    bits = []
    bit = 2
    while bit < count:
        bits.append(bit)
        bit *= 2
    for bit in bits:
        half = total.shape[0] // 2
        upper = (me & bit) != 0
        low, high = total[:half], total[half:]
        got = partner(jnp.where(upper, low, high), bit, count)
        total = jnp.where(upper, high, low) + got
    for bit in bits[::-1]:
        other = partner(total, bit, count)
        upper = (me & bit) != 0
        total = jnp.where(
            upper, jnp.concatenate([other, total]), jnp.concatenate([total, other])
        )
    other = partner(total, 1, count)
    first = jnp.where(gy == 0, total, other)
    second = jnp.where(gy == 0, other, total)

    def weights(v):
        v = v[:WROWS].reshape(27, 32, 2, HID)
        return v.transpose(0, 2, 1, 3).reshape(27, HID, HID)

    def blocks(v):
        v = v[WROWS : WROWS + 24].reshape(2, 12, 2, HID)
        return v.transpose(2, 0, 1, 3).reshape(4, 12, HID)

    last = jnp.concatenate(
        [second[WROWS + 24 : WROWS + 32, :HID], second[WROWS + 24 : WROWS + 28, HID:]], axis=0
    )
    parts = jnp.concatenate([blocks(first), blocks(second), last[None]], axis=0)
    grad_a = parts.reshape(27, 4, HID)[:, :3].transpose(0, 2, 1)
    tail = first[WROWS + 24 : WROWS + 27]
    return (
        pressure,
        tail[2, :1],
        grad_a,
        tail[0, :HID],
        weights(first),
        tail[0, HID:],
        weights(second),
        tail[1, :HID],
        tail[1, HID:],
    )


def solution(mesh):
    grid = P(("grp", "gx"), "gy", None)
    part = P("grp")
    stack = P("grp", None, None)
    return jax.shard_map(
        on_device,
        mesh=mesh,
        in_specs=(P(None, ("grp", "gx"), "gy", None), part, grid, grid) + (P(),) * 9,
        out_specs=(grid, part, stack, part, stack, part, stack, part, part),
        check_vma=False,
    )
```

```python
import functools

import jax
import jax.numpy as jnp
from jax import lax
from jax.experimental import pallas as pl
from jax.experimental.pallas import tpu as pltpu
from jax.sharding import PartitionSpec as P

F32 = jnp.float32
BF16 = jnp.bfloat16
AXES = ("gx", "gy")
HID = 64
NZ = 128
NY = 16
YY = NY + 2
PLANES = 12
MID = 5
FRAME = 12
WROWS = 864
ROWS = 896
TAIL = 16
VMEM_LIMIT = 40 * 1024 * 1024


def shift_right(v):
    lane = lax.broadcasted_iota(jnp.int32, v.shape, v.ndim - 1)
    return jnp.where(lane == 0, 0.0, pltpu.roll(v, 1, v.ndim - 1))


def shift_left(v):
    lane = lax.broadcasted_iota(jnp.int32, v.shape, v.ndim - 1)
    return jnp.where(lane == NZ - 1, 0.0, pltpu.roll(v, NZ - 1, v.ndim - 1))


def dot_nn(a, b):
    return jnp.dot(a, b, preferred_element_type=F32)


def dot_nt(a, b):
    return lax.dot_general(a, b, (((1,), (1,)), ((), ())), preferred_element_type=F32)


def taps(src, X, y):
    out = []
    for a in range(3):
        for b in range(3):
            out.append(
                jnp.concatenate([src[X + a - 1, y + b - 1], src[X + a - 1, y + b]], axis=1)
            )
    return jnp.concatenate(out, axis=0)


def lane_taps(Y, k):
    part = Y[:, k * NZ : (k + 1) * NZ]
    return part[HID : 2 * HID] + shift_right(part[:HID]) + shift_left(part[2 * HID :])


def activate(z):
    sig = 0.5 * jnp.tanh(0.5 * z) + 0.5
    return z * sig, sig


def slope_of(z, sig):
    return sig * (1.0 + z * (1.0 - sig))


def lhs_kernel(wa_ref, wb_ref, wc_ref, fa, fb, fc, tb, tc):
    fa[...] = jnp.zeros(fa.shape, BF16)
    for k in range(9):
        for e in range(3):
            c = 16 * k + 4 * e
            fa[:, c : c + 3] = wa_ref[3 * k + e]
    for w, fwd, bwd in ((wb_ref, fb, tb), (wc_ref, fc, tc)):
        for e in range(3):
            rows = slice(e * HID, (e + 1) * HID)
            for k in range(0, 9, 2):
                c = k * HID
                lo = w[3 * k + e].astype(F32)
                blo = w[26 - (3 * k + e)].astype(F32)
                if k < 8:
                    hi = w[3 * k + 3 + e].astype(F32)
                    bhi = w[26 - (3 * k + 3 + e)].astype(F32)
                    fwd[rows, c : c + 2 * HID] = jnp.concatenate([lo, hi], axis=1).astype(BF16)
                    both = jnp.concatenate([blo, bhi], axis=0)
                    bwd[rows, c : c + 2 * HID] = both.T.astype(BF16)
                else:
                    fwd[rows, c : c + HID] = lo.astype(BF16)
                    both = jnp.concatenate([blo, blo], axis=0)
                    bwd[rows, c : c + HID] = both.T[:, :HID].astype(BF16)


def forward_kernel(
    pos_ref,
    home_ref,
    invd_ref,
    hb_ref,
    gath_ref,
    wa_ref,
    wb_ref,
    wc_ref,
    ba_ref,
    bb_ref,
    bc_ref,
    hw_ref,
    p_out,
    gs_out,
    loss_out,
    head_out,
    x0_out,
    h1_out,
    h2_out,
    s1,
    s2,
    s3,
    inv_ref,
    x0s,
    liq,
    scl,
    f1,
    h1,
    h2,
    h3o,
    pf,
    rs,
    *,
    n_slots,
    cells,
):
    gx = pos_ref[0]
    gy = pos_ref[1]
    for s in range(n_slots):
        inv_ref[home_ref[s]] = s

    for ref in (x0s, h1, h2):
        z = jnp.zeros(ref.shape[2:], ref.dtype)
        for X in range(PLANES):
            ref[X, 0] = z
            ref[X, NY + 1] = z
    for ref in (liq, scl, f1, pf, rs):
        for X in range(PLANES):
            ref[X] = jnp.zeros((YY, NZ), F32)

    def load_plane(X, c):
        xg = 2 * gx - MID + X
        ok = jnp.where((xg >= 0) & (xg < 2 * n_slots), 1.0, 0.0).astype(F32)
        xc = jnp.clip(xg, 0, 2 * n_slots - 1)
        home = xc // 2
        half = xc - 2 * home
        slot = inv_ref[home]
        row4 = lax.broadcasted_iota(jnp.int32, (4, NZ), 0)
        for y in range(NY):
            fb = gath_ref[2 * slot + y // 8, half, y % 8].astype(F32) * ok
            mb = gath_ref[2 * home + y // 8, half, y % 8].astype(F32)
            lq = mb[2:3] * ok
            cl = mb[3:4]
            sc = jnp.zeros((1, NZ), F32)
            for k in range(4):
                sc = jnp.where(cl == k, invd_ref[k], sc)
            base = jnp.where(row4 < 2, fb, jnp.where(row4 == 2, mb * ok, 0.0))
            k12 = jnp.concatenate(
                [shift_right(base), base, shift_left(base), jnp.zeros((4, NZ), F32)], axis=0
            )
            x0s[X, y + 1] = k12.astype(BF16)
            liq[X, y + 1 : y + 2, :] = lq
            scl[X, y + 1 : y + 2, :] = sc * lq
            f1[X, y + 1 : y + 2, :] = fb[1:2]
        return c

    lax.fori_loop(0, PLANES, load_plane, 0)

    def planes(count, body):
        def step(i, c):
            body(i)
            return c

        lax.fori_loop(0, count, step, 0)

    y4 = gy * 4 + 1

    def layer1(X, slot):
        for j in range(6):
            y = y4 + 2 * j
            Y = dot_nn(wa_ref[...], taps(x0s, X, y))
            for k in range(2):
                z = Y[:, k * NZ : (k + 1) * NZ] + ba_ref[...]
                m = liq[X, pl.ds(y + k, 1), :]
                act, sig = activate(z)
                h1[X, y + k] = (act * m).astype(BF16)
                if slot is not None:
                    s1[slot, 2 * j + k] = slope_of(z, sig) * m

    planes(8, lambda i: layer1(1 + i + 2 * (i // 4), None))
    planes(2, lambda i: layer1(MID + i, i))

    def layer2(X, slot):
        for j in range(6):
            y = y4 + 2 * j
            Y = dot_nn(wb_ref[...], taps(h1, X, y))
            for k in range(2):
                z = lane_taps(Y, k) + bb_ref[...]
                m = liq[X, pl.ds(y + k, 1), :]
                act, sig = activate(z)
                h2[X, y + k] = (act * m).astype(BF16)
                if slot is not None:
                    s2[slot, 2 * j + k] = slope_of(z, sig) * m

    planes(4, lambda i: layer2(2 + i + 4 * (i // 2), None))
    planes(4, lambda i: layer2(MID - 1 + i, i))

    y2 = gy * 6 + 1

    def layer3(X, slot, own):
        for j in range(5):
            y = y2 + 2 * j
            Y = dot_nn(wc_ref[...], taps(h2, X, y))
            for k in range(2):
                z = lane_taps(Y, k) + bc_ref[...]
                m = liq[X, pl.ds(y + k, 1), :]
                act, sig = activate(z)
                h3 = (act * m).astype(BF16)
                score = jnp.sum(hw_ref[...] * h3.astype(F32), axis=0, keepdims=True)
                pf[X, pl.ds(y + k, 1), :] = m * (score + hb_ref[0])
                s3[slot, 2 * j + k] = slope_of(z, sig) * m
                if own is not None:
                    h3o[own, 2 * j + k] = h3

    planes(4, lambda i: layer3(3 + i + 2 * (i // 2), i + 2 * (i // 2), None))
    planes(2, lambda i: layer3(MID + i, 2 + i, i))

    def operator(val, X):
        v = val[X, 1 : NY + 1, :]
        s = scl[X, 1 : NY + 1, :]
        q = liq[X, 1 : NY + 1, :]

        def term(nv, ns, nq):
            return 0.5 * (s * nq + ns * q) * (nv - v)

        total = term(val[X + 1, 1 : NY + 1, :], scl[X + 1, 1 : NY + 1, :], liq[X + 1, 1 : NY + 1, :])
        total += term(val[X - 1, 1 : NY + 1, :], scl[X - 1, 1 : NY + 1, :], liq[X - 1, 1 : NY + 1, :])
        total += term(val[X, 2 : NY + 2, :], scl[X, 2 : NY + 2, :], liq[X, 2 : NY + 2, :])
        total += term(val[X, 0:NY, :], scl[X, 0:NY, :], liq[X, 0:NY, :])
        total += term(shift_left(v), shift_left(s), shift_left(q))
        total += term(shift_right(v), shift_right(s), shift_right(q))
        return total

    for X in range(MID - 1, MID + 3):
        rs[X, 1 : NY + 1, :] = operator(pf, X) - liq[X, 1 : NY + 1, :] * f1[X, 1 : NY + 1, :]
    own_y = pl.ds(pl.multiple_of(gy * 8, 8) + 1, 8)
    loss = jnp.zeros((8, NZ), F32)
    for k in range(2):
        p_out[k] = pf[MID + k, own_y, :]
        r = rs[MID + k, own_y, :]
        loss += r * r
    loss_out[...] = loss * (1.0 / cells)
    for X in range(MID - 1, MID + 3):
        rs[X] = rs[X] * (2.0 / cells)
    for k in range(2):
        X = MID + k
        pf[k, 1 : NY + 1, :] = liq[X, 1 : NY + 1, :] * operator(rs, X)
    for k in range(2):
        gs_out[k] = pf[k, own_y, :]

    head = jnp.zeros((HID, NZ), F32)
    for i in range(16):
        X, dy = i // 8, i % 8
        head += pf[X, pl.ds(gy * 8 + 1 + dy, 1), :] * h3o[X, gy * 2 + dy].astype(F32)
    head_out[...] = head

    f0 = gy * 6

    def copy_out(i):
        for l in range(FRAME):
            x0_out[i, l] = x0s[MID - 1 + i, f0 + l]
            h1_out[i, l] = h1[MID - 1 + i, f0 + l]
            h2_out[i, l] = h2[MID - 1 + i, f0 + l]

    planes(4, copy_out)


def backward_kernel(
    pos_ref,
    gl_ref,
    gm_ref,
    gr_ref,
    loss_ref,
    head_ref,
    x0_ref,
    h1_ref,
    h2_ref,
    s1,
    s2,
    s3,
    wbt_ref,
    wct_ref,
    hw_ref,
    keep_ref,
    send_ref,
    gs,
    g3,
    g2,
    g1,
    gcat,
    hcat,
    acc,
):
    gy = pos_ref[1]
    for k in range(2):
        gs[k] = gl_ref[k]
        gs[2 + k] = gm_ref[k]
        gs[4 + k] = gr_ref[k]
    for ref in (g3, g2):
        z = jnp.zeros((HID, NZ), BF16)
        for X in range(ref.shape[0]):
            ref[X, 0] = z
            ref[X, FRAME - 1] = z

    def planes(count, body):
        def step(i, c):
            body(i)
            return c

        lax.fori_loop(0, count, step, 0)

    def back3(X):
        for j in range(10):
            g = gs[X, pl.ds(gy * 6 + j, 1), :]
            g3[X, j + 1] = (g * hw_ref[...] * s3[X, j]).astype(BF16)

    planes(6, back3)

    for X in range(2):
        for r in range(WROWS, ROWS, 8):
            acc[X, r : r + 8, :] = jnp.zeros((8, NZ), F32)
    own = gy * 2 + 1

    def weight_grad(g_ref, g_off, h_ref, which):
        bias = jnp.zeros((HID, NZ), F32)
        for i in range(16):
            X, dy = i // 8, i % 8
            y = own + dy
            raw = g_ref[g_off + X, y]
            g = raw.astype(F32)
            bias += g
            cols = slice(i * NZ, (i + 1) * NZ)
            gcat[0:HID, cols] = shift_left(g).astype(BF16)
            gcat[HID : 2 * HID, cols] = raw
            gcat[2 * HID : 3 * HID, cols] = shift_right(g).astype(BF16)
            for a in range(3):
                for b in range(3):
                    k = 3 * a + b
                    hcat[k * HID : (k + 1) * HID, cols] = h_ref[X + a, y + b - 1]
        W = dot_nt(gcat[...], hcat[...])
        for a in range(3):
            for b in range(3):
                for e in range(3):
                    t = 9 * a + 3 * b + e
                    k = 3 * a + b
                    blk = W[e * HID : (e + 1) * HID, k * HID : (k + 1) * HID]
                    acc[which, t * 32 : (t + 1) * 32, 0:HID] = blk[:32]
                    acc[which, t * 32 : (t + 1) * 32, HID:NZ] = blk[32:]
        return bias

    bias_c = weight_grad(g3, 2, h2_ref, 1)

    def back2(X):
        for j in range(5):
            y = 1 + 2 * j
            Y = dot_nn(wct_ref[...], taps(g3, X + 1, y))
            for k in range(2):
                row = gy * 2 + 2 * j + k
                g2[X, y + k] = (lane_taps(Y, k) * s2[X, row]).astype(BF16)

    planes(4, back2)
    bias_b = weight_grad(g2, 1, h1_ref, 0)

    def back1(X):
        for j in range(4):
            y = own + 2 * j
            Y = dot_nn(wbt_ref[...], taps(g2, X + 1, y))
            for k in range(2):
                row = gy * 4 + 2 * j + k
                g1[X, 2 * j + k] = (lane_taps(Y, k) * s1[X, row]).astype(BF16)

    planes(2, back1)
    bias_a = jnp.zeros((HID, NZ), F32)
    for i in range(16):
        X, dy = i // 8, i % 8
        y = own + dy
        cols = slice(i * NZ, (i + 1) * NZ)
        raw = g1[X, dy]
        bias_a += raw.astype(F32)
        gcat[0:HID, cols] = raw
        for a in range(3):
            for b in range(3):
                k = 3 * a + b
                hcat[k * 16 : (k + 1) * 16, cols] = x0_ref[X + a, y + b - 1]
    A = dot_nt(hcat[0:144, :], gcat[0:HID, :])
    for k in range(8):
        blk = A[16 * k : 16 * k + 12]
        which, spot = k // 4, k % 4
        r0 = WROWS + 12 * (spot % 2)
        c0 = HID * (spot // 2)
        acc[which, r0 : r0 + 12, c0 : c0 + HID] = blk
    acc[1, WROWS + 24 : WROWS + 32, 0:HID] = A[128:136]
    acc[1, WROWS + 24 : WROWS + 28, HID:NZ] = A[136:140]
    sums = [
        jnp.sum(v, axis=1, keepdims=True).reshape(1, HID)
        for v in (bias_a, bias_b, bias_c, head_ref[...])
    ]
    total = jnp.sum(jnp.sum(loss_ref[...], axis=0, keepdims=True), axis=1, keepdims=True)
    keep_ref[0:ROWS] = acc[gy]
    send_ref[0:ROWS] = acc[1 - gy]
    for ref in (keep_ref, send_ref):
        ref[ROWS : ROWS + 8, :] = jnp.zeros((8, NZ), F32)
        for j in range(2):
            ref[ROWS + j : ROWS + j + 1, :] = jnp.concatenate(
                [sums[2 * j], sums[2 * j + 1]], axis=1
            )
        ref[ROWS + 2 : ROWS + 3, :] = jnp.broadcast_to(total, (1, NZ))


def partner(value, bit, count):
    return lax.ppermute(value, AXES, [(i, i ^ bit) for i in range(count)])


def gather_all(block, me, count):
    value = block[None]
    bit = 1
    while bit < count:
        other = partner(value, bit, count)
        upper = (me & bit) != 0
        value = jnp.where(
            upper, jnp.concatenate([other, value]), jnp.concatenate([value, other])
        )
        bit *= 2
    return value


def two_parts(v):
    high = rounded(v)
    return high, rounded(v - high)


def rounded(v):
    return lax.reduce_precision(v, 8, 7)


def sum_all(keep, send, me, count):
    total = keep + partner(send, 1, count)
    body, tail = total[:ROWS], total[ROWS:]
    half = ROWS // 2
    upper = (me & 2) != 0
    high, low = two_parts(tail)
    away = lax.dynamic_slice_in_dim(body, jnp.where(upper, 0, half), half)
    sent = jnp.concatenate([rounded(away), high, low]).astype(BF16)
    got = partner(sent, 2, count).astype(F32)
    body = lax.dynamic_slice_in_dim(body, jnp.where(upper, half, 0), half) + got[:half]
    tail = tail + got[half : half + 8] + got[half + 8 :]
    bit = 4
    while bit < count:
        high, low = two_parts(tail)
        body = rounded(body)
        sent = jnp.concatenate([body, high, low]).astype(BF16)
        got = partner(sent, bit, count).astype(F32)
        body = body + got[:half]
        tail = (high + low) + (got[half : half + 8] + got[half + 8 :])
        bit *= 2
    body = body.astype(BF16)
    other = partner(body, 2, count)
    body = jnp.where(upper, jnp.concatenate([other, body]), jnp.concatenate([body, other]))
    other = partner(body, 1, count)
    odd = (me & 1) != 0
    first = jnp.where(odd, other, body)
    second = jnp.where(odd, body, other)
    return first.astype(F32), second.astype(F32), tail


def on_device(
    loaded_fields,
    brick_home,
    liquid_mask,
    density_class,
    inverse_density,
    conv_a,
    bias_a,
    conv_b,
    bias_b,
    conv_c,
    bias_c,
    head_weight,
    head_bias,
):
    n_slots = lax.axis_size("gx")
    count = n_slots * lax.axis_size("gy")
    gx = lax.axis_index("gx")
    gy = lax.axis_index("gy")
    me = gx * 2 + gy
    cells = 2 * n_slots * NY * NZ
    smem = pl.BlockSpec(memory_space=pltpu.SMEM)
    vmem = pl.BlockSpec(memory_space=pltpu.VMEM)
    params = pltpu.CompilerParams(vmem_limit_bytes=VMEM_LIMIT)

    lhs = jax.ShapeDtypeStruct((3 * HID, 9 * HID), BF16)
    wa, wb, wc, wbt, wct = pl.pallas_call(
        lhs_kernel,
        out_shape=(jax.ShapeDtypeStruct((HID, 144), BF16), lhs, lhs, lhs, lhs),
        in_specs=[vmem] * 3,
        out_specs=(vmem,) * 5,
        compiler_params=params,
        name="lhs",
    )(conv_a, conv_b, conv_c)

    block = jnp.stack(
        [
            loaded_fields[0],
            loaded_fields[1],
            liquid_mask.astype(BF16),
            density_class.astype(BF16),
        ],
        axis=2,
    )
    gath = gather_all(block, me, count)

    def wide(v):
        return jnp.broadcast_to(v.astype(F32)[:, None], (HID, NZ))

    pos = jnp.stack([gx, gy]).astype(jnp.int32)
    head_wide = wide(head_weight)

    def shaped(shape, kind):
        return jax.ShapeDtypeStruct(shape, kind)

    (pressure, score, loss, head, x0o, h1o, h2o, s1, s2, s3) = pl.pallas_call(
        functools.partial(forward_kernel, n_slots=n_slots, cells=cells),
        out_shape=(
            shaped((2, 8, NZ), F32),
            shaped((2, 8, NZ), F32),
            shaped((8, NZ), F32),
            shaped((HID, NZ), F32),
            shaped((4, FRAME, 16, NZ), BF16),
            shaped((4, FRAME, HID, NZ), BF16),
            shaped((4, FRAME, HID, NZ), BF16),
            shaped((2, 12, HID, NZ), F32),
            shaped((4, 12, HID, NZ), F32),
            shaped((6, 10, HID, NZ), F32),
        ),
        in_specs=[smem] * 4 + [vmem] * 8,
        out_specs=(vmem,) * 10,
        scratch_shapes=[
            pltpu.SMEM((n_slots,), jnp.int32),
            pltpu.VMEM((PLANES, YY, 16, NZ), BF16),
            pltpu.VMEM((PLANES, YY, NZ), F32),
            pltpu.VMEM((PLANES, YY, NZ), F32),
            pltpu.VMEM((PLANES, YY, NZ), F32),
            pltpu.VMEM((PLANES, YY, HID, NZ), BF16),
            pltpu.VMEM((PLANES, YY, HID, NZ), BF16),
            pltpu.VMEM((2, 10, HID, NZ), BF16),
            pltpu.VMEM((PLANES, YY, NZ), F32),
            pltpu.VMEM((PLANES, YY, NZ), F32),
        ],
        compiler_params=params,
        name="forward",
    )(
        pos,
        brick_home,
        inverse_density,
        head_bias,
        gath,
        wa,
        wb,
        wc,
        wide(bias_a),
        wide(bias_b),
        wide(bias_c),
        head_wide,
    )

    other = partner(score, 1, count)
    middle = jnp.where(
        gy == 0, jnp.concatenate([score, other], 1), jnp.concatenate([other, score], 1)
    )
    up = [(i, i + 1) for i in range(n_slots - 1)]
    left = lax.ppermute(middle, "gx", up)
    right = lax.ppermute(middle, "gx", [(j, i) for i, j in up])

    keep, send = pl.pallas_call(
        backward_kernel,
        out_shape=(shaped((ROWS + 8, NZ), F32), shaped((ROWS + 8, NZ), F32)),
        in_specs=[smem] + [vmem] * 14,
        out_specs=(vmem, vmem),
        scratch_shapes=[
            pltpu.VMEM((6, NY, NZ), F32),
            pltpu.VMEM((6, FRAME, HID, NZ), BF16),
            pltpu.VMEM((4, FRAME, HID, NZ), BF16),
            pltpu.VMEM((2, 8, HID, NZ), BF16),
            pltpu.VMEM((3 * HID, 16 * NZ), BF16),
            pltpu.VMEM((9 * HID, 16 * NZ), BF16),
            pltpu.VMEM((2, ROWS, NZ), F32),
        ],
        compiler_params=params,
        name="backward",
    )(
        pos,
        left,
        middle,
        right,
        loss,
        head,
        x0o,
        h1o,
        h2o,
        s1,
        s2,
        s3,
        wbt,
        wct,
        head_wide,
    )

    first, second, tail = sum_all(keep, send, me, count)

    def weights(v):
        v = v[:WROWS].reshape(27, 32, 2, HID)
        return v.transpose(0, 2, 1, 3).reshape(27, HID, HID)

    def blocks(v):
        v = v[WROWS : WROWS + 24].reshape(2, 12, 2, HID)
        return v.transpose(2, 0, 1, 3).reshape(4, 12, HID)

    last = jnp.concatenate(
        [second[WROWS + 24 : WROWS + 32, :HID], second[WROWS + 24 : WROWS + 28, HID:]], axis=0
    )
    parts = jnp.concatenate([blocks(first), blocks(second), last[None]], axis=0)
    grad_a = parts.reshape(27, 4, HID)[:, :3].transpose(0, 2, 1)
    return (
        pressure,
        tail[2, :1],
        grad_a,
        tail[0, :HID],
        weights(first),
        tail[0, HID:],
        weights(second),
        tail[1, :HID],
        tail[1, HID:],
    )


def solution(mesh):
    grid = P(("grp", "gx"), "gy", None)
    part = P("grp")
    stack = P("grp", None, None)
    return jax.shard_map(
        on_device,
        mesh=mesh,
        in_specs=(P(None, ("grp", "gx"), "gy", None), part, grid, grid) + (P(),) * 9,
        out_specs=(grid, part, stack, part, stack, part, stack, part, part),
        check_vma=False,
    )
```

```python
import functools

import jax
import jax.numpy as jnp
from jax import lax
from jax.experimental import pallas as pl
from jax.experimental.pallas import tpu as pltpu
from jax.sharding import PartitionSpec as P

F32 = jnp.float32
BF16 = jnp.bfloat16
AXES = ("gx", "gy")
HID = 64
NZ = 128
NY = 16
YY = NY + 2
PLANES = 12
MID = 5
FRAME = 12
WROWS = 864
ROWS = 896
TAIL = 16
VMEM_LIMIT = 24 * 1024 * 1024
S1, S2, S3, HEAD, LOSS, S_BLOCKS = 0, 24, 72, 132, 133, 134
H1, H2, X0, WB, WC, H_BLOCKS = 0, 48, 96, 108, 123, 138


def shift_right(v):
    lane = lax.broadcasted_iota(jnp.int32, v.shape, v.ndim - 1)
    return jnp.where(lane == 0, 0.0, pltpu.roll(v, 1, v.ndim - 1))


def shift_left(v):
    lane = lax.broadcasted_iota(jnp.int32, v.shape, v.ndim - 1)
    return jnp.where(lane == NZ - 1, 0.0, pltpu.roll(v, NZ - 1, v.ndim - 1))


def dot_nn(a, b):
    return jnp.dot(a, b, preferred_element_type=F32)


def dot_nt(a, b):
    return lax.dot_general(a, b, (((1,), (1,)), ((), ())), preferred_element_type=F32)


def taps(src, X, y):
    out = []
    for a in range(3):
        for b in range(3):
            out.append(
                jnp.concatenate([src[X + a - 1, y + b - 1], src[X + a - 1, y + b]], axis=1)
            )
    return jnp.concatenate(out, axis=0)


def lane_taps(Y, k):
    part = Y[:, k * NZ : (k + 1) * NZ]
    return part[HID : 2 * HID] + shift_right(part[:HID]) + shift_left(part[2 * HID :])


def activate(z):
    sig = 0.5 * jnp.tanh(0.5 * z) + 0.5
    return z * sig, sig


def slope_of(z, sig):
    return sig * (1.0 + z * (1.0 - sig))


def payload_kernel(fields_hbm, liquid_hbm, class_hbm, out_ref, fields, liquid, classes, rows, sems):
    copies = [
        pltpu.make_async_copy(src, dst, sems.at[i])
        for i, (src, dst) in enumerate(
            ((fields_hbm, fields), (liquid_hbm, liquid), (class_hbm, classes))
        )
    ]
    for copy in copies:
        copy.start()
    for copy in copies:
        copy.wait()
    for x in range(2):
        planes = (fields[0, x], fields[1, x], liquid[x], classes[x])
        for p, plane in enumerate(planes):
            plane = plane.astype(F32)
            for y in range(8):
                rows[x, y, p : p + 1, :] = plane[y : y + 1]
    out_ref[...] = rows[...].astype(BF16)


def lhs_kernel(wa_hbm, wb_hbm, wc_hbm, fa, fb, fc, tb, tc, wa_ref, wb_ref, wc_ref, sems):
    copies = [
        pltpu.make_async_copy(src, dst, sems.at[i])
        for i, (src, dst) in enumerate(((wb_hbm, wb_ref), (wc_hbm, wc_ref), (wa_hbm, wa_ref)))
    ]
    for copy in copies:
        copy.start()
    for which, (w, fwd, bwd) in enumerate(((wb_ref, fb, tb), (wc_ref, fc, tc))):
        copies[which].wait()
        for e in range(3):
            rows = slice(e * HID, (e + 1) * HID)
            for k in range(0, 9, 2):
                c = k * HID
                lo = w[3 * k + e].astype(F32)
                blo = w[26 - (3 * k + e)].astype(F32)
                if k < 8:
                    hi = w[3 * k + 3 + e].astype(F32)
                    bhi = w[26 - (3 * k + 3 + e)].astype(F32)
                    fwd[rows, c : c + 2 * HID] = jnp.concatenate([lo, hi], axis=1).astype(BF16)
                else:
                    bhi = blo
                    fwd[rows, c : c + HID] = lo.astype(BF16)
                bwd[3 * (k // 2) + e] = jnp.concatenate([blo, bhi], axis=0).T.astype(BF16)
    copies[2].wait()
    tap = lax.broadcasted_iota(jnp.int32, (27, 144), 0)
    col = lax.broadcasted_iota(jnp.int32, (27, 144), 1)
    total = jnp.zeros((HID, 144), F32)
    for ch in range(3):
        spot = 16 * (tap // 3) + 4 * (tap - 3 * (tap // 3)) + ch
        pick = jnp.where(col == spot, 1.0, 0.0).astype(BF16)
        total += dot_nn(wa_ref[ch].astype(F32).T.astype(BF16), pick)
    fa[...] = total.astype(BF16)


def forward_kernel(
    pos_ref,
    home_ref,
    invd_ref,
    hb_ref,
    mine_ref,
    other_ref,
    wa_ref,
    wb_ref,
    wc_ref,
    tb_ref,
    tc_ref,
    ba_ref,
    bb_ref,
    bc_ref,
    hw_ref,
    p_out,
    gs_out,
    sbuf,
    hbuf,
    inv_ref,
    x0s,
    liq,
    scl,
    f1,
    h1,
    h2,
    h3o,
    pf,
    rs,
    *,
    n_slots,
    cells,
):
    gx = pos_ref[0]
    gy = pos_ref[1]
    for s in range(n_slots):
        inv_ref[home_ref[s]] = s

    for ref in (x0s, h1, h2):
        z = jnp.zeros(ref.shape[2:], ref.dtype)
        for X in range(PLANES):
            ref[X, 0] = z
            ref[X, NY + 1] = z
    for ref in (liq, scl, f1, pf, rs):
        for X in range(PLANES):
            ref[X] = jnp.zeros((YY, NZ), F32)

    def load_plane(X, c):
        xg = 2 * gx - MID + X
        ok = jnp.where((xg >= 0) & (xg < 2 * n_slots), 1.0, 0.0).astype(F32)
        xc = jnp.clip(xg, 0, 2 * n_slots - 1)
        home = xc // 2
        half = xc - 2 * home
        slot = inv_ref[home]
        row4 = lax.broadcasted_iota(jnp.int32, (4, NZ), 0)
        for i in range(NY):
            src = (mine_ref, other_ref)[i // 8]
            fb = src[slot, half, i % 8].astype(F32) * ok
            mb = src[home, half, i % 8].astype(F32)
            y = 8 * (gy if i < 8 else 1 - gy) + i % 8
            lq = mb[2:3] * ok
            cl = mb[3:4]
            sc = jnp.zeros((1, NZ), F32)
            for k in range(4):
                sc = jnp.where(cl == k, invd_ref[k], sc)
            base = jnp.where(row4 < 2, fb, jnp.where(row4 == 2, mb * ok, 0.0))
            k12 = jnp.concatenate(
                [shift_right(base), base, shift_left(base), jnp.zeros((4, NZ), F32)], axis=0
            )
            x0s[X, y + 1] = k12.astype(BF16)
            liq[X, pl.ds(y + 1, 1), :] = lq
            scl[X, pl.ds(y + 1, 1), :] = sc * lq
            f1[X, pl.ds(y + 1, 1), :] = fb[1:2]
        return c

    lax.fori_loop(0, PLANES, load_plane, 0)

    def planes(count, body):
        def step(i, c):
            body(i)
            return c

        lax.fori_loop(0, count, step, 0)

    y4 = gy * 4 + 1

    def layer1(X, slot):
        for j in range(6):
            y = y4 + 2 * j
            Y = dot_nn(wa_ref[...], taps(x0s, X, y))
            for k in range(2):
                z = Y[:, k * NZ : (k + 1) * NZ] + ba_ref[...]
                m = liq[X, pl.ds(y + k, 1), :]
                act, sig = activate(z)
                h1[X, y + k] = (act * m).astype(BF16)
                if slot is not None:
                    sbuf[S1 + 12 * slot + 2 * j + k] = slope_of(z, sig) * m

    planes(8, lambda i: layer1(1 + i + 2 * (i // 4), None))
    planes(2, lambda i: layer1(MID + i, i))

    def layer2(X, slot):
        for j in range(6):
            y = y4 + 2 * j
            Y = dot_nn(wb_ref[...], taps(h1, X, y))
            for k in range(2):
                z = lane_taps(Y, k) + bb_ref[...]
                m = liq[X, pl.ds(y + k, 1), :]
                act, sig = activate(z)
                h2[X, y + k] = (act * m).astype(BF16)
                if slot is not None:
                    sbuf[S2 + 12 * slot + 2 * j + k] = slope_of(z, sig) * m

    planes(4, lambda i: layer2(2 + i + 4 * (i // 2), None))
    planes(4, lambda i: layer2(MID - 1 + i, i))

    y2 = gy * 6 + 1

    def layer3(X, slot, own):
        for j in range(5):
            y = y2 + 2 * j
            Y = dot_nn(wc_ref[...], taps(h2, X, y))
            for k in range(2):
                z = lane_taps(Y, k) + bc_ref[...]
                m = liq[X, pl.ds(y + k, 1), :]
                act, sig = activate(z)
                h3 = (act * m).astype(BF16)
                score = jnp.sum(hw_ref[...] * h3.astype(F32), axis=0, keepdims=True)
                pf[X, pl.ds(y + k, 1), :] = m * (score + hb_ref[0])
                sbuf[S3 + 10 * slot + 2 * j + k] = slope_of(z, sig) * m
                if own is not None:
                    h3o[own, 2 * j + k] = h3

    planes(4, lambda i: layer3(3 + i + 2 * (i // 2), i + 2 * (i // 2), None))
    planes(2, lambda i: layer3(MID + i, 2 + i, i))

    def operator(val, X):
        v = val[X, 1 : NY + 1, :]
        s = scl[X, 1 : NY + 1, :]
        q = liq[X, 1 : NY + 1, :]

        def term(nv, ns, nq):
            return 0.5 * (s * nq + ns * q) * (nv - v)

        total = term(val[X + 1, 1 : NY + 1, :], scl[X + 1, 1 : NY + 1, :], liq[X + 1, 1 : NY + 1, :])
        total += term(val[X - 1, 1 : NY + 1, :], scl[X - 1, 1 : NY + 1, :], liq[X - 1, 1 : NY + 1, :])
        total += term(val[X, 2 : NY + 2, :], scl[X, 2 : NY + 2, :], liq[X, 2 : NY + 2, :])
        total += term(val[X, 0:NY, :], scl[X, 0:NY, :], liq[X, 0:NY, :])
        total += term(shift_left(v), shift_left(s), shift_left(q))
        total += term(shift_right(v), shift_right(s), shift_right(q))
        return total

    for X in range(MID - 1, MID + 3):
        rs[X, 1 : NY + 1, :] = operator(pf, X) - liq[X, 1 : NY + 1, :] * f1[X, 1 : NY + 1, :]
    own_y = pl.ds(pl.multiple_of(gy * 8, 8) + 1, 8)
    loss = jnp.zeros((8, NZ), F32)
    for k in range(2):
        p_out[k] = pf[MID + k, own_y, :]
        r = rs[MID + k, own_y, :]
        loss += r * r
    sbuf[LOSS, 0:8, :] = loss * (1.0 / cells)
    for X in range(MID - 1, MID + 3):
        rs[X] = rs[X] * (2.0 / cells)
    for k in range(2):
        X = MID + k
        pf[k, 1 : NY + 1, :] = liq[X, 1 : NY + 1, :] * operator(rs, X)
    for k in range(2):
        gs_out[k] = pf[k, own_y, :]

    head = jnp.zeros((HID, NZ), F32)
    for i in range(16):
        X, dy = i // 8, i % 8
        head += pf[X, pl.ds(gy * 8 + 1 + dy, 1), :] * h3o[X, gy * 2 + dy].astype(F32)
    sbuf[HEAD] = head

    f0 = gy * 6

    def copy_out(i):
        for l in range(FRAME):
            r = (l % 4) * 16
            hbuf[X0 + 3 * i + l // 4, r : r + 16, :] = x0s[MID - 1 + i, f0 + l]
            hbuf[H1 + FRAME * i + l] = h1[MID - 1 + i, f0 + l]
            hbuf[H2 + FRAME * i + l] = h2[MID - 1 + i, f0 + l]

    planes(4, copy_out)
    for r in range(15):
        hbuf[WB + r] = tb_ref[r]
        hbuf[WC + r] = tc_ref[r]


def backward_kernel(
    pos_ref,
    gm_ref,
    gmo_ref,
    p1_ref,
    p1o_ref,
    p2_ref,
    p2o_ref,
    sbuf,
    hbuf,
    hw_ref,
    keep_ref,
    send_ref,
    gs,
    g3,
    g2,
    g1,
    gcat,
    hcat,
    acc,
    wbt_ref,
    wct_ref,
):
    gy = pos_ref[1]
    even = pos_ref[0] % 2 == 0
    own_half = pl.ds(pl.multiple_of(8 * gy, 8), 8)
    far_half = pl.ds(pl.multiple_of(8 - 8 * gy, 8), 8)
    for half, gm, p1, p2 in (
        (own_half, gm_ref, p1_ref, p2_ref),
        (far_half, gmo_ref, p1o_ref, p2o_ref),
    ):
        for k in range(2):
            gs[k, half, :] = jnp.where(even, p2[k], p1[k])
            gs[2 + k, half, :] = gm[k]
            gs[4 + k, half, :] = jnp.where(even, p1[k], p2[k])
    for base, ref in ((WB, wbt_ref), (WC, wct_ref)):
        for e in range(3):
            rows = slice(e * HID, (e + 1) * HID)
            for t in range(4):
                ref[rows, t * NZ : (t + 1) * NZ] = hbuf[base + 3 * t + e]
            ref[rows, 4 * NZ : 4 * NZ + HID] = hbuf[base + 12 + e][:, :HID]
    for ref in (g3, g2):
        z = jnp.zeros((HID, NZ), BF16)
        for X in range(ref.shape[0]):
            ref[X, 0] = z
            ref[X, FRAME - 1] = z

    def planes(count, body):
        def step(i, c):
            body(i)
            return c

        lax.fori_loop(0, count, step, 0)

    def back3(X):
        for j in range(10):
            g = gs[X, pl.ds(gy * 6 + j, 1), :]
            g3[X, j + 1] = (g * hw_ref[...] * sbuf[S3 + 10 * X + j]).astype(BF16)

    planes(6, back3)

    for X in range(2):
        for r in range(WROWS, ROWS, 8):
            acc[X, r : r + 8, :] = jnp.zeros((8, NZ), F32)
    own = gy * 2 + 1

    def weight_grad(g_ref, g_off, h_base, which):
        bias = jnp.zeros((HID, NZ), F32)
        for i in range(16):
            X, dy = i // 8, i % 8
            y = own + dy
            raw = g_ref[g_off + X, y]
            g = raw.astype(F32)
            bias += g
            cols = slice(i * NZ, (i + 1) * NZ)
            gcat[0:HID, cols] = shift_left(g).astype(BF16)
            gcat[HID : 2 * HID, cols] = raw
            gcat[2 * HID : 3 * HID, cols] = shift_right(g).astype(BF16)
            for a in range(3):
                for b in range(3):
                    k = 3 * a + b
                    hcat[k * HID : (k + 1) * HID, cols] = hbuf[h_base + FRAME * (X + a) + y + b - 1]
        W = dot_nt(gcat[...], hcat[...])
        for a in range(3):
            for b in range(3):
                for e in range(3):
                    t = 9 * a + 3 * b + e
                    k = 3 * a + b
                    blk = W[e * HID : (e + 1) * HID, k * HID : (k + 1) * HID]
                    acc[which, t * 32 : (t + 1) * 32, 0:HID] = blk[:32]
                    acc[which, t * 32 : (t + 1) * 32, HID:NZ] = blk[32:]
        return bias

    bias_c = weight_grad(g3, 2, H2, 1)

    def back2(X):
        for j in range(5):
            y = 1 + 2 * j
            Y = dot_nn(wct_ref[...], taps(g3, X + 1, y))
            for k in range(2):
                row = gy * 2 + 2 * j + k
                g2[X, y + k] = (lane_taps(Y, k) * sbuf[S2 + 12 * X + row]).astype(BF16)

    planes(4, back2)
    bias_b = weight_grad(g2, 1, H1, 0)

    def back1(X):
        for j in range(4):
            y = own + 2 * j
            Y = dot_nn(wbt_ref[...], taps(g2, X + 1, y))
            for k in range(2):
                row = gy * 4 + 2 * j + k
                g1[X, 2 * j + k] = (lane_taps(Y, k) * sbuf[S1 + 12 * X + row]).astype(BF16)

    planes(2, back1)
    bias_a = jnp.zeros((HID, NZ), F32)
    for i in range(16):
        X, dy = i // 8, i % 8
        y = own + dy
        cols = slice(i * NZ, (i + 1) * NZ)
        raw = g1[X, dy]
        bias_a += raw.astype(F32)
        gcat[0:HID, cols] = raw
        for a in range(3):
            for b in range(3):
                k = 3 * a + b
                l = y + b - 1
                q = l // 4
                hcat[k * 16 : (k + 1) * 16, cols] = hbuf[
                    X0 + 3 * (X + a) + q, pl.ds(pl.multiple_of((l - 4 * q) * 16, 16), 16), :
                ]
    A = dot_nt(hcat[0:144, :], gcat[0:HID, :])
    for k in range(8):
        blk = A[16 * k : 16 * k + 12]
        which, spot = k // 4, k % 4
        r0 = WROWS + 12 * (spot % 2)
        c0 = HID * (spot // 2)
        acc[which, r0 : r0 + 12, c0 : c0 + HID] = blk
    acc[1, WROWS + 24 : WROWS + 32, 0:HID] = A[128:136]
    acc[1, WROWS + 24 : WROWS + 28, HID:NZ] = A[136:140]
    sums = [
        jnp.sum(v, axis=1, keepdims=True).reshape(1, HID)
        for v in (bias_a, bias_b, bias_c, sbuf[HEAD])
    ]
    total = jnp.sum(jnp.sum(sbuf[LOSS, 0:8, :], axis=0, keepdims=True), axis=1, keepdims=True)
    keep_ref[0:ROWS] = acc[gy]
    send_ref[0:ROWS] = acc[1 - gy]
    for ref in (keep_ref, send_ref):
        ref[ROWS : ROWS + 8, :] = jnp.zeros((8, NZ), F32)
        for j in range(2):
            ref[ROWS + j : ROWS + j + 1, :] = jnp.concatenate(
                [sums[2 * j], sums[2 * j + 1]], axis=1
            )
        ref[ROWS + 2 : ROWS + 3, :] = jnp.broadcast_to(total, (1, NZ))


def finish_kernel(pos_ref, a_ref, b_ref, c_ref, d_ref, gb_hbm, gc_hbm, ga_ref, stage, first, sems):
    gy = pos_ref[1]
    upper = (pos_ref[0]) % 2

    def unpack(ref, which, half):
        for j in range(14):
            v = ref[32 * j : 32 * j + 32].astype(F32)
            stage[which, 14 * half + j, 0:32, :] = v[:, :HID]
            stage[which, 14 * half + j, 32:HID, :] = v[:, HID:]

    unpack(a_ref, gy, upper)
    unpack(b_ref, gy, 1 - upper)
    unpack(c_ref, 1 - gy, upper)
    unpack(d_ref, 1 - gy, 1 - upper)
    copies = [
        pltpu.make_async_copy(stage.at[i, pl.ds(0, 27)], dst, sems.at[i])
        for i, dst in enumerate((gb_hbm, gc_hbm))
    ]
    for copy in copies:
        copy.start()
    first[0:24] = stage[0, 27, 0:24]
    first[24:48] = stage[0, 27, 32:56]
    first[48:72] = stage[1, 27, 0:24]
    first[72:96] = stage[1, 27, 32:56]
    first[96:104] = stage[1, 27, 24:32]
    first[104:108] = stage[1, 27, 56:60]
    for ch in range(3):
        ga_ref[ch] = first[pl.ds(ch, 27, stride=4), :]
    for copy in copies:
        copy.wait()


def partner(value, bit, count):
    return lax.ppermute(value, AXES, [(i, i ^ bit) for i in range(count)])


def gather_all(block, me, count):
    value = block[None]
    bit = 2
    while bit < count:
        other = partner(value, bit, count)
        upper = (me & bit) != 0
        value = jnp.where(
            upper, jnp.concatenate([other, value]), jnp.concatenate([value, other])
        )
        bit *= 2
    return value


def two_parts(v):
    high = rounded(v)
    return high, rounded(v - high)


def rounded(v):
    return lax.reduce_precision(v, 8, 7)


def sum_all(keep, send, me, count):
    total = keep + partner(send, 1, count)
    body, tail = total[:ROWS], total[ROWS:]
    half = ROWS // 2
    upper = (me & 2) != 0
    high, low = two_parts(tail)
    away = lax.dynamic_slice_in_dim(body, jnp.where(upper, 0, half), half)
    sent = jnp.concatenate([rounded(away), high, low]).astype(BF16)
    got = partner(sent, 2, count).astype(F32)
    body = lax.dynamic_slice_in_dim(body, jnp.where(upper, half, 0), half) + got[:half]
    tail = tail + got[half : half + 8] + got[half + 8 :]
    bit = 4
    while bit < count:
        high, low = two_parts(tail)
        body = rounded(body)
        sent = jnp.concatenate([body, high, low]).astype(BF16)
        got = partner(sent, bit, count).astype(F32)
        body = body + got[:half]
        tail = (high + low) + (got[half : half + 8] + got[half + 8 :])
        bit *= 2
    body = body.astype(BF16)
    beside = partner(body, 2, count)
    far = partner(body, 1, count)
    return body, beside, far, partner(beside, 1, count), tail


def on_device(
    loaded_fields,
    brick_home,
    liquid_mask,
    density_class,
    inverse_density,
    conv_a,
    bias_a,
    conv_b,
    bias_b,
    conv_c,
    bias_c,
    head_weight,
    head_bias,
):
    n_slots = lax.axis_size("gx")
    count = n_slots * lax.axis_size("gy")
    gx = lax.axis_index("gx")
    gy = lax.axis_index("gy")
    me = gx * 2 + gy
    cells = 2 * n_slots * NY * NZ
    smem = pl.BlockSpec(memory_space=pltpu.SMEM)
    vmem = pl.BlockSpec(memory_space=pltpu.VMEM)
    params = pltpu.CompilerParams(vmem_limit_bytes=VMEM_LIMIT)

    hbm = pl.BlockSpec(memory_space=pl.ANY)

    def shaped(shape, kind):
        return jax.ShapeDtypeStruct(shape, kind)

    block = pl.pallas_call(
        payload_kernel,
        out_shape=shaped((2, 8, 4, NZ), BF16),
        in_specs=[hbm] * 3,
        out_specs=vmem,
        scratch_shapes=[
            pltpu.VMEM((2, 2, 8, NZ), BF16),
            pltpu.VMEM((2, 8, NZ), jnp.int32),
            pltpu.VMEM((2, 8, NZ), jnp.int32),
            pltpu.VMEM((2, 8, 4, NZ), F32),
            pltpu.SemaphoreType.DMA((3,)),
        ],
        compiler_params=params,
        name="payload",
    )(loaded_fields, liquid_mask, density_class)
    mine = gather_all(block, me, count)
    across = partner(mine, 1, count)

    lhs = shaped((3 * HID, 9 * HID), BF16)
    turned = shaped((15, HID, NZ), BF16)
    wa, wb, wc, wbt, wct = pl.pallas_call(
        lhs_kernel,
        out_shape=(shaped((HID, 144), BF16), lhs, lhs, turned, turned),
        in_specs=[hbm] * 3,
        out_specs=(vmem,) * 5,
        scratch_shapes=[
            pltpu.VMEM((3, 27, HID), BF16),
            pltpu.VMEM((27, HID, HID), BF16),
            pltpu.VMEM((27, HID, HID), BF16),
            pltpu.SemaphoreType.DMA((3,)),
        ],
        compiler_params=params,
        name="lhs",
    )(conv_a.transpose(2, 0, 1), conv_b, conv_c)

    def wide(v):
        return jnp.broadcast_to(v.astype(F32)[:, None], (HID, NZ))

    pos = jnp.stack([gx, gy]).astype(jnp.int32)
    head_wide = wide(head_weight)

    pressure, score, sbuf, hbuf = pl.pallas_call(
        functools.partial(forward_kernel, n_slots=n_slots, cells=cells),
        out_shape=(
            shaped((2, 8, NZ), F32),
            shaped((2, 8, NZ), F32),
            shaped((S_BLOCKS, HID, NZ), F32),
            shaped((H_BLOCKS, HID, NZ), BF16),
        ),
        in_specs=[smem] * 4 + [vmem] * 11,
        out_specs=(vmem,) * 4,
        scratch_shapes=[
            pltpu.SMEM((n_slots,), jnp.int32),
            pltpu.VMEM((PLANES, YY, 16, NZ), BF16),
            pltpu.VMEM((PLANES, YY, NZ), F32),
            pltpu.VMEM((PLANES, YY, NZ), F32),
            pltpu.VMEM((PLANES, YY, NZ), F32),
            pltpu.VMEM((PLANES, YY, HID, NZ), BF16),
            pltpu.VMEM((PLANES, YY, HID, NZ), BF16),
            pltpu.VMEM((2, 10, HID, NZ), BF16),
            pltpu.VMEM((PLANES, YY, NZ), F32),
            pltpu.VMEM((PLANES, YY, NZ), F32),
        ],
        compiler_params=params,
        name="forward",
    )(
        pos,
        brick_home,
        inverse_density,
        head_bias,
        mine,
        across,
        wa,
        wb,
        wc,
        wbt,
        wct,
        wide(bias_a),
        wide(bias_b),
        wide(bias_c),
        head_wide,
    )

    swap1 = lax.ppermute(score, "gx", [(i, i ^ 1) for i in range(n_slots)])
    swap2 = lax.ppermute(score, "gx", [(i, ((i + 1) ^ 1) - 1) for i in range(1, n_slots - 1)])
    scores = []
    for value in (score, swap1, swap2):
        scores += [value, partner(value, 1, count)]

    keep, send = pl.pallas_call(
        backward_kernel,
        out_shape=(shaped((ROWS + 8, NZ), F32), shaped((ROWS + 8, NZ), F32)),
        in_specs=[smem] + [vmem] * 9,
        out_specs=(vmem, vmem),
        scratch_shapes=[
            pltpu.VMEM((6, NY, NZ), F32),
            pltpu.VMEM((6, FRAME, HID, NZ), BF16),
            pltpu.VMEM((4, FRAME, HID, NZ), BF16),
            pltpu.VMEM((2, 8, HID, NZ), BF16),
            pltpu.VMEM((3 * HID, 16 * NZ), BF16),
            pltpu.VMEM((9 * HID, 16 * NZ), BF16),
            pltpu.VMEM((2, ROWS, NZ), F32),
            pltpu.VMEM((3 * HID, 9 * HID), BF16),
            pltpu.VMEM((3 * HID, 9 * HID), BF16),
        ],
        compiler_params=params,
        name="backward",
    )(
        pos,
        *scores,
        sbuf,
        hbuf,
        head_wide,
    )

    *pieces, tail = sum_all(keep, send, me, count)
    weights = shaped((27, HID, HID), F32)
    grad_b, grad_c, grad_a = pl.pallas_call(
        finish_kernel,
        out_shape=(weights, weights, shaped((3, 27, HID), F32)),
        in_specs=[smem] + [vmem] * 4,
        out_specs=(hbm, hbm, vmem),
        scratch_shapes=[
            pltpu.VMEM((2, 28, HID, HID), F32),
            pltpu.VMEM((112, HID), F32),
            pltpu.SemaphoreType.DMA((2,)),
        ],
        compiler_params=params,
        name="finish",
    )(pos, *pieces)
    return (
        pressure,
        tail[2, :1],
        grad_a.transpose(1, 2, 0),
        tail[0, :HID],
        grad_b,
        tail[0, HID:],
        grad_c,
        tail[1, :HID],
        tail[1, HID:],
    )


def solution(mesh):
    grid = P(("grp", "gx"), "gy", None)
    part = P("grp")
    stack = P("grp", None, None)
    return jax.shard_map(
        on_device,
        mesh=mesh,
        in_specs=(P(None, ("grp", "gx"), "gy", None), part, grid, grid) + (P(),) * 9,
        out_specs=(grid, part, stack, part, stack, part, stack, part, part),
        check_vma=False,
    )
```

```python
import functools

import jax
import jax.numpy as jnp
from jax import lax
from jax.experimental import pallas as pl
from jax.experimental.pallas import tpu as pltpu
from jax.sharding import PartitionSpec as P

F32 = jnp.float32
BF16 = jnp.bfloat16
AXES = ("gx", "gy")
HID = 64
NZ = 128
NY = 16
YY = NY + 2
PLANES = 12
MID = 5
FRAME = 12
WROWS = 864
ROWS = 896
TAIL = 16
VMEM_LIMIT = 24 * 1024 * 1024
S1, S2, S3, HEAD, LOSS, S_BLOCKS = 0, 24, 72, 132, 133, 134
H1, H2, X0, WB, WC, H_BLOCKS = 0, 48, 96, 108, 123, 138


def shift_right(v):
    lane = lax.broadcasted_iota(jnp.int32, v.shape, v.ndim - 1)
    return jnp.where(lane == 0, 0.0, pltpu.roll(v, 1, v.ndim - 1))


def shift_left(v):
    lane = lax.broadcasted_iota(jnp.int32, v.shape, v.ndim - 1)
    return jnp.where(lane == NZ - 1, 0.0, pltpu.roll(v, NZ - 1, v.ndim - 1))


def dot_nn(a, b):
    return jnp.dot(a, b, preferred_element_type=F32)


def dot_nt(a, b):
    return lax.dot_general(a, b, (((1,), (1,)), ((), ())), preferred_element_type=F32)


def taps(src, X, y):
    out = []
    for a in range(3):
        for b in range(3):
            out.append(
                jnp.concatenate([src[X + a - 1, y + b - 1], src[X + a - 1, y + b]], axis=1)
            )
    return jnp.concatenate(out, axis=0)


def lane_taps(Y, k):
    part = Y[:, k * NZ : (k + 1) * NZ]
    return part[HID : 2 * HID] + shift_right(part[:HID]) + shift_left(part[2 * HID :])


def activate(z):
    sig = 0.5 * jnp.tanh(0.5 * z) + 0.5
    return z * sig, sig


def slope_of(z, sig):
    return sig * (1.0 + z * (1.0 - sig))


def payload_kernel(fields_hbm, liquid_hbm, class_hbm, out_ref, fields, liquid, classes, rows, sems):
    copies = [
        pltpu.make_async_copy(src, dst, sems.at[i])
        for i, (src, dst) in enumerate(
            ((fields_hbm, fields), (liquid_hbm, liquid), (class_hbm, classes))
        )
    ]
    for copy in copies:
        copy.start()
    for copy in copies:
        copy.wait()
    for x in range(2):
        planes = (fields[0, x], fields[1, x], liquid[x], classes[x])
        for p, plane in enumerate(planes):
            plane = plane.astype(F32)
            for y in range(8):
                rows[x, y, p : p + 1, :] = plane[y : y + 1]
    out_ref[...] = rows[...].astype(BF16)


def lhs_kernel(
    wb_hbm,
    wc_hbm,
    wa_hbm,
    ba_hbm,
    bb_hbm,
    bc_hbm,
    hw_hbm,
    fa,
    fb,
    fc,
    tb,
    tc,
    wide_ref,
    wb_ref,
    wc_ref,
    wa_ref,
    ba_ref,
    bb_ref,
    bc_ref,
    hw_ref,
    sems,
):
    copies = [
        pltpu.make_async_copy(src, dst, sems.at[i])
        for i, (src, dst) in enumerate(
            (
                (wb_hbm, wb_ref),
                (wc_hbm, wc_ref),
                (wa_hbm, wa_ref),
                (ba_hbm, ba_ref),
                (bb_hbm, bb_ref),
                (bc_hbm, bc_ref),
                (hw_hbm, hw_ref),
            )
        )
    ]
    for copy in copies:
        copy.start()
    for which, (w, fwd, bwd) in enumerate(((wb_ref, fb, tb), (wc_ref, fc, tc))):
        copies[which].wait()
        for e in range(3):
            rows = slice(e * HID, (e + 1) * HID)
            for k in range(0, 9, 2):
                c = k * HID
                lo = w[3 * k + e].astype(F32)
                blo = w[26 - (3 * k + e)].astype(F32)
                if k < 8:
                    hi = w[3 * k + 3 + e].astype(F32)
                    bhi = w[26 - (3 * k + 3 + e)].astype(F32)
                    fwd[rows, c : c + 2 * HID] = jnp.concatenate([lo, hi], axis=1).astype(BF16)
                else:
                    bhi = blo
                    fwd[rows, c : c + HID] = lo.astype(BF16)
                bwd[3 * (k // 2) + e] = jnp.concatenate([blo, bhi], axis=0).T.astype(BF16)
    copies[2].wait()
    tap = lax.broadcasted_iota(jnp.int32, (27, 144), 0)
    col = lax.broadcasted_iota(jnp.int32, (27, 144), 1)
    total = jnp.zeros((HID, 144), F32)
    for ch in range(3):
        spot = 16 * (tap // 3) + 4 * (tap - 3 * (tap // 3)) + ch
        pick = jnp.where(col == spot, 1.0, 0.0).astype(BF16)
        total += dot_nn(wa_ref[ch].astype(F32).T.astype(BF16), pick)
    fa[...] = total.astype(BF16)
    for i, ref in enumerate((ba_ref, bb_ref, bc_ref, hw_ref)):
        copies[3 + i].wait()
        wide_ref[i] = jnp.broadcast_to(ref[...].astype(F32), (NZ, HID)).T


def forward_kernel(
    pos_ref,
    home_hbm,
    invd_hbm,
    hb_ref,
    mine_ref,
    other_ref,
    wa_ref,
    wb_ref,
    wc_ref,
    tb_ref,
    tc_ref,
    wide_ref,
    p_out,
    gs_out,
    sbuf,
    hbuf,
    home_ref,
    invd_ref,
    sems,
    inv_ref,
    x0s,
    liq,
    scl,
    f1,
    h1,
    h2,
    h3o,
    pf,
    rs,
    *,
    n_slots,
    cells,
):
    gx = pos_ref[0]
    gy = pos_ref[1]
    copies = [
        pltpu.make_async_copy(src, dst, sems.at[i])
        for i, (src, dst) in enumerate(
            ((home_hbm, home_ref), (invd_hbm, invd_ref))
        )
    ]
    for copy in copies:
        copy.start()

    for ref in (x0s, h1, h2):
        z = jnp.zeros(ref.shape[2:], ref.dtype)
        for X in range(PLANES):
            ref[X, 0] = z
            ref[X, NY + 1] = z
    for ref in (liq, scl, f1, pf, rs):
        for X in range(PLANES):
            ref[X] = jnp.zeros((YY, NZ), F32)
    for copy in copies:
        copy.wait()
    for s in range(n_slots):
        inv_ref[home_ref[s]] = s

    def load_plane(X, c):
        xg = 2 * gx - MID + X
        ok = jnp.where((xg >= 0) & (xg < 2 * n_slots), 1.0, 0.0).astype(F32)
        xc = jnp.clip(xg, 0, 2 * n_slots - 1)
        home = xc // 2
        half = xc - 2 * home
        slot = inv_ref[home]
        row4 = lax.broadcasted_iota(jnp.int32, (4, NZ), 0)
        for i in range(NY):
            src = (mine_ref, other_ref)[i // 8]
            fb = src[slot, half, i % 8].astype(F32) * ok
            mb = src[home, half, i % 8].astype(F32)
            y = 8 * (gy if i < 8 else 1 - gy) + i % 8
            lq = mb[2:3] * ok
            cl = mb[3:4]
            sc = jnp.zeros((1, NZ), F32)
            for k in range(4):
                sc = jnp.where(cl == k, invd_ref[k], sc)
            base = jnp.where(row4 < 2, fb, jnp.where(row4 == 2, mb * ok, 0.0))
            k12 = jnp.concatenate(
                [shift_right(base), base, shift_left(base), jnp.zeros((4, NZ), F32)], axis=0
            )
            x0s[X, y + 1] = k12.astype(BF16)
            liq[X, pl.ds(y + 1, 1), :] = lq
            scl[X, pl.ds(y + 1, 1), :] = sc * lq
            f1[X, pl.ds(y + 1, 1), :] = fb[1:2]
        return c

    lax.fori_loop(0, PLANES, load_plane, 0)

    def planes(count, body):
        def step(i, c):
            body(i)
            return c

        lax.fori_loop(0, count, step, 0)

    y4 = gy * 4 + 1

    def layer1(X, slot):
        for j in range(6):
            y = y4 + 2 * j
            Y = dot_nn(wa_ref[...], taps(x0s, X, y))
            for k in range(2):
                z = Y[:, k * NZ : (k + 1) * NZ] + wide_ref[0]
                m = liq[X, pl.ds(y + k, 1), :]
                act, sig = activate(z)
                h1[X, y + k] = (act * m).astype(BF16)
                if slot is not None:
                    sbuf[S1 + 12 * slot + 2 * j + k] = slope_of(z, sig) * m

    planes(8, lambda i: layer1(1 + i + 2 * (i // 4), None))
    planes(2, lambda i: layer1(MID + i, i))

    def layer2(X, slot):
        for j in range(6):
            y = y4 + 2 * j
            Y = dot_nn(wb_ref[...], taps(h1, X, y))
            for k in range(2):
                z = lane_taps(Y, k) + wide_ref[1]
                m = liq[X, pl.ds(y + k, 1), :]
                act, sig = activate(z)
                h2[X, y + k] = (act * m).astype(BF16)
                if slot is not None:
                    sbuf[S2 + 12 * slot + 2 * j + k] = slope_of(z, sig) * m

    planes(4, lambda i: layer2(2 + i + 4 * (i // 2), None))
    planes(4, lambda i: layer2(MID - 1 + i, i))

    y2 = gy * 6 + 1

    def layer3(X, slot, own):
        for j in range(5):
            y = y2 + 2 * j
            Y = dot_nn(wc_ref[...], taps(h2, X, y))
            for k in range(2):
                z = lane_taps(Y, k) + wide_ref[2]
                m = liq[X, pl.ds(y + k, 1), :]
                act, sig = activate(z)
                h3 = (act * m).astype(BF16)
                score = jnp.sum(wide_ref[3] * h3.astype(F32), axis=0, keepdims=True)
                pf[X, pl.ds(y + k, 1), :] = m * (score + hb_ref[0])
                sbuf[S3 + 10 * slot + 2 * j + k] = slope_of(z, sig) * m
                if own is not None:
                    h3o[own, 2 * j + k] = h3

    planes(4, lambda i: layer3(3 + i + 2 * (i // 2), i + 2 * (i // 2), None))
    planes(2, lambda i: layer3(MID + i, 2 + i, i))

    def operator(val, X):
        v = val[X, 1 : NY + 1, :]
        s = scl[X, 1 : NY + 1, :]
        q = liq[X, 1 : NY + 1, :]

        def term(nv, ns, nq):
            return 0.5 * (s * nq + ns * q) * (nv - v)

        total = term(val[X + 1, 1 : NY + 1, :], scl[X + 1, 1 : NY + 1, :], liq[X + 1, 1 : NY + 1, :])
        total += term(val[X - 1, 1 : NY + 1, :], scl[X - 1, 1 : NY + 1, :], liq[X - 1, 1 : NY + 1, :])
        total += term(val[X, 2 : NY + 2, :], scl[X, 2 : NY + 2, :], liq[X, 2 : NY + 2, :])
        total += term(val[X, 0:NY, :], scl[X, 0:NY, :], liq[X, 0:NY, :])
        total += term(shift_left(v), shift_left(s), shift_left(q))
        total += term(shift_right(v), shift_right(s), shift_right(q))
        return total

    for X in range(MID - 1, MID + 3):
        rs[X, 1 : NY + 1, :] = operator(pf, X) - liq[X, 1 : NY + 1, :] * f1[X, 1 : NY + 1, :]
    own_y = pl.ds(pl.multiple_of(gy * 8, 8) + 1, 8)
    loss = jnp.zeros((8, NZ), F32)
    for k in range(2):
        p_out[k] = pf[MID + k, own_y, :]
        r = rs[MID + k, own_y, :]
        loss += r * r
    sbuf[LOSS, 0:8, :] = loss * (1.0 / cells)
    for X in range(MID - 1, MID + 3):
        rs[X] = rs[X] * (2.0 / cells)
    for k in range(2):
        X = MID + k
        pf[k, 1 : NY + 1, :] = liq[X, 1 : NY + 1, :] * operator(rs, X)
    for k in range(2):
        gs_out[k] = pf[k, own_y, :]

    head = jnp.zeros((HID, NZ), F32)
    for i in range(16):
        X, dy = i // 8, i % 8
        head += pf[X, pl.ds(gy * 8 + 1 + dy, 1), :] * h3o[X, gy * 2 + dy].astype(F32)
    sbuf[HEAD] = head

    f0 = gy * 6

    def copy_out(i):
        for l in range(FRAME):
            r = (l % 4) * 16
            hbuf[X0 + 3 * i + l // 4, r : r + 16, :] = x0s[MID - 1 + i, f0 + l]
            hbuf[H1 + FRAME * i + l] = h1[MID - 1 + i, f0 + l]
            hbuf[H2 + FRAME * i + l] = h2[MID - 1 + i, f0 + l]

    planes(4, copy_out)
    for r in range(15):
        hbuf[WB + r] = tb_ref[r]
        hbuf[WC + r] = tc_ref[r]


def backward_kernel(
    pos_ref,
    gm_ref,
    gmo_ref,
    p1_ref,
    p1o_ref,
    p2_ref,
    p2o_ref,
    sbuf,
    hbuf,
    wide_ref,
    keep_ref,
    send_ref,
    gs,
    g3,
    g2,
    g1,
    gcat,
    hcat,
    acc,
    wbt_ref,
    wct_ref,
):
    gy = pos_ref[1]
    even = pos_ref[0] % 2 == 0
    own_half = pl.ds(pl.multiple_of(8 * gy, 8), 8)
    far_half = pl.ds(pl.multiple_of(8 - 8 * gy, 8), 8)
    for half, gm, p1, p2 in (
        (own_half, gm_ref, p1_ref, p2_ref),
        (far_half, gmo_ref, p1o_ref, p2o_ref),
    ):
        for k in range(2):
            gs[k, half, :] = jnp.where(even, p2[k], p1[k])
            gs[2 + k, half, :] = gm[k]
            gs[4 + k, half, :] = jnp.where(even, p1[k], p2[k])
    for base, ref in ((WB, wbt_ref), (WC, wct_ref)):
        for e in range(3):
            rows = slice(e * HID, (e + 1) * HID)
            for t in range(4):
                ref[rows, t * NZ : (t + 1) * NZ] = hbuf[base + 3 * t + e]
            ref[rows, 4 * NZ : 4 * NZ + HID] = hbuf[base + 12 + e][:, :HID]
    for ref in (g3, g2):
        z = jnp.zeros((HID, NZ), BF16)
        for X in range(ref.shape[0]):
            ref[X, 0] = z
            ref[X, FRAME - 1] = z

    def planes(count, body):
        def step(i, c):
            body(i)
            return c

        lax.fori_loop(0, count, step, 0)

    def back3(X):
        for j in range(10):
            g = gs[X, pl.ds(gy * 6 + j, 1), :]
            g3[X, j + 1] = (g * wide_ref[3] * sbuf[S3 + 10 * X + j]).astype(BF16)

    planes(6, back3)

    for X in range(2):
        for r in range(WROWS, ROWS, 8):
            acc[X, r : r + 8, :] = jnp.zeros((8, NZ), F32)
    own = gy * 2 + 1

    def weight_grad(g_ref, g_off, h_base, which):
        bias = jnp.zeros((HID, NZ), F32)
        for i in range(16):
            X, dy = i // 8, i % 8
            y = own + dy
            raw = g_ref[g_off + X, y]
            g = raw.astype(F32)
            bias += g
            cols = slice(i * NZ, (i + 1) * NZ)
            gcat[0:HID, cols] = shift_left(g).astype(BF16)
            gcat[HID : 2 * HID, cols] = raw
            gcat[2 * HID : 3 * HID, cols] = shift_right(g).astype(BF16)
            for a in range(3):
                for b in range(3):
                    k = 3 * a + b
                    hcat[k * HID : (k + 1) * HID, cols] = hbuf[h_base + FRAME * (X + a) + y + b - 1]
        W = dot_nt(gcat[...], hcat[...])
        for a in range(3):
            for b in range(3):
                for e in range(3):
                    t = 9 * a + 3 * b + e
                    k = 3 * a + b
                    blk = W[e * HID : (e + 1) * HID, k * HID : (k + 1) * HID]
                    acc[which, t * 32 : (t + 1) * 32, 0:HID] = blk[:32]
                    acc[which, t * 32 : (t + 1) * 32, HID:NZ] = blk[32:]
        return bias

    bias_c = weight_grad(g3, 2, H2, 1)

    def back2(X):
        for j in range(5):
            y = 1 + 2 * j
            Y = dot_nn(wct_ref[...], taps(g3, X + 1, y))
            for k in range(2):
                row = gy * 2 + 2 * j + k
                g2[X, y + k] = (lane_taps(Y, k) * sbuf[S2 + 12 * X + row]).astype(BF16)

    planes(4, back2)
    bias_b = weight_grad(g2, 1, H1, 0)

    def back1(X):
        for j in range(4):
            y = own + 2 * j
            Y = dot_nn(wbt_ref[...], taps(g2, X + 1, y))
            for k in range(2):
                row = gy * 4 + 2 * j + k
                g1[X, 2 * j + k] = (lane_taps(Y, k) * sbuf[S1 + 12 * X + row]).astype(BF16)

    planes(2, back1)
    bias_a = jnp.zeros((HID, NZ), F32)
    for i in range(16):
        X, dy = i // 8, i % 8
        y = own + dy
        cols = slice(i * NZ, (i + 1) * NZ)
        raw = g1[X, dy]
        bias_a += raw.astype(F32)
        gcat[0:HID, cols] = raw
        for a in range(3):
            for b in range(3):
                k = 3 * a + b
                l = y + b - 1
                q = l // 4
                hcat[k * 16 : (k + 1) * 16, cols] = hbuf[
                    X0 + 3 * (X + a) + q, pl.ds(pl.multiple_of((l - 4 * q) * 16, 16), 16), :
                ]
    A = dot_nt(hcat[0:144, :], gcat[0:HID, :])
    for k in range(8):
        blk = A[16 * k : 16 * k + 12]
        which, spot = k // 4, k % 4
        r0 = WROWS + 12 * (spot % 2)
        c0 = HID * (spot // 2)
        acc[which, r0 : r0 + 12, c0 : c0 + HID] = blk
    acc[1, WROWS + 24 : WROWS + 32, 0:HID] = A[128:136]
    acc[1, WROWS + 24 : WROWS + 28, HID:NZ] = A[136:140]
    sums = [
        jnp.sum(v, axis=1, keepdims=True).reshape(1, HID)
        for v in (bias_a, bias_b, bias_c, sbuf[HEAD])
    ]
    total = jnp.sum(jnp.sum(sbuf[LOSS, 0:8, :], axis=0, keepdims=True), axis=1, keepdims=True)
    keep_ref[0:ROWS] = acc[gy]
    send_ref[0:ROWS] = acc[1 - gy]
    for ref in (keep_ref, send_ref):
        ref[ROWS : ROWS + 8, :] = jnp.zeros((8, NZ), F32)
        for j in range(2):
            ref[ROWS + j : ROWS + j + 1, :] = jnp.concatenate(
                [sums[2 * j], sums[2 * j + 1]], axis=1
            )
        ref[ROWS + 2 : ROWS + 3, :] = jnp.broadcast_to(total, (1, NZ))


def finish_kernel(pos_ref, a_ref, b_ref, c_ref, d_ref, gb_hbm, gc_hbm, ga_ref, stage, first, sems):
    gy = pos_ref[1]
    upper = (pos_ref[0]) % 2

    def unpack(ref, which, half):
        for j in range(14):
            v = ref[32 * j : 32 * j + 32].astype(F32)
            stage[which, 14 * half + j, 0:32, :] = v[:, :HID]
            stage[which, 14 * half + j, 32:HID, :] = v[:, HID:]

    unpack(a_ref, gy, upper)
    unpack(b_ref, gy, 1 - upper)
    unpack(c_ref, 1 - gy, upper)
    unpack(d_ref, 1 - gy, 1 - upper)
    copies = [
        pltpu.make_async_copy(stage.at[i, pl.ds(0, 27)], dst, sems.at[i])
        for i, dst in enumerate((gb_hbm, gc_hbm))
    ]
    for copy in copies:
        copy.start()
    first[0:24] = stage[0, 27, 0:24]
    first[24:48] = stage[0, 27, 32:56]
    first[48:72] = stage[1, 27, 0:24]
    first[72:96] = stage[1, 27, 32:56]
    first[96:104] = stage[1, 27, 24:32]
    first[104:108] = stage[1, 27, 56:60]
    for ch in range(3):
        ga_ref[ch] = first[pl.ds(ch, 27, stride=4), :]
    for copy in copies:
        copy.wait()


def partner(value, bit, count):
    return lax.ppermute(value, AXES, [(i, i ^ bit) for i in range(count)])


def gather_stage(value, bit, me, count):
    other = partner(value, bit, count)
    upper = (me & bit) != 0
    return jnp.where(upper, jnp.concatenate([other, value]), jnp.concatenate([value, other]))


def two_parts(v):
    high = rounded(v)
    return high, rounded(v - high)


def rounded(v):
    return lax.reduce_precision(v, 8, 7)


def sum_all(keep, send, me, count):
    total = keep + partner(send, 1, count)
    body, tail = total[:ROWS], total[ROWS:]
    half = ROWS // 2
    upper = (me & 2) != 0
    high, low = two_parts(tail)
    away = lax.dynamic_slice_in_dim(body, jnp.where(upper, 0, half), half)
    sent = jnp.concatenate([rounded(away), high, low]).astype(BF16)
    got = partner(sent, 2, count).astype(F32)
    body = lax.dynamic_slice_in_dim(body, jnp.where(upper, half, 0), half) + got[:half]
    tail = tail + got[half : half + 8] + got[half + 8 :]
    bit = 4
    while bit < count:
        high, low = two_parts(tail)
        body = rounded(body)
        sent = jnp.concatenate([body, high, low]).astype(BF16)
        got = partner(sent, bit, count).astype(F32)
        body = body + got[:half]
        tail = (high + low) + (got[half : half + 8] + got[half + 8 :])
        bit *= 2
    body = body.astype(BF16)
    beside = partner(body, 2, count)
    far = partner(body, 1, count)
    return body, beside, far, partner(beside, 1, count), tail


def on_device(
    loaded_fields,
    brick_home,
    liquid_mask,
    density_class,
    inverse_density,
    conv_a,
    bias_a,
    conv_b,
    bias_b,
    conv_c,
    bias_c,
    head_weight,
    head_bias,
):
    n_slots = lax.axis_size("gx")
    count = n_slots * lax.axis_size("gy")
    gx = lax.axis_index("gx")
    gy = lax.axis_index("gy")
    me = gx * 2 + gy
    cells = 2 * n_slots * NY * NZ
    smem = pl.BlockSpec(memory_space=pltpu.SMEM)
    vmem = pl.BlockSpec(memory_space=pltpu.VMEM)
    params = pltpu.CompilerParams(vmem_limit_bytes=VMEM_LIMIT)

    hbm = pl.BlockSpec(memory_space=pl.ANY)

    def shaped(shape, kind):
        return jax.ShapeDtypeStruct(shape, kind)

    def off_chip(v):
        return pltpu.with_memory_space_constraint(v, pltpu.HBM)

    block = pl.pallas_call(
        payload_kernel,
        out_shape=shaped((2, 8, 4, NZ), BF16),
        in_specs=[hbm] * 3,
        out_specs=vmem,
        scratch_shapes=[
            pltpu.VMEM((2, 2, 8, NZ), BF16),
            pltpu.VMEM((2, 8, NZ), jnp.int32),
            pltpu.VMEM((2, 8, NZ), jnp.int32),
            pltpu.VMEM((2, 8, 4, NZ), F32),
            pltpu.SemaphoreType.DMA((3,)),
        ],
        compiler_params=params,
        name="payload",
    )(*map(off_chip, (loaded_fields, liquid_mask, density_class)))
    mine = block[None]
    bit = 2
    while 2 * bit < count:
        mine = gather_stage(mine, bit, me, count)
        bit *= 2
    weights = (
        conv_b,
        conv_c,
        conv_a.transpose(2, 0, 1),
        *(v.reshape(1, HID) for v in (bias_a, bias_b, bias_c, head_weight)),
    )
    mine, weights = lax.optimization_barrier((mine, weights))
    lhs = shaped((3 * HID, 9 * HID), BF16)
    turned = shaped((15, HID, NZ), BF16)
    made = pl.pallas_call(
        lhs_kernel,
        out_shape=(
            shaped((HID, 144), BF16),
            lhs,
            lhs,
            turned,
            turned,
            shaped((4, HID, NZ), F32),
        ),
        in_specs=[hbm] * 7,
        out_specs=(vmem,) * 6,
        scratch_shapes=[
            pltpu.VMEM((27, HID, HID), BF16),
            pltpu.VMEM((27, HID, HID), BF16),
            pltpu.VMEM((3, 27, HID), BF16),
            pltpu.VMEM((1, HID), F32),
            pltpu.VMEM((1, HID), F32),
            pltpu.VMEM((1, HID), F32),
            pltpu.VMEM((1, HID), BF16),
            pltpu.SemaphoreType.DMA((7,)),
        ],
        compiler_params=params,
        name="lhs",
    )(*map(off_chip, weights))
    mine = gather_stage(mine, bit, me, count)
    mine, made = lax.optimization_barrier((mine, made))
    across = partner(mine, 1, count)
    wide = made[5]

    pos = jnp.stack([gx, gy]).astype(jnp.int32)

    pressure, score, sbuf, hbuf = pl.pallas_call(
        functools.partial(forward_kernel, n_slots=n_slots, cells=cells),
        out_shape=(
            shaped((2, 8, NZ), F32),
            shaped((2, 8, NZ), F32),
            shaped((S_BLOCKS, HID, NZ), F32),
            shaped((H_BLOCKS, HID, NZ), BF16),
        ),
        in_specs=[smem] + [hbm] * 2 + [smem] + [vmem] * 8,
        out_specs=(vmem,) * 4,
        scratch_shapes=[
            pltpu.SMEM((n_slots,), jnp.int32),
            pltpu.SMEM((4,), F32),
            pltpu.SemaphoreType.DMA((2,)),
            pltpu.SMEM((n_slots,), jnp.int32),
            pltpu.VMEM((PLANES, YY, 16, NZ), BF16),
            pltpu.VMEM((PLANES, YY, NZ), F32),
            pltpu.VMEM((PLANES, YY, NZ), F32),
            pltpu.VMEM((PLANES, YY, NZ), F32),
            pltpu.VMEM((PLANES, YY, HID, NZ), BF16),
            pltpu.VMEM((PLANES, YY, HID, NZ), BF16),
            pltpu.VMEM((2, 10, HID, NZ), BF16),
            pltpu.VMEM((PLANES, YY, NZ), F32),
            pltpu.VMEM((PLANES, YY, NZ), F32),
        ],
        compiler_params=params,
        name="forward",
    )(
        pos,
        off_chip(brick_home),
        off_chip(inverse_density),
        head_bias,
        mine,
        across,
        *made,
    )

    swap1 = lax.ppermute(score, "gx", [(i, i ^ 1) for i in range(n_slots)])
    swap2 = lax.ppermute(score, "gx", [(i, ((i + 1) ^ 1) - 1) for i in range(1, n_slots - 1)])
    scores = []
    for value in (score, swap1, swap2):
        scores += [value, partner(value, 1, count)]

    keep, send = pl.pallas_call(
        backward_kernel,
        out_shape=(shaped((ROWS + 8, NZ), F32), shaped((ROWS + 8, NZ), F32)),
        in_specs=[smem] + [vmem] * 9,
        out_specs=(vmem, vmem),
        scratch_shapes=[
            pltpu.VMEM((6, NY, NZ), F32),
            pltpu.VMEM((6, FRAME, HID, NZ), BF16),
            pltpu.VMEM((4, FRAME, HID, NZ), BF16),
            pltpu.VMEM((2, 8, HID, NZ), BF16),
            pltpu.VMEM((3 * HID, 16 * NZ), BF16),
            pltpu.VMEM((9 * HID, 16 * NZ), BF16),
            pltpu.VMEM((2, ROWS, NZ), F32),
            pltpu.VMEM((3 * HID, 9 * HID), BF16),
            pltpu.VMEM((3 * HID, 9 * HID), BF16),
        ],
        compiler_params=params,
        name="backward",
    )(
        pos,
        *scores,
        sbuf,
        hbuf,
        wide,
    )

    *pieces, tail = sum_all(keep, send, me, count)
    weights = shaped((27, HID, HID), F32)
    grad_b, grad_c, grad_a = pl.pallas_call(
        finish_kernel,
        out_shape=(weights, weights, shaped((3, 27, HID), F32)),
        in_specs=[smem] + [vmem] * 4,
        out_specs=(hbm, hbm, vmem),
        scratch_shapes=[
            pltpu.VMEM((2, 28, HID, HID), F32),
            pltpu.VMEM((112, HID), F32),
            pltpu.SemaphoreType.DMA((2,)),
        ],
        compiler_params=params,
        name="finish",
    )(pos, *pieces)
    return (
        pressure,
        tail[2, :1],
        grad_a.transpose(1, 2, 0),
        tail[0, :HID],
        grad_b,
        tail[0, HID:],
        grad_c,
        tail[1, :HID],
        tail[1, HID:],
    )


def solution(mesh):
    grid = P(("grp", "gx"), "gy", None)
    part = P("grp")
    stack = P("grp", None, None)
    return jax.shard_map(
        on_device,
        mesh=mesh,
        in_specs=(P(None, ("grp", "gx"), "gy", None), part, grid, grid) + (P(),) * 9,
        out_specs=(grid, part, stack, part, stack, part, stack, part, part),
        check_vma=False,
    )
```

```python
import functools

import jax
import jax.numpy as jnp
from jax import lax
from jax.experimental import pallas as pl
from jax.experimental.pallas import tpu as pltpu
from jax.sharding import PartitionSpec as P

F32 = jnp.float32
BF16 = jnp.bfloat16
AXES = ("gx", "gy")
HID = 64
NZ = 128
NY = 16
YY = NY + 2
PLANES = 12
MID = 5
FRAME = 12
WROWS = 864
ROWS = 896
TAIL = 16
VMEM_LIMIT = 24 * 1024 * 1024
S1, S2, S3, HEAD, LOSS, S_BLOCKS = 0, 24, 72, 132, 133, 134
H1, H2, X0, WB, WC, H_BLOCKS = 0, 48, 96, 108, 144, 180


def shift_right(v):
    lane = lax.broadcasted_iota(jnp.int32, v.shape, v.ndim - 1)
    return jnp.where(lane == 0, 0.0, pltpu.roll(v, 1, v.ndim - 1))


def shift_left(v):
    lane = lax.broadcasted_iota(jnp.int32, v.shape, v.ndim - 1)
    return jnp.where(lane == NZ - 1, 0.0, pltpu.roll(v, NZ - 1, v.ndim - 1))


def dot_nn(a, b):
    return jnp.dot(a, b, preferred_element_type=F32)


def dot_nt(a, b):
    return lax.dot_general(a, b, (((1,), (1,)), ((), ())), preferred_element_type=F32)


def taps(src, X, y):
    out = []
    for a in range(3):
        for b in range(3):
            out.append(
                jnp.concatenate([src[X + a - 1, y + b - 1], src[X + a - 1, y + b]], axis=1)
            )
    return jnp.concatenate(out, axis=0)


def pair_taps(src, X, y):
    out = []
    for b in range(3):
        for x in range(4):
            out.append(
                jnp.concatenate([src[X + x - 1, y + b - 1], src[X + x - 1, y + b]], axis=1)
            )
    return jnp.concatenate(out, axis=0)


def lane_taps(Y, d, k):
    part = Y[d * 3 * HID : (d + 1) * 3 * HID, k * NZ : (k + 1) * NZ]
    return part[HID : 2 * HID] + shift_right(part[:HID]) + shift_left(part[2 * HID :])


def activate(z):
    sig = 0.5 * jnp.tanh(0.5 * z) + 0.5
    return z * sig, sig


def slope_of(z, sig):
    return sig * (1.0 + z * (1.0 - sig))


def payload_kernel(fields_hbm, liquid_hbm, class_hbm, out_ref, fields, liquid, classes, rows, sems):
    copies = [
        pltpu.make_async_copy(src, dst, sems.at[i])
        for i, (src, dst) in enumerate(
            ((fields_hbm, fields), (liquid_hbm, liquid), (class_hbm, classes))
        )
    ]
    for copy in copies:
        copy.start()
    for copy in copies:
        copy.wait()
    for x in range(2):
        planes = (fields[0, x], fields[1, x], liquid[x], classes[x])
        for p, plane in enumerate(planes):
            plane = plane.astype(F32)
            for y in range(8):
                rows[x, y, p : p + 1, :] = plane[y : y + 1]
    out_ref[...] = rows[...].astype(BF16)


def conv_lhs(w, fwd, bwd):
    zero = jnp.zeros((HID, HID), F32)
    for b in range(3):
        for e in range(3):
            ahead = [w[9 * a + 3 * b + e].astype(F32) for a in range(3)]
            back = [w[26 - (9 * a + 3 * b + e)].astype(F32) for a in range(3)]
            for d in range(2):
                for half in range(2):
                    low, high = 2 * half - d, 2 * half + 1 - d
                    rows = slice((3 * d + e) * HID, (3 * d + e + 1) * HID)
                    tile = 2 * b + half
                    pick = [
                        [v[a] if 0 <= a <= 2 else zero for a in (low, high)] for v in (ahead, back)
                    ]
                    fwd[rows, tile * NZ : (tile + 1) * NZ] = jnp.concatenate(
                        pick[0], axis=1
                    ).astype(BF16)
                    bwd[6 * tile + 3 * d + e] = jnp.concatenate(pick[1], axis=0).T.astype(BF16)


def second_lhs_kernel(wb_hbm, wa_hbm, fa, fb, tb, wb_ref, wa_ref, sems):
    copies = [
        pltpu.make_async_copy(src, dst, sems.at[i])
        for i, (src, dst) in enumerate(((wb_hbm, wb_ref), (wa_hbm, wa_ref)))
    ]
    for copy in copies:
        copy.start()
    for copy in copies:
        copy.wait()
    conv_lhs(wb_ref, fb, tb)
    tap = lax.broadcasted_iota(jnp.int32, (27, 144), 0)
    col = lax.broadcasted_iota(jnp.int32, (27, 144), 1)
    total = jnp.zeros((HID, 144), F32)
    for ch in range(3):
        spot = 16 * (tap // 3) + 4 * (tap - 3 * (tap // 3)) + ch
        pick = jnp.where(col == spot, 1.0, 0.0).astype(BF16)
        total += dot_nn(wa_ref[ch].astype(F32).T.astype(BF16), pick)
    fa[...] = total.astype(BF16)


def third_lhs_kernel(
    wc_hbm,
    ba_hbm,
    bb_hbm,
    bc_hbm,
    hw_hbm,
    fc,
    tc,
    wide_ref,
    wc_ref,
    ba_ref,
    bb_ref,
    bc_ref,
    hw_ref,
    sems,
):
    copies = [
        pltpu.make_async_copy(src, dst, sems.at[i])
        for i, (src, dst) in enumerate(
            (
                (wc_hbm, wc_ref),
                (ba_hbm, ba_ref),
                (bb_hbm, bb_ref),
                (bc_hbm, bc_ref),
                (hw_hbm, hw_ref),
            )
        )
    ]
    for copy in copies:
        copy.start()
    for copy in copies:
        copy.wait()
    for i, ref in enumerate((ba_ref, bb_ref, bc_ref, hw_ref)):
        wide_ref[i] = jnp.broadcast_to(ref[...].astype(F32), (NZ, HID)).T
    conv_lhs(wc_ref, fc, tc)


def forward_kernel(
    pos_ref,
    home_hbm,
    invd_hbm,
    hb_ref,
    mine_ref,
    other_ref,
    wa_ref,
    wb_ref,
    tb_ref,
    wc_ref,
    tc_ref,
    wide_ref,
    p_out,
    gs_out,
    sbuf,
    hbuf,
    home_ref,
    invd_ref,
    sems,
    inv_ref,
    x0s,
    liq,
    scl,
    f1,
    h1,
    h2,
    h3o,
    pf,
    rs,
    *,
    n_slots,
    cells,
):
    gx = pos_ref[0]
    gy = pos_ref[1]
    copies = [
        pltpu.make_async_copy(src, dst, sems.at[i])
        for i, (src, dst) in enumerate(
            ((home_hbm, home_ref), (invd_hbm, invd_ref))
        )
    ]
    for copy in copies:
        copy.start()

    for ref in (x0s, h1, h2):
        z = jnp.zeros(ref.shape[2:], ref.dtype)
        for X in range(PLANES):
            ref[X, 0] = z
            ref[X, NY + 1] = z
    for ref in (liq, scl, f1, pf, rs):
        for X in range(PLANES):
            ref[X] = jnp.zeros((YY, NZ), F32)
    for copy in copies:
        copy.wait()
    for s in range(n_slots):
        inv_ref[home_ref[s]] = s

    def load_plane(X, c):
        xg = 2 * gx - MID + X
        ok = jnp.where((xg >= 0) & (xg < 2 * n_slots), 1.0, 0.0).astype(F32)
        xc = jnp.clip(xg, 0, 2 * n_slots - 1)
        home = xc // 2
        half = xc - 2 * home
        slot = inv_ref[home]
        row4 = lax.broadcasted_iota(jnp.int32, (4, NZ), 0)
        for i in range(NY):
            src = (mine_ref, other_ref)[i // 8]
            fb = src[slot, half, i % 8].astype(F32) * ok
            mb = src[home, half, i % 8].astype(F32)
            y = 8 * (gy if i < 8 else 1 - gy) + i % 8
            lq = mb[2:3] * ok
            cl = mb[3:4]
            sc = jnp.zeros((1, NZ), F32)
            for k in range(4):
                sc = jnp.where(cl == k, invd_ref[k], sc)
            base = jnp.where(row4 < 2, fb, jnp.where(row4 == 2, mb * ok, 0.0))
            k12 = jnp.concatenate(
                [shift_right(base), base, shift_left(base), jnp.zeros((4, NZ), F32)], axis=0
            )
            x0s[X, y + 1] = k12.astype(BF16)
            liq[X, pl.ds(y + 1, 1), :] = lq
            scl[X, pl.ds(y + 1, 1), :] = sc * lq
            f1[X, pl.ds(y + 1, 1), :] = fb[1:2]
        return c

    lax.fori_loop(0, PLANES, load_plane, 0)

    def planes(count, body):
        def step(i, c):
            body(i)
            return c

        lax.fori_loop(0, count, step, 0)

    y4 = gy * 4 + 1

    def layer1(X, slot):
        for j in range(6):
            y = y4 + 2 * j
            Y = dot_nn(wa_ref[...], taps(x0s, X, y))
            for k in range(2):
                z = Y[:, k * NZ : (k + 1) * NZ] + wide_ref[0]
                m = liq[X, pl.ds(y + k, 1), :]
                act, sig = activate(z)
                h1[X, y + k] = (act * m).astype(BF16)
                if slot is not None:
                    sbuf[S1 + 12 * slot + 2 * j + k] = slope_of(z, sig) * m

    planes(8, lambda i: layer1(1 + i + 2 * (i // 4), None))
    planes(2, lambda i: layer1(MID + i, i))

    def layer2(X, slot):
        for j in range(6):
            y = y4 + 2 * j
            Y = dot_nn(wb_ref[...], pair_taps(h1, X, y))
            for d in range(2):
                for k in range(2):
                    z = lane_taps(Y, d, k) + wide_ref[1]
                    m = liq[X + d, pl.ds(y + k, 1), :]
                    act, sig = activate(z)
                    h2[X + d, y + k] = (act * m).astype(BF16)
                    if slot is not None:
                        sbuf[S2 + 12 * (slot + d) + 2 * j + k] = slope_of(z, sig) * m

    planes(2, lambda i: layer2(2 + 6 * i, None))
    planes(2, lambda i: layer2(MID - 1 + 2 * i, 2 * i))

    y2 = gy * 6 + 1

    def layer3(i):
        X = MID - 2 + 2 * i
        for j in range(5):
            y = y2 + 2 * j
            Y = dot_nn(wc_ref[...], pair_taps(h2, X, y))
            for d in range(2):
                for k in range(2):
                    z = lane_taps(Y, d, k) + wide_ref[2]
                    m = liq[X + d, pl.ds(y + k, 1), :]
                    act, sig = activate(z)
                    h3 = (act * m).astype(BF16)
                    score = jnp.sum(wide_ref[3] * h3.astype(F32), axis=0, keepdims=True)
                    pf[X + d, pl.ds(y + k, 1), :] = m * (score + hb_ref[0])
                    sbuf[S3 + 10 * (2 * i + d) + 2 * j + k] = slope_of(z, sig) * m
                    h3o[2 * i + d, 2 * j + k] = h3

    planes(3, layer3)

    def operator(val, X):
        v = val[X, 1 : NY + 1, :]
        s = scl[X, 1 : NY + 1, :]
        q = liq[X, 1 : NY + 1, :]

        def term(nv, ns, nq):
            return 0.5 * (s * nq + ns * q) * (nv - v)

        total = term(val[X + 1, 1 : NY + 1, :], scl[X + 1, 1 : NY + 1, :], liq[X + 1, 1 : NY + 1, :])
        total += term(val[X - 1, 1 : NY + 1, :], scl[X - 1, 1 : NY + 1, :], liq[X - 1, 1 : NY + 1, :])
        total += term(val[X, 2 : NY + 2, :], scl[X, 2 : NY + 2, :], liq[X, 2 : NY + 2, :])
        total += term(val[X, 0:NY, :], scl[X, 0:NY, :], liq[X, 0:NY, :])
        total += term(shift_left(v), shift_left(s), shift_left(q))
        total += term(shift_right(v), shift_right(s), shift_right(q))
        return total

    for X in range(MID - 1, MID + 3):
        rs[X, 1 : NY + 1, :] = operator(pf, X) - liq[X, 1 : NY + 1, :] * f1[X, 1 : NY + 1, :]
    own_y = pl.ds(pl.multiple_of(gy * 8, 8) + 1, 8)
    loss = jnp.zeros((8, NZ), F32)
    for k in range(2):
        p_out[k] = pf[MID + k, own_y, :]
        r = rs[MID + k, own_y, :]
        loss += r * r
    sbuf[LOSS, 0:8, :] = loss * (1.0 / cells)
    for X in range(MID - 1, MID + 3):
        rs[X] = rs[X] * (2.0 / cells)
    for k in range(2):
        X = MID + k
        pf[k, 1 : NY + 1, :] = liq[X, 1 : NY + 1, :] * operator(rs, X)
    for k in range(2):
        gs_out[k] = pf[k, own_y, :]

    head = jnp.zeros((HID, NZ), F32)
    for i in range(16):
        X, dy = i // 8, i % 8
        head += pf[X, pl.ds(gy * 8 + 1 + dy, 1), :] * h3o[2 + X, gy * 2 + dy].astype(F32)
    sbuf[HEAD] = head

    f0 = gy * 6

    def copy_out(i):
        for l in range(FRAME):
            r = (l % 4) * 16
            hbuf[X0 + 3 * i + l // 4, r : r + 16, :] = x0s[MID - 1 + i, f0 + l]
            hbuf[H1 + FRAME * i + l] = h1[MID - 1 + i, f0 + l]
            hbuf[H2 + FRAME * i + l] = h2[MID - 1 + i, f0 + l]

    planes(4, copy_out)
    for r in range(36):
        hbuf[WB + r] = tb_ref[r]
        hbuf[WC + r] = tc_ref[r]


def backward_kernel(
    pos_ref,
    gm_ref,
    gmo_ref,
    p2_ref,
    p2o_ref,
    p1_ref,
    p1o_ref,
    sbuf,
    hbuf,
    wide_ref,
    keep_ref,
    send_ref,
    gs,
    g3,
    g2,
    g1,
    gcat,
    hcat,
    acc,
):
    gy = pos_ref[1]
    even = pos_ref[0] % 2 == 0
    own_half = pl.ds(pl.multiple_of(8 * gy, 8), 8)
    far_half = pl.ds(pl.multiple_of(8 - 8 * gy, 8), 8)
    for half, gm, p1, p2 in (
        (own_half, gm_ref, p1_ref, p2_ref),
        (far_half, gmo_ref, p1o_ref, p2o_ref),
    ):
        for k in range(2):
            gs[k, half, :] = jnp.where(even, p2[k], p1[k])
            gs[2 + k, half, :] = gm[k]
            gs[4 + k, half, :] = jnp.where(even, p1[k], p2[k])
    def lhs_at(base):
        tiles = [
            jnp.concatenate([hbuf[base + 6 * t + r] for r in range(6)], axis=0) for t in range(6)
        ]
        return jnp.concatenate(tiles, axis=1)

    for ref in (g3, g2):
        z = jnp.zeros((HID, NZ), BF16)
        for X in range(ref.shape[0]):
            ref[X, 0] = z
            ref[X, FRAME - 1] = z

    def planes(count, body):
        def step(i, c):
            body(i)
            return c

        lax.fori_loop(0, count, step, 0)

    def back3(X):
        for j in range(10):
            g = gs[X, pl.ds(gy * 6 + j, 1), :]
            g3[X, j + 1] = (g * wide_ref[3] * sbuf[S3 + 10 * X + j]).astype(BF16)

    planes(6, back3)

    for X in range(2):
        for r in range(WROWS, ROWS, 8):
            acc[X, r : r + 8, :] = jnp.zeros((8, NZ), F32)
    own = gy * 2 + 1

    def weight_grad(g_ref, g_off, h_base, which):
        bias = jnp.zeros((HID, NZ), F32)
        for i in range(16):
            X, dy = i // 8, i % 8
            y = own + dy
            raw = g_ref[g_off + X, y]
            g = raw.astype(F32)
            bias += g
            cols = slice(i * NZ, (i + 1) * NZ)
            gcat[0:HID, cols] = shift_left(g).astype(BF16)
            gcat[HID : 2 * HID, cols] = raw
            gcat[2 * HID : 3 * HID, cols] = shift_right(g).astype(BF16)
            for a in range(3):
                for b in range(3):
                    k = 3 * a + b
                    hcat[k * HID : (k + 1) * HID, cols] = hbuf[h_base + FRAME * (X + a) + y + b - 1]
        W = dot_nt(gcat[...], hcat[...])
        for a in range(3):
            for b in range(3):
                for e in range(3):
                    t = 9 * a + 3 * b + e
                    k = 3 * a + b
                    blk = W[e * HID : (e + 1) * HID, k * HID : (k + 1) * HID]
                    acc[which, t * 32 : (t + 1) * 32, 0:HID] = blk[:32]
                    acc[which, t * 32 : (t + 1) * 32, HID:NZ] = blk[32:]
        return bias

    bias_c = weight_grad(g3, 2, H2, 1)

    def back2(i):
        X = 2 * i
        for j in range(5):
            y = 1 + 2 * j
            Y = dot_nn(lhs_at(WC), pair_taps(g3, X + 1, y))
            for d in range(2):
                for k in range(2):
                    row = gy * 2 + 2 * j + k
                    g2[X + d, y + k] = (
                        lane_taps(Y, d, k) * sbuf[S2 + 12 * (X + d) + row]
                    ).astype(BF16)

    planes(2, back2)
    bias_b = weight_grad(g2, 1, H1, 0)

    for j in range(4):
        y = own + 2 * j
        Y = dot_nn(lhs_at(WB), pair_taps(g2, 1, y))
        for d in range(2):
            for k in range(2):
                row = gy * 4 + 2 * j + k
                g1[d, 2 * j + k] = (lane_taps(Y, d, k) * sbuf[S1 + 12 * d + row]).astype(BF16)

    bias_a = jnp.zeros((HID, NZ), F32)
    for i in range(16):
        X, dy = i // 8, i % 8
        y = own + dy
        cols = slice(i * NZ, (i + 1) * NZ)
        raw = g1[X, dy]
        bias_a += raw.astype(F32)
        gcat[0:HID, cols] = raw
        for a in range(3):
            for b in range(3):
                k = 3 * a + b
                l = y + b - 1
                q = l // 4
                hcat[k * 16 : (k + 1) * 16, cols] = hbuf[
                    X0 + 3 * (X + a) + q, pl.ds(pl.multiple_of((l - 4 * q) * 16, 16), 16), :
                ]
    A = dot_nt(hcat[0:144, :], gcat[0:HID, :])
    for k in range(8):
        blk = A[16 * k : 16 * k + 12]
        which, spot = k // 4, k % 4
        r0 = WROWS + 12 * (spot % 2)
        c0 = HID * (spot // 2)
        acc[which, r0 : r0 + 12, c0 : c0 + HID] = blk
    acc[1, WROWS + 24 : WROWS + 32, 0:HID] = A[128:136]
    acc[1, WROWS + 24 : WROWS + 28, HID:NZ] = A[136:140]
    sums = [
        jnp.sum(v, axis=1, keepdims=True).reshape(1, HID)
        for v in (bias_a, bias_b, bias_c, sbuf[HEAD])
    ]
    total = jnp.sum(jnp.sum(sbuf[LOSS, 0:8, :], axis=0, keepdims=True), axis=1, keepdims=True)
    keep_ref[0:ROWS] = acc[gy]
    send_ref[0:ROWS] = acc[1 - gy]
    for ref in (keep_ref, send_ref):
        ref[ROWS : ROWS + 8, :] = jnp.zeros((8, NZ), F32)
        for j in range(2):
            ref[ROWS + j : ROWS + j + 1, :] = jnp.concatenate(
                [sums[2 * j], sums[2 * j + 1]], axis=1
            )
        ref[ROWS + 2 : ROWS + 3, :] = jnp.broadcast_to(total, (1, NZ))


def finish_kernel(pos_ref, a_ref, b_ref, c_ref, d_ref, gb_hbm, gc_hbm, ga_ref, stage, first, sems):
    gy = pos_ref[1]
    upper = (pos_ref[0]) % 2

    def unpack(ref, which, half):
        for j in range(14):
            v = ref[32 * j : 32 * j + 32].astype(F32)
            stage[which, 14 * half + j, 0:32, :] = v[:, :HID]
            stage[which, 14 * half + j, 32:HID, :] = v[:, HID:]

    unpack(a_ref, gy, upper)
    unpack(b_ref, gy, 1 - upper)
    unpack(c_ref, 1 - gy, upper)
    unpack(d_ref, 1 - gy, 1 - upper)
    copies = [
        pltpu.make_async_copy(stage.at[i, pl.ds(0, 27)], dst, sems.at[i])
        for i, dst in enumerate((gb_hbm, gc_hbm))
    ]
    for copy in copies:
        copy.start()
    first[0:24] = stage[0, 27, 0:24]
    first[24:48] = stage[0, 27, 32:56]
    first[48:72] = stage[1, 27, 0:24]
    first[72:96] = stage[1, 27, 32:56]
    first[96:104] = stage[1, 27, 24:32]
    first[104:108] = stage[1, 27, 56:60]
    for ch in range(3):
        ga_ref[ch] = first[pl.ds(ch, 27, stride=4), :]
    for copy in copies:
        copy.wait()


def partner(value, bit, count):
    return lax.ppermute(value, AXES, [(i, i ^ bit) for i in range(count)])


def gather_stage(value, bit, me, count):
    other = partner(value, bit, count)
    upper = (me & bit) != 0
    return jnp.where(upper, jnp.concatenate([other, value]), jnp.concatenate([value, other]))


def two_parts(v):
    high = rounded(v)
    return high, rounded(v - high)


def rounded(v):
    return lax.reduce_precision(v, 8, 7)


def sum_all(keep, send, me, count):
    total = keep + partner(send, 1, count)
    body, tail = total[:ROWS], total[ROWS:]
    half = ROWS // 2
    upper = (me & 2) != 0
    high, low = two_parts(tail)
    away = lax.dynamic_slice_in_dim(body, jnp.where(upper, 0, half), half)
    sent = jnp.concatenate([rounded(away), high, low]).astype(BF16)
    got = partner(sent, 2, count).astype(F32)
    body = lax.dynamic_slice_in_dim(body, jnp.where(upper, half, 0), half) + got[:half]
    tail = tail + got[half : half + 8] + got[half + 8 :]
    bit = 4
    while bit < count:
        high, low = two_parts(tail)
        body = rounded(body)
        sent = jnp.concatenate([body, high, low]).astype(BF16)
        got = partner(sent, bit, count).astype(F32)
        body = body + got[:half]
        tail = (high + low) + (got[half : half + 8] + got[half + 8 :])
        bit *= 2
    body = body.astype(BF16)
    beside = partner(body, 2, count)
    far = partner(body, 1, count)
    return body, beside, far, partner(beside, 1, count), tail


def on_device(
    loaded_fields,
    brick_home,
    liquid_mask,
    density_class,
    inverse_density,
    conv_a,
    bias_a,
    conv_b,
    bias_b,
    conv_c,
    bias_c,
    head_weight,
    head_bias,
):
    n_slots = lax.axis_size("gx")
    count = n_slots * lax.axis_size("gy")
    gx = lax.axis_index("gx")
    gy = lax.axis_index("gy")
    me = gx * 2 + gy
    cells = 2 * n_slots * NY * NZ
    smem = pl.BlockSpec(memory_space=pltpu.SMEM)
    vmem = pl.BlockSpec(memory_space=pltpu.VMEM)
    params = pltpu.CompilerParams(vmem_limit_bytes=VMEM_LIMIT)

    hbm = pl.BlockSpec(memory_space=pl.ANY)

    def shaped(shape, kind):
        return jax.ShapeDtypeStruct(shape, kind)

    def off_chip(v):
        return pltpu.with_memory_space_constraint(v, pltpu.HBM)

    block = pl.pallas_call(
        payload_kernel,
        out_shape=shaped((2, 8, 4, NZ), BF16),
        in_specs=[hbm] * 3,
        out_specs=vmem,
        scratch_shapes=[
            pltpu.VMEM((2, 2, 8, NZ), BF16),
            pltpu.VMEM((2, 8, NZ), jnp.int32),
            pltpu.VMEM((2, 8, NZ), jnp.int32),
            pltpu.VMEM((2, 8, 4, NZ), F32),
            pltpu.SemaphoreType.DMA((3,)),
        ],
        compiler_params=params,
        name="payload",
    )(*map(off_chip, (loaded_fields, liquid_mask, density_class)))
    lhs = shaped((6 * HID, 12 * HID), BF16)
    turned = shaped((36, HID, NZ), BF16)
    vector = pltpu.VMEM((1, HID), F32)

    def layouts2(args):
        return pl.pallas_call(
            second_lhs_kernel,
            out_shape=(shaped((HID, 144), BF16), lhs, turned),
            in_specs=[hbm] * 2,
            out_specs=(vmem,) * 3,
            scratch_shapes=[
                pltpu.VMEM((27, HID, HID), BF16),
                pltpu.VMEM((3, 27, HID), BF16),
                pltpu.SemaphoreType.DMA((2,)),
            ],
            compiler_params=params,
            name="lhs2",
        )(*map(off_chip, args))

    def layouts3(args):
        return pl.pallas_call(
            third_lhs_kernel,
            out_shape=(lhs, turned, shaped((4, HID, NZ), F32)),
            in_specs=[hbm] * 5,
            out_specs=(vmem,) * 3,
            scratch_shapes=[
                pltpu.VMEM((27, HID, HID), BF16),
                vector,
                vector,
                vector,
                pltpu.VMEM((1, HID), BF16),
                pltpu.SemaphoreType.DMA((5,)),
            ],
            compiler_params=params,
            name="lhs3",
        )(*map(off_chip, args))

    jobs = [
        (layouts2, (conv_b, conv_a.transpose(2, 0, 1))),
        (layouts3, (conv_c, *(v.reshape(1, HID) for v in (bias_a, bias_b, bias_c, head_weight)))),
    ]
    made = []
    mine = block[None]
    bit = 2
    while bit < count:
        if bit > 2 and jobs:
            job, args = jobs.pop(0)
            mine, args = lax.optimization_barrier((mine, args))
            results = job(args)
            mine = gather_stage(mine, bit, me, count)
            mine, results = lax.optimization_barrier((mine, results))
            made += results
        else:
            mine = gather_stage(mine, bit, me, count)
        bit *= 2
    for job, args in jobs:
        made += job(args)
    across = partner(mine, 1, count)
    wide = made[5]

    pos = jnp.stack([gx, gy]).astype(jnp.int32)

    pressure, score, sbuf, hbuf = pl.pallas_call(
        functools.partial(forward_kernel, n_slots=n_slots, cells=cells),
        out_shape=(
            shaped((2, 8, NZ), F32),
            shaped((2, 8, NZ), F32),
            shaped((S_BLOCKS, HID, NZ), F32),
            shaped((H_BLOCKS, HID, NZ), BF16),
        ),
        in_specs=[smem] + [hbm] * 2 + [smem] + [vmem] * 8,
        out_specs=(vmem,) * 4,
        scratch_shapes=[
            pltpu.SMEM((n_slots,), jnp.int32),
            pltpu.SMEM((4,), F32),
            pltpu.SemaphoreType.DMA((2,)),
            pltpu.SMEM((n_slots,), jnp.int32),
            pltpu.VMEM((PLANES, YY, 16, NZ), BF16),
            pltpu.VMEM((PLANES, YY, NZ), F32),
            pltpu.VMEM((PLANES, YY, NZ), F32),
            pltpu.VMEM((PLANES, YY, NZ), F32),
            pltpu.VMEM((PLANES, YY, HID, NZ), BF16),
            pltpu.VMEM((PLANES, YY, HID, NZ), BF16),
            pltpu.VMEM((6, 10, HID, NZ), BF16),
            pltpu.VMEM((PLANES, YY, NZ), F32),
            pltpu.VMEM((PLANES, YY, NZ), F32),
        ],
        compiler_params=params,
        name="forward",
    )(
        pos,
        off_chip(brick_home),
        off_chip(inverse_density),
        head_bias,
        mine,
        across,
        *made,
    )

    swap2 = lax.ppermute(score, "gx", [(i, ((i + 1) ^ 1) - 1) for i in range(1, n_slots - 1)])
    swap1 = lax.ppermute(score, "gx", [(i, i ^ 1) for i in range(n_slots)])
    scores = []
    for value in (score, swap2, swap1):
        scores += [value, partner(value, 1, count)]

    keep, send = pl.pallas_call(
        backward_kernel,
        out_shape=(shaped((ROWS + 8, NZ), F32), shaped((ROWS + 8, NZ), F32)),
        in_specs=[smem] + [vmem] * 9,
        out_specs=(vmem, vmem),
        scratch_shapes=[
            pltpu.VMEM((6, NY, NZ), F32),
            pltpu.VMEM((6, FRAME, HID, NZ), BF16),
            pltpu.VMEM((4, FRAME, HID, NZ), BF16),
            pltpu.VMEM((2, 8, HID, NZ), BF16),
            pltpu.VMEM((3 * HID, 16 * NZ), BF16),
            pltpu.VMEM((9 * HID, 16 * NZ), BF16),
            pltpu.VMEM((2, ROWS, NZ), F32),
        ],
        compiler_params=params,
        name="backward",
    )(
        pos,
        *scores,
        sbuf,
        hbuf,
        wide,
    )

    *pieces, tail = sum_all(keep, send, me, count)
    weights = shaped((27, HID, HID), F32)
    grad_b, grad_c, grad_a = pl.pallas_call(
        finish_kernel,
        out_shape=(weights, weights, shaped((3, 27, HID), F32)),
        in_specs=[smem] + [vmem] * 4,
        out_specs=(hbm, hbm, vmem),
        scratch_shapes=[
            pltpu.VMEM((2, 28, HID, HID), F32),
            pltpu.VMEM((112, HID), F32),
            pltpu.SemaphoreType.DMA((2,)),
        ],
        compiler_params=params,
        name="finish",
    )(pos, *pieces)
    return (
        pressure,
        tail[2, :1],
        grad_a.transpose(1, 2, 0),
        tail[0, :HID],
        grad_b,
        tail[0, HID:],
        grad_c,
        tail[1, :HID],
        tail[1, HID:],
    )


def solution(mesh):
    grid = P(("grp", "gx"), "gy", None)
    part = P("grp")
    stack = P("grp", None, None)
    return jax.shard_map(
        on_device,
        mesh=mesh,
        in_specs=(P(None, ("grp", "gx"), "gy", None), part, grid, grid) + (P(),) * 9,
        out_specs=(grid, part, stack, part, stack, part, stack, part, part),
        check_vma=False,
    )
```

```python
import functools

import jax
import jax.numpy as jnp
from jax import lax
from jax.experimental import pallas as pl
from jax.experimental.pallas import tpu as pltpu
from jax.sharding import PartitionSpec as P

F32 = jnp.float32
BF16 = jnp.bfloat16
AXES = ("gx", "gy")
HID = 64
NZ = 128
NY = 16
YY = NY + 2
PLANES = 12
MID = 5
FRAME = 12
WROWS = 864
ROWS = 896
TAIL = 16
VMEM_LIMIT = 24 * 1024 * 1024
S1, S2, S3, HEAD, LOSS, S_BLOCKS = 0, 24, 72, 132, 133, 134
H1, H2, X0, WB, WC, H_BLOCKS = 0, 48, 96, 108, 144, 180


def shift_right(v):
    lane = lax.broadcasted_iota(jnp.int32, v.shape, v.ndim - 1)
    return jnp.where(lane == 0, 0.0, pltpu.roll(v, 1, v.ndim - 1))


def shift_left(v):
    lane = lax.broadcasted_iota(jnp.int32, v.shape, v.ndim - 1)
    return jnp.where(lane == NZ - 1, 0.0, pltpu.roll(v, NZ - 1, v.ndim - 1))


def dot_nn(a, b):
    return jnp.dot(a, b, preferred_element_type=F32)


def dot_nt(a, b):
    return lax.dot_general(a, b, (((1,), (1,)), ((), ())), preferred_element_type=F32)


def taps(src, X, y):
    out = []
    for a in range(3):
        for b in range(3):
            out.append(
                jnp.concatenate([src[X + a - 1, y + b - 1], src[X + a - 1, y + b]], axis=1)
            )
    return jnp.concatenate(out, axis=0)


def pair_taps(src, X, y):
    out = []
    for b in range(3):
        for x in range(4):
            out.append(
                jnp.concatenate([src[X + x - 1, y + b - 1], src[X + x - 1, y + b]], axis=1)
            )
    return jnp.concatenate(out, axis=0)


def lane_taps(Y, d, k):
    part = Y[d * 3 * HID : (d + 1) * 3 * HID, k * NZ : (k + 1) * NZ]
    return part[HID : 2 * HID] + shift_right(part[:HID]) + shift_left(part[2 * HID :])


def activate(z):
    sig = 0.5 * jnp.tanh(0.5 * z) + 0.5
    return z * sig, sig


def slope_of(z, sig):
    return sig * (1.0 + z * (1.0 - sig))


def payload_kernel(fields_hbm, liquid_hbm, class_hbm, out_ref, fields, liquid, classes, rows, sems):
    copies = [
        pltpu.make_async_copy(src, dst, sems.at[i])
        for i, (src, dst) in enumerate(
            ((fields_hbm, fields), (liquid_hbm, liquid), (class_hbm, classes))
        )
    ]
    for copy in copies:
        copy.start()
    for copy in copies:
        copy.wait()
    for x in range(2):
        planes = (fields[0, x], fields[1, x], liquid[x], classes[x])
        for p, plane in enumerate(planes):
            plane = plane.astype(F32)
            for y in range(8):
                rows[x, y, p : p + 1, :] = plane[y : y + 1]
    out_ref[...] = rows[...].astype(BF16)


def conv_lhs(w, fwd, bwd):
    zero = jnp.zeros((HID, HID), F32)
    for b in range(3):
        for e in range(3):
            ahead = [w[9 * a + 3 * b + e].astype(F32) for a in range(3)]
            back = [w[26 - (9 * a + 3 * b + e)].astype(F32) for a in range(3)]
            for d in range(2):
                for half in range(2):
                    low, high = 2 * half - d, 2 * half + 1 - d
                    rows = slice((3 * d + e) * HID, (3 * d + e + 1) * HID)
                    tile = 2 * b + half
                    pick = [
                        [v[a] if 0 <= a <= 2 else zero for a in (low, high)] for v in (ahead, back)
                    ]
                    fwd[rows, tile * NZ : (tile + 1) * NZ] = jnp.concatenate(
                        pick[0], axis=1
                    ).astype(BF16)
                    bwd[6 * tile + 3 * d + e] = jnp.concatenate(pick[1], axis=0).T.astype(BF16)


def second_lhs_kernel(wb_hbm, wa_hbm, fa, fb, tb, wb_ref, wa_ref, sems):
    copies = [
        pltpu.make_async_copy(src, dst, sems.at[i])
        for i, (src, dst) in enumerate(((wb_hbm, wb_ref), (wa_hbm, wa_ref)))
    ]
    for copy in copies:
        copy.start()
    for copy in copies:
        copy.wait()
    conv_lhs(wb_ref, fb, tb)
    tap = lax.broadcasted_iota(jnp.int32, (27, 144), 0)
    col = lax.broadcasted_iota(jnp.int32, (27, 144), 1)
    total = jnp.zeros((HID, 144), F32)
    for ch in range(3):
        spot = 16 * (tap // 3) + 4 * (tap - 3 * (tap // 3)) + ch
        pick = jnp.where(col == spot, 1.0, 0.0).astype(BF16)
        total += dot_nn(wa_ref[ch].astype(F32).T.astype(BF16), pick)
    fa[...] = total.astype(BF16)


def third_lhs_kernel(
    wc_hbm,
    ba_hbm,
    bb_hbm,
    bc_hbm,
    hw_hbm,
    fc,
    tc,
    wide_ref,
    wc_ref,
    ba_ref,
    bb_ref,
    bc_ref,
    hw_ref,
    sems,
):
    copies = [
        pltpu.make_async_copy(src, dst, sems.at[i])
        for i, (src, dst) in enumerate(
            (
                (wc_hbm, wc_ref),
                (ba_hbm, ba_ref),
                (bb_hbm, bb_ref),
                (bc_hbm, bc_ref),
                (hw_hbm, hw_ref),
            )
        )
    ]
    for copy in copies:
        copy.start()
    for copy in copies:
        copy.wait()
    for i, ref in enumerate((ba_ref, bb_ref, bc_ref, hw_ref)):
        wide_ref[i] = jnp.broadcast_to(ref[...].astype(F32), (NZ, HID)).T
    conv_lhs(wc_ref, fc, tc)


def forward_kernel(
    pos_ref,
    home_hbm,
    invd_hbm,
    hb_ref,
    mine_ref,
    other_ref,
    wa_ref,
    wb_ref,
    tb_ref,
    wc_ref,
    tc_ref,
    wide_ref,
    p_out,
    gs_out,
    sbuf,
    hbuf,
    home_ref,
    invd_ref,
    sems,
    inv_ref,
    x0s,
    liq,
    scl,
    f1,
    h1,
    h2,
    h3o,
    pf,
    rs,
    *,
    n_slots,
    cells,
):
    gx = pos_ref[0]
    gy = pos_ref[1]
    copies = [
        pltpu.make_async_copy(src, dst, sems.at[i])
        for i, (src, dst) in enumerate(
            ((home_hbm, home_ref), (invd_hbm, invd_ref))
        )
    ]
    for copy in copies:
        copy.start()

    for ref in (x0s, h1, h2):
        z = jnp.zeros(ref.shape[2:], ref.dtype)
        for X in range(PLANES):
            ref[X, 0] = z
            ref[X, NY + 1] = z
    for ref in (liq, scl, f1, pf, rs):
        for X in range(PLANES):
            ref[X] = jnp.zeros((YY, NZ), F32)
    for copy in copies:
        copy.wait()
    for s in range(n_slots):
        inv_ref[home_ref[s]] = s

    def load_plane(X, c):
        xg = 2 * gx - MID + X
        ok = jnp.where((xg >= 0) & (xg < 2 * n_slots), 1.0, 0.0).astype(F32)
        xc = jnp.clip(xg, 0, 2 * n_slots - 1)
        home = xc // 2
        half = xc - 2 * home
        slot = inv_ref[home]
        row4 = lax.broadcasted_iota(jnp.int32, (4, NZ), 0)
        for i in range(NY):
            src = (mine_ref, other_ref)[i // 8]
            fb = src[slot, half, i % 8].astype(F32) * ok
            mb = src[home, half, i % 8].astype(F32)
            y = 8 * (gy if i < 8 else 1 - gy) + i % 8
            lq = mb[2:3] * ok
            cl = mb[3:4]
            sc = jnp.zeros((1, NZ), F32)
            for k in range(4):
                sc = jnp.where(cl == k, invd_ref[k], sc)
            base = jnp.where(row4 < 2, fb, jnp.where(row4 == 2, mb * ok, 0.0))
            k12 = jnp.concatenate(
                [shift_right(base), base, shift_left(base), jnp.zeros((4, NZ), F32)], axis=0
            )
            x0s[X, y + 1] = k12.astype(BF16)
            liq[X, pl.ds(y + 1, 1), :] = lq
            scl[X, pl.ds(y + 1, 1), :] = sc * lq
            f1[X, pl.ds(y + 1, 1), :] = fb[1:2]
        return c

    lax.fori_loop(0, PLANES, load_plane, 0)

    def planes(count, body):
        def step(i, c):
            body(i)
            return c

        lax.fori_loop(0, count, step, 0)

    y4 = gy * 4 + 1

    def layer1(X, slot):
        for j in range(6):
            y = y4 + 2 * j
            Y = dot_nn(wa_ref[...], taps(x0s, X, y))
            for k in range(2):
                z = Y[:, k * NZ : (k + 1) * NZ] + wide_ref[0]
                m = liq[X, pl.ds(y + k, 1), :]
                act, sig = activate(z)
                h1[X, y + k] = (act * m).astype(BF16)
                if slot is not None:
                    sbuf[S1 + 12 * slot + 2 * j + k] = slope_of(z, sig) * m

    planes(8, lambda i: layer1(1 + i + 2 * (i // 4), None))
    planes(2, lambda i: layer1(MID + i, i))

    def layer2(X, slot):
        for j in range(6):
            y = y4 + 2 * j
            Y = dot_nn(wb_ref[...], pair_taps(h1, X, y))
            for d in range(2):
                for k in range(2):
                    z = lane_taps(Y, d, k) + wide_ref[1]
                    m = liq[X + d, pl.ds(y + k, 1), :]
                    act, sig = activate(z)
                    h2[X + d, y + k] = (act * m).astype(BF16)
                    if slot is not None:
                        sbuf[S2 + 12 * (slot + d) + 2 * j + k] = slope_of(z, sig) * m

    planes(2, lambda i: layer2(2 + 6 * i, None))
    planes(2, lambda i: layer2(MID - 1 + 2 * i, 2 * i))

    y2 = gy * 6 + 1

    def layer3(i):
        X = MID - 2 + 2 * i
        for j in range(5):
            y = y2 + 2 * j
            Y = dot_nn(wc_ref[...], pair_taps(h2, X, y))
            for d in range(2):
                for k in range(2):
                    z = lane_taps(Y, d, k) + wide_ref[2]
                    m = liq[X + d, pl.ds(y + k, 1), :]
                    act, sig = activate(z)
                    h3 = (act * m).astype(BF16)
                    score = jnp.sum(wide_ref[3] * h3.astype(F32), axis=0, keepdims=True)
                    pf[X + d, pl.ds(y + k, 1), :] = m * (score + hb_ref[0])
                    sbuf[S3 + 10 * (2 * i + d) + 2 * j + k] = slope_of(z, sig) * m
                    h3o[2 * i + d, 2 * j + k] = h3

    planes(3, layer3)

    def operator(val, X):
        v = val[X, 1 : NY + 1, :]
        s = scl[X, 1 : NY + 1, :]
        q = liq[X, 1 : NY + 1, :]

        def term(nv, ns, nq):
            return 0.5 * (s * nq + ns * q) * (nv - v)

        total = term(val[X + 1, 1 : NY + 1, :], scl[X + 1, 1 : NY + 1, :], liq[X + 1, 1 : NY + 1, :])
        total += term(val[X - 1, 1 : NY + 1, :], scl[X - 1, 1 : NY + 1, :], liq[X - 1, 1 : NY + 1, :])
        total += term(val[X, 2 : NY + 2, :], scl[X, 2 : NY + 2, :], liq[X, 2 : NY + 2, :])
        total += term(val[X, 0:NY, :], scl[X, 0:NY, :], liq[X, 0:NY, :])
        total += term(shift_left(v), shift_left(s), shift_left(q))
        total += term(shift_right(v), shift_right(s), shift_right(q))
        return total

    for X in range(MID - 1, MID + 3):
        rs[X, 1 : NY + 1, :] = operator(pf, X) - liq[X, 1 : NY + 1, :] * f1[X, 1 : NY + 1, :]
    own_y = pl.ds(pl.multiple_of(gy * 8, 8) + 1, 8)
    loss = jnp.zeros((8, NZ), F32)
    for k in range(2):
        p_out[k] = pf[MID + k, own_y, :]
        r = rs[MID + k, own_y, :]
        loss += r * r
    sbuf[LOSS, 0:8, :] = loss * (1.0 / cells)
    for X in range(MID - 1, MID + 3):
        rs[X] = rs[X] * (2.0 / cells)
    for k in range(2):
        X = MID + k
        pf[k, 1 : NY + 1, :] = liq[X, 1 : NY + 1, :] * operator(rs, X)
    for k in range(2):
        gs_out[k] = pf[k, own_y, :]

    head = jnp.zeros((HID, NZ), F32)
    for i in range(16):
        X, dy = i // 8, i % 8
        head += pf[X, pl.ds(gy * 8 + 1 + dy, 1), :] * h3o[2 + X, gy * 2 + dy].astype(F32)
    sbuf[HEAD] = head

    f0 = gy * 6

    def copy_out(i):
        for l in range(FRAME):
            r = (l % 4) * 16
            hbuf[X0 + 3 * i + l // 4, r : r + 16, :] = x0s[MID - 1 + i, f0 + l]
            hbuf[H1 + FRAME * i + l] = h1[MID - 1 + i, f0 + l]
            hbuf[H2 + FRAME * i + l] = h2[MID - 1 + i, f0 + l]

    planes(4, copy_out)
    for r in range(36):
        hbuf[WB + r] = tb_ref[r]
        hbuf[WC + r] = tc_ref[r]


def stack_gradient(raw, gcat, cols):
    g = raw.astype(F32)
    gcat[0:HID, cols] = shift_left(g).astype(BF16)
    gcat[HID : 2 * HID, cols] = raw
    gcat[2 * HID : 3 * HID, cols] = shift_right(g).astype(BF16)
    return g


def store_weights(W, ref):
    for a in range(3):
        for b in range(3):
            for e in range(3):
                t = 9 * a + 3 * b + e
                k = 3 * a + b
                blk = W[e * HID : (e + 1) * HID, k * HID : (k + 1) * HID]
                ref[t * 32 : (t + 1) * 32, 0:HID] = blk[:32]
                ref[t * 32 : (t + 1) * 32, HID:NZ] = blk[32:]


def early_kernel(pos_ref, score_ref, sbuf, hbuf, wide_ref, gc_ref, bias_ref, cat_ref, gcat, hcat):
    gy = pos_ref[1]
    own = gy * 2 + 1
    bias = jnp.zeros((HID, NZ), F32)
    for i in range(16):
        X, dy = i // 8, i % 8
        y = own + dy
        g = score_ref[X, dy : dy + 1, :]
        raw = (g * wide_ref[3] * sbuf[S3 + 10 * (X + 2) + y - 1]).astype(BF16)
        cols = slice(i * NZ, (i + 1) * NZ)
        bias += stack_gradient(raw, gcat, cols)
        for a in range(3):
            for b in range(3):
                k = 3 * a + b
                row = FRAME * (X + a) + y + b - 1
                hcat[k * HID : (k + 1) * HID, cols] = hbuf[H2 + row]
                cat_ref[k * HID : (k + 1) * HID, cols] = hbuf[H1 + row]
                l = y + b - 1
                q = l // 4
                cat_ref[9 * HID + k * 16 : 9 * HID + (k + 1) * 16, cols] = hbuf[
                    X0 + 3 * (X + a) + q, pl.ds(pl.multiple_of((l - 4 * q) * 16, 16), 16), :
                ]
    bias_ref[...] = bias
    store_weights(dot_nt(gcat[...], hcat[...]), gc_ref)


def backward_kernel(
    pos_ref,
    gm_ref,
    gmo_ref,
    p2_ref,
    p2o_ref,
    p1_ref,
    p1o_ref,
    sbuf,
    hbuf,
    wide_ref,
    gc_ref,
    bias_ref,
    cat_ref,
    keep_ref,
    send_ref,
    gs,
    g3,
    g2,
    g1,
    gcat,
    acc,
):
    gy = pos_ref[1]
    even = pos_ref[0] % 2 == 0
    own_half = pl.ds(pl.multiple_of(8 * gy, 8), 8)
    far_half = pl.ds(pl.multiple_of(8 - 8 * gy, 8), 8)
    for half, gm, p1, p2 in (
        (own_half, gm_ref, p1_ref, p2_ref),
        (far_half, gmo_ref, p1o_ref, p2o_ref),
    ):
        for k in range(2):
            gs[k, half, :] = jnp.where(even, p2[k], p1[k])
            gs[2 + k, half, :] = gm[k]
            gs[4 + k, half, :] = jnp.where(even, p1[k], p2[k])

    def lhs_at(base):
        tiles = [
            jnp.concatenate([hbuf[base + 6 * t + r] for r in range(6)], axis=0) for t in range(6)
        ]
        return jnp.concatenate(tiles, axis=1)

    for ref in (g3, g2):
        z = jnp.zeros((HID, NZ), BF16)
        for X in range(ref.shape[0]):
            ref[X, 0] = z
            ref[X, FRAME - 1] = z

    def planes(count, body):
        def step(i, c):
            body(i)
            return c

        lax.fori_loop(0, count, step, 0)

    def back3(X):
        for j in range(10):
            g = gs[X, pl.ds(gy * 6 + j, 1), :]
            g3[X, j + 1] = (g * wide_ref[3] * sbuf[S3 + 10 * X + j]).astype(BF16)

    planes(6, back3)

    for X in range(2):
        for r in range(WROWS, ROWS, 8):
            acc[X, r : r + 8, :] = jnp.zeros((8, NZ), F32)
    own = gy * 2 + 1

    def back2(i):
        X = 2 * i
        for j in range(5):
            y = 1 + 2 * j
            Y = dot_nn(lhs_at(WC), pair_taps(g3, X + 1, y))
            for d in range(2):
                for k in range(2):
                    row = gy * 2 + 2 * j + k
                    g2[X + d, y + k] = (
                        lane_taps(Y, d, k) * sbuf[S2 + 12 * (X + d) + row]
                    ).astype(BF16)

    planes(2, back2)
    bias_b = jnp.zeros((HID, NZ), F32)
    for i in range(16):
        cols = slice(i * NZ, (i + 1) * NZ)
        bias_b += stack_gradient(g2[1 + i // 8, own + i % 8], gcat, cols)
    store_weights(dot_nt(gcat[...], cat_ref[0 : 9 * HID, :]), acc.at[0])

    for j in range(4):
        y = own + 2 * j
        Y = dot_nn(lhs_at(WB), pair_taps(g2, 1, y))
        for d in range(2):
            for k in range(2):
                row = gy * 4 + 2 * j + k
                g1[d, 2 * j + k] = (lane_taps(Y, d, k) * sbuf[S1 + 12 * d + row]).astype(BF16)

    bias_a = jnp.zeros((HID, NZ), F32)
    for i in range(16):
        raw = g1[i // 8, i % 8]
        bias_a += raw.astype(F32)
        gcat[0:HID, i * NZ : (i + 1) * NZ] = raw
    A = dot_nt(cat_ref[9 * HID : 9 * HID + 144, :], gcat[0:HID, :])
    for k in range(8):
        blk = A[16 * k : 16 * k + 12]
        which, spot = k // 4, k % 4
        r0 = WROWS + 12 * (spot % 2)
        c0 = HID * (spot // 2)
        acc[which, r0 : r0 + 12, c0 : c0 + HID] = blk
    acc[1, WROWS + 24 : WROWS + 32, 0:HID] = A[128:136]
    acc[1, WROWS + 24 : WROWS + 28, HID:NZ] = A[136:140]
    sums = [
        jnp.sum(v, axis=1, keepdims=True).reshape(1, HID)
        for v in (bias_a, bias_b, bias_ref[...], sbuf[HEAD])
    ]
    total = jnp.sum(jnp.sum(sbuf[LOSS, 0:8, :], axis=0, keepdims=True), axis=1, keepdims=True)
    acc[1, 0:WROWS, :] = gc_ref[...]
    keep_ref[0:ROWS] = acc[gy]
    send_ref[0:ROWS] = acc[1 - gy]
    for ref in (keep_ref, send_ref):
        ref[ROWS : ROWS + 8, :] = jnp.zeros((8, NZ), F32)
        for j in range(2):
            ref[ROWS + j : ROWS + j + 1, :] = jnp.concatenate(
                [sums[2 * j], sums[2 * j + 1]], axis=1
            )
        ref[ROWS + 2 : ROWS + 3, :] = jnp.broadcast_to(total, (1, NZ))


def unpack_half(pos_ref, half, mine_ref, far_ref, stage, gb_hbm, gc_hbm, sems):
    gy = pos_ref[1]
    for ref, which in ((mine_ref, gy), (far_ref, 1 - gy)):
        for j in range(14):
            v = ref[32 * j : 32 * j + 32].astype(F32)
            stage[which, j, 0:32, :] = v[:, :HID]
            stage[which, j, 32:HID, :] = v[:, HID:]
    most = [
        pltpu.make_async_copy(stage.at[i, pl.ds(0, 13)], dst.at[pl.ds(14 * half, 13)], sems.at[i])
        for i, dst in enumerate((gb_hbm, gc_hbm))
    ]
    rest = [
        pltpu.make_async_copy(stage.at[i, 13], dst.at[13], sems.at[2 + i])
        for i, dst in enumerate((gb_hbm, gc_hbm))
    ]
    for copy in most:
        copy.start()

    @pl.when(half == 0)
    def _():
        for copy in rest:
            copy.start()
        for copy in rest:
            copy.wait()

    return most


def near_kernel(pos_ref, mine_ref, far_ref, gb_hbm, gc_hbm, extra_ref, stage, sems):
    half = pos_ref[0] % 2
    most = unpack_half(pos_ref, half, mine_ref, far_ref, stage, gb_hbm, gc_hbm, sems)
    for i in range(2):
        extra_ref[i] = stage[i, 13]
    for copy in most:
        copy.wait()


def finish_kernel(
    pos_ref, mine_ref, far_ref, extra_ref, gb_in, gc_in, gb_hbm, gc_hbm, ga_ref, stage, first, sems
):
    half = 1 - pos_ref[0] % 2
    most = unpack_half(pos_ref, half, mine_ref, far_ref, stage, gb_hbm, gc_hbm, sems)
    zero, one = [jnp.where(half == 1, stage[i, 13], extra_ref[i]) for i in range(2)]
    first[0:24] = zero[0:24]
    first[24:48] = zero[32:56]
    first[48:72] = one[0:24]
    first[72:96] = one[32:56]
    first[96:104] = one[24:32]
    first[104:108] = one[56:60]
    for ch in range(3):
        ga_ref[ch] = first[pl.ds(ch, 27, stride=4), :]
    for copy in most:
        copy.wait()


def partner(value, bit, count):
    return lax.ppermute(value, AXES, [(i, i ^ bit) for i in range(count)])


def gather_stage(value, bit, me, count):
    other = partner(value, bit, count)
    upper = (me & bit) != 0
    return jnp.where(upper, jnp.concatenate([other, value]), jnp.concatenate([value, other]))


def two_parts(v):
    high = rounded(v)
    return high, rounded(v - high)


def rounded(v):
    return lax.reduce_precision(v, 8, 7)


def sum_all(keep, send, me, count):
    total = keep + partner(send, 1, count)
    body, tail = total[:ROWS], total[ROWS:]
    half = ROWS // 2
    upper = (me & 2) != 0
    high, low = two_parts(tail)
    away = lax.dynamic_slice_in_dim(body, jnp.where(upper, 0, half), half)
    sent = jnp.concatenate([rounded(away), high, low]).astype(BF16)
    got = partner(sent, 2, count).astype(F32)
    body = lax.dynamic_slice_in_dim(body, jnp.where(upper, half, 0), half) + got[:half]
    tail = tail + got[half : half + 8] + got[half + 8 :]
    bit = 4
    while bit < count:
        high, low = two_parts(tail)
        body = rounded(body)
        sent = jnp.concatenate([body, high, low]).astype(BF16)
        got = partner(sent, bit, count).astype(F32)
        body = body + got[:half]
        tail = (high + low) + (got[half : half + 8] + got[half + 8 :])
        bit *= 2
    body = body.astype(BF16)
    beside = partner(body, 2, count)
    far = partner(body, 1, count)
    return body, far, beside, tail


def on_device(
    loaded_fields,
    brick_home,
    liquid_mask,
    density_class,
    inverse_density,
    conv_a,
    bias_a,
    conv_b,
    bias_b,
    conv_c,
    bias_c,
    head_weight,
    head_bias,
):
    n_slots = lax.axis_size("gx")
    count = n_slots * lax.axis_size("gy")
    gx = lax.axis_index("gx")
    gy = lax.axis_index("gy")
    me = gx * 2 + gy
    cells = 2 * n_slots * NY * NZ
    smem = pl.BlockSpec(memory_space=pltpu.SMEM)
    vmem = pl.BlockSpec(memory_space=pltpu.VMEM)
    params = pltpu.CompilerParams(vmem_limit_bytes=VMEM_LIMIT)

    hbm = pl.BlockSpec(memory_space=pl.ANY)

    def shaped(shape, kind):
        return jax.ShapeDtypeStruct(shape, kind)

    def off_chip(v):
        return pltpu.with_memory_space_constraint(v, pltpu.HBM)

    block = pl.pallas_call(
        payload_kernel,
        out_shape=shaped((2, 8, 4, NZ), BF16),
        in_specs=[hbm] * 3,
        out_specs=vmem,
        scratch_shapes=[
            pltpu.VMEM((2, 2, 8, NZ), BF16),
            pltpu.VMEM((2, 8, NZ), jnp.int32),
            pltpu.VMEM((2, 8, NZ), jnp.int32),
            pltpu.VMEM((2, 8, 4, NZ), F32),
            pltpu.SemaphoreType.DMA((3,)),
        ],
        compiler_params=params,
        name="payload",
    )(*map(off_chip, (loaded_fields, liquid_mask, density_class)))
    lhs = shaped((6 * HID, 12 * HID), BF16)
    turned = shaped((36, HID, NZ), BF16)
    vector = pltpu.VMEM((1, HID), F32)

    def layouts2(args):
        return pl.pallas_call(
            second_lhs_kernel,
            out_shape=(shaped((HID, 144), BF16), lhs, turned),
            in_specs=[hbm] * 2,
            out_specs=(vmem,) * 3,
            scratch_shapes=[
                pltpu.VMEM((27, HID, HID), BF16),
                pltpu.VMEM((3, 27, HID), BF16),
                pltpu.SemaphoreType.DMA((2,)),
            ],
            compiler_params=params,
            name="lhs2",
        )(*map(off_chip, args))

    def layouts3(args):
        return pl.pallas_call(
            third_lhs_kernel,
            out_shape=(lhs, turned, shaped((4, HID, NZ), F32)),
            in_specs=[hbm] * 5,
            out_specs=(vmem,) * 3,
            scratch_shapes=[
                pltpu.VMEM((27, HID, HID), BF16),
                vector,
                vector,
                vector,
                pltpu.VMEM((1, HID), BF16),
                pltpu.SemaphoreType.DMA((5,)),
            ],
            compiler_params=params,
            name="lhs3",
        )(*map(off_chip, args))

    jobs = [
        (layouts2, (conv_b, conv_a.transpose(2, 0, 1))),
        (layouts3, (conv_c, *(v.reshape(1, HID) for v in (bias_a, bias_b, bias_c, head_weight)))),
    ]
    made = []
    mine = block[None]
    bit = 2
    while bit < count:
        if bit > 2 and jobs:
            job, args = jobs.pop(0)
            mine, args = lax.optimization_barrier((mine, args))
            results = job(args)
            mine = gather_stage(mine, bit, me, count)
            mine, results = lax.optimization_barrier((mine, results))
            made += results
        else:
            mine = gather_stage(mine, bit, me, count)
        bit *= 2
    for job, args in jobs:
        made += job(args)
    across = partner(mine, 1, count)
    wide = made[5]

    pos = jnp.stack([gx, gy]).astype(jnp.int32)

    pressure, score, sbuf, hbuf = pl.pallas_call(
        functools.partial(forward_kernel, n_slots=n_slots, cells=cells),
        out_shape=(
            shaped((2, 8, NZ), F32),
            shaped((2, 8, NZ), F32),
            shaped((S_BLOCKS, HID, NZ), F32),
            shaped((H_BLOCKS, HID, NZ), BF16),
        ),
        in_specs=[smem] + [hbm] * 2 + [smem] + [vmem] * 8,
        out_specs=(vmem,) * 4,
        scratch_shapes=[
            pltpu.SMEM((n_slots,), jnp.int32),
            pltpu.SMEM((4,), F32),
            pltpu.SemaphoreType.DMA((2,)),
            pltpu.SMEM((n_slots,), jnp.int32),
            pltpu.VMEM((PLANES, YY, 16, NZ), BF16),
            pltpu.VMEM((PLANES, YY, NZ), F32),
            pltpu.VMEM((PLANES, YY, NZ), F32),
            pltpu.VMEM((PLANES, YY, NZ), F32),
            pltpu.VMEM((PLANES, YY, HID, NZ), BF16),
            pltpu.VMEM((PLANES, YY, HID, NZ), BF16),
            pltpu.VMEM((6, 10, HID, NZ), BF16),
            pltpu.VMEM((PLANES, YY, NZ), F32),
            pltpu.VMEM((PLANES, YY, NZ), F32),
        ],
        compiler_params=params,
        name="forward",
    )(
        pos,
        off_chip(brick_home),
        off_chip(inverse_density),
        head_bias,
        mine,
        across,
        *made,
    )

    swap2 = lax.ppermute(score, "gx", [(i, ((i + 1) ^ 1) - 1) for i in range(1, n_slots - 1)])
    swap1 = lax.ppermute(score, "gx", [(i, i ^ 1) for i in range(n_slots)])
    across_score = partner(score, 1, count)
    early = pl.pallas_call(
        early_kernel,
        out_shape=(
            shaped((WROWS, NZ), F32),
            shaped((HID, NZ), F32),
            shaped((9 * HID + 144, 16 * NZ), BF16),
        ),
        in_specs=[smem] + [vmem] * 4,
        out_specs=(vmem,) * 3,
        scratch_shapes=[
            pltpu.VMEM((3 * HID, 16 * NZ), BF16),
            pltpu.VMEM((9 * HID, 16 * NZ), BF16),
        ],
        compiler_params=params,
        name="early",
    )(pos, score, sbuf, hbuf, wide)
    early, swap2, swap1 = lax.optimization_barrier((early, swap2, swap1))
    scores = [score, across_score]
    for value in (swap2, swap1):
        scores += [value, partner(value, 1, count)]

    keep, send = pl.pallas_call(
        backward_kernel,
        out_shape=(shaped((ROWS + 8, NZ), F32), shaped((ROWS + 8, NZ), F32)),
        in_specs=[smem] + [vmem] * 12,
        out_specs=(vmem, vmem),
        scratch_shapes=[
            pltpu.VMEM((6, NY, NZ), F32),
            pltpu.VMEM((6, FRAME, HID, NZ), BF16),
            pltpu.VMEM((4, FRAME, HID, NZ), BF16),
            pltpu.VMEM((2, 8, HID, NZ), BF16),
            pltpu.VMEM((3 * HID, 16 * NZ), BF16),
            pltpu.VMEM((2, ROWS, NZ), F32),
        ],
        compiler_params=params,
        name="backward",
    )(
        pos,
        *scores,
        sbuf,
        hbuf,
        wide,
        *early,
    )

    body, far, beside, tail = sum_all(keep, send, me, count)
    weights = shaped((27, HID, HID), F32)
    stage = pltpu.VMEM((2, 14, HID, HID), F32)
    near = pl.pallas_call(
        near_kernel,
        out_shape=(weights, weights, shaped((2, HID, HID), F32)),
        in_specs=[smem] + [vmem] * 2,
        out_specs=(hbm, hbm, vmem),
        scratch_shapes=[stage, pltpu.SemaphoreType.DMA((4,))],
        compiler_params=params,
        name="near",
    )(pos, body, far)
    near, beside = lax.optimization_barrier((near, beside))
    half_b, half_c, extra = near
    grad_b, grad_c, grad_a = pl.pallas_call(
        finish_kernel,
        out_shape=(weights, weights, shaped((3, 27, HID), F32)),
        in_specs=[smem] + [vmem] * 3 + [hbm] * 2,
        out_specs=(hbm, hbm, vmem),
        scratch_shapes=[
            stage,
            pltpu.VMEM((112, HID), F32),
            pltpu.SemaphoreType.DMA((4,)),
        ],
        input_output_aliases={4: 0, 5: 1},
        compiler_params=params,
        name="finish",
    )(pos, beside, partner(beside, 1, count), extra, half_b, half_c)
    return (
        pressure,
        tail[2, :1],
        grad_a.transpose(1, 2, 0),
        tail[0, :HID],
        grad_b,
        tail[0, HID:],
        grad_c,
        tail[1, :HID],
        tail[1, HID:],
    )


def solution(mesh):
    grid = P(("grp", "gx"), "gy", None)
    part = P("grp")
    stack = P("grp", None, None)
    return jax.shard_map(
        on_device,
        mesh=mesh,
        in_specs=(P(None, ("grp", "gx"), "gy", None), part, grid, grid) + (P(),) * 9,
        out_specs=(grid, part, stack, part, stack, part, stack, part, part),
        check_vma=False,
    )
```

```python
import functools

import jax
import jax.numpy as jnp
from jax import lax
from jax.experimental import pallas as pl
from jax.experimental.pallas import tpu as pltpu
from jax.sharding import PartitionSpec as P

F32 = jnp.float32
BF16 = jnp.bfloat16
AXES = ("gx", "gy")
HID = 64
NZ = 128
NY = 16
YY = NY + 2
PLANES = 12
MID = 5
FRAME = 12
WROWS = 864
ROWS = 896
TAIL = 16
VMEM_LIMIT = 24 * 1024 * 1024
S1, S2, S3, HEAD, LOSS, S_BLOCKS = 0, 24, 72, 132, 133, 134
H1, H2, X0, WB, WC, H_BLOCKS = 0, 48, 96, 108, 144, 180


def shift_right(v):
    lane = lax.broadcasted_iota(jnp.int32, v.shape, v.ndim - 1)
    return jnp.where(lane == 0, 0.0, pltpu.roll(v, 1, v.ndim - 1))


def shift_left(v):
    lane = lax.broadcasted_iota(jnp.int32, v.shape, v.ndim - 1)
    return jnp.where(lane == NZ - 1, 0.0, pltpu.roll(v, NZ - 1, v.ndim - 1))


def dot_nn(a, b):
    return jnp.dot(a, b, preferred_element_type=F32)


def dot_nt(a, b):
    return lax.dot_general(a, b, (((1,), (1,)), ((), ())), preferred_element_type=F32)


def taps(src, X, y):
    out = []
    for a in range(3):
        for b in range(3):
            out.append(
                jnp.concatenate([src[X + a - 1, y + b - 1], src[X + a - 1, y + b]], axis=1)
            )
    return jnp.concatenate(out, axis=0)


def pair_taps(src, X, y):
    out = []
    for b in range(3):
        for x in range(4):
            out.append(
                jnp.concatenate([src[X + x - 1, y + b - 1], src[X + x - 1, y + b]], axis=1)
            )
    return jnp.concatenate(out, axis=0)


def lane_taps(Y, d, k):
    part = Y[d * 3 * HID : (d + 1) * 3 * HID, k * NZ : (k + 1) * NZ]
    return part[HID : 2 * HID] + shift_right(part[:HID]) + shift_left(part[2 * HID :])


def activate(z):
    sig = 0.5 * jnp.tanh(0.5 * z) + 0.5
    return z * sig, sig


def slope_of(z, sig):
    return sig * (1.0 + z * (1.0 - sig))


def payload_kernel(fields_hbm, liquid_hbm, class_hbm, out_ref, fields, liquid, classes, rows, sems):
    copies = [
        pltpu.make_async_copy(src, dst, sems.at[i])
        for i, (src, dst) in enumerate(
            ((fields_hbm, fields), (liquid_hbm, liquid), (class_hbm, classes))
        )
    ]
    for copy in copies:
        copy.start()
    for copy in copies:
        copy.wait()
    for x in range(2):
        planes = (fields[0, x], fields[1, x], liquid[x], classes[x])
        for p, plane in enumerate(planes):
            plane = plane.astype(F32)
            for y in range(8):
                rows[x, y, p : p + 1, :] = plane[y : y + 1]
    out_ref[...] = rows[...].astype(BF16)


def conv_lhs(w, fwd, bwd):
    zero = jnp.zeros((HID, HID), F32)
    for b in range(3):
        for e in range(3):
            ahead = [w[9 * a + 3 * b + e].astype(F32) for a in range(3)]
            back = [w[26 - (9 * a + 3 * b + e)].astype(F32) for a in range(3)]
            for d in range(2):
                for half in range(2):
                    low, high = 2 * half - d, 2 * half + 1 - d
                    rows = slice((3 * d + e) * HID, (3 * d + e + 1) * HID)
                    tile = 2 * b + half
                    pick = [
                        [v[a] if 0 <= a <= 2 else zero for a in (low, high)] for v in (ahead, back)
                    ]
                    fwd[rows, tile * NZ : (tile + 1) * NZ] = jnp.concatenate(
                        pick[0], axis=1
                    ).astype(BF16)
                    bwd[6 * tile + 3 * d + e] = jnp.concatenate(pick[1], axis=0).T.astype(BF16)


def second_lhs_kernel(wb_hbm, wa_hbm, fa, fb, tb, wb_ref, wa_ref, sems):
    copies = [
        pltpu.make_async_copy(src, dst, sems.at[i])
        for i, (src, dst) in enumerate(((wb_hbm, wb_ref), (wa_hbm, wa_ref)))
    ]
    for copy in copies:
        copy.start()
    for copy in copies:
        copy.wait()
    conv_lhs(wb_ref, fb, tb)
    tap = lax.broadcasted_iota(jnp.int32, (27, 144), 0)
    col = lax.broadcasted_iota(jnp.int32, (27, 144), 1)
    total = jnp.zeros((HID, 144), F32)
    for ch in range(3):
        spot = 16 * (tap // 3) + 4 * (tap - 3 * (tap // 3)) + ch
        pick = jnp.where(col == spot, 1.0, 0.0).astype(BF16)
        total += dot_nn(wa_ref[ch].astype(F32).T.astype(BF16), pick)
    fa[...] = total.astype(BF16)


def third_lhs_kernel(
    wc_hbm,
    ba_hbm,
    bb_hbm,
    bc_hbm,
    hw_hbm,
    home_hbm,
    invd_hbm,
    fc,
    tc,
    wide_ref,
    home_ref,
    invd_ref,
    wc_ref,
    ba_ref,
    bb_ref,
    bc_ref,
    hw_ref,
    sems,
):
    copies = [
        pltpu.make_async_copy(src, dst, sems.at[i])
        for i, (src, dst) in enumerate(
            (
                (wc_hbm, wc_ref),
                (ba_hbm, ba_ref),
                (bb_hbm, bb_ref),
                (bc_hbm, bc_ref),
                (hw_hbm, hw_ref),
                (home_hbm, home_ref),
                (invd_hbm, invd_ref),
            )
        )
    ]
    for copy in copies:
        copy.start()
    for copy in copies:
        copy.wait()
    for i, ref in enumerate((ba_ref, bb_ref, bc_ref, hw_ref)):
        wide_ref[i] = jnp.broadcast_to(ref[...].astype(F32), (NZ, HID)).T
    conv_lhs(wc_ref, fc, tc)


def forward_kernel(
    home_ref,
    invd_ref,
    hb_ref,
    mine_ref,
    other_ref,
    wa_ref,
    wb_ref,
    tb_ref,
    wc_ref,
    tc_ref,
    wide_ref,
    p_hbm,
    gs_out,
    sbuf,
    hbuf,
    p_out,
    sems,
    inv_ref,
    x0s,
    liq,
    scl,
    f1,
    h1,
    h2,
    h3o,
    pf,
    rs,
    *,
    n_slots,
    cells,
):
    gx = lax.axis_index("gx")
    gy = lax.axis_index("gy")
    for ref in (x0s, h1, h2):
        z = jnp.zeros(ref.shape[2:], ref.dtype)
        for X in range(PLANES):
            ref[X, 0] = z
            ref[X, NY + 1] = z
    for ref in (liq, scl, f1, pf, rs):
        for X in range(PLANES):
            ref[X] = jnp.zeros((YY, NZ), F32)
    for s in range(n_slots):
        inv_ref[home_ref[s]] = s

    def load_plane(X, c):
        xg = 2 * gx - MID + X
        ok = jnp.where((xg >= 0) & (xg < 2 * n_slots), 1.0, 0.0).astype(F32)
        xc = jnp.clip(xg, 0, 2 * n_slots - 1)
        home = xc // 2
        half = xc - 2 * home
        slot = inv_ref[home]
        row4 = lax.broadcasted_iota(jnp.int32, (4, NZ), 0)
        for i in range(NY):
            src = (mine_ref, other_ref)[i // 8]
            fb = src[slot, half, i % 8].astype(F32) * ok
            mb = src[home, half, i % 8].astype(F32)
            y = 8 * (gy if i < 8 else 1 - gy) + i % 8
            lq = mb[2:3] * ok
            cl = mb[3:4]
            sc = jnp.zeros((1, NZ), F32)
            for k in range(4):
                sc = jnp.where(cl == k, invd_ref[k], sc)
            base = jnp.where(row4 < 2, fb, jnp.where(row4 == 2, mb * ok, 0.0))
            k12 = jnp.concatenate(
                [shift_right(base), base, shift_left(base), jnp.zeros((4, NZ), F32)], axis=0
            )
            x0s[X, y + 1] = k12.astype(BF16)
            liq[X, pl.ds(y + 1, 1), :] = lq
            scl[X, pl.ds(y + 1, 1), :] = sc * lq
            f1[X, pl.ds(y + 1, 1), :] = fb[1:2]
        return c

    lax.fori_loop(0, PLANES, load_plane, 0)

    def planes(count, body):
        def step(i, c):
            body(i)
            return c

        lax.fori_loop(0, count, step, 0)

    y4 = gy * 4 + 1

    def layer1(X, slot):
        for j in range(6):
            y = y4 + 2 * j
            Y = dot_nn(wa_ref[...], taps(x0s, X, y))
            for k in range(2):
                z = Y[:, k * NZ : (k + 1) * NZ] + wide_ref[0]
                m = liq[X, pl.ds(y + k, 1), :]
                act, sig = activate(z)
                h1[X, y + k] = (act * m).astype(BF16)
                if slot is not None:
                    sbuf[S1 + 12 * slot + 2 * j + k] = slope_of(z, sig) * m

    planes(8, lambda i: layer1(1 + i + 2 * (i // 4), None))
    planes(2, lambda i: layer1(MID + i, i))

    def layer2(X, slot):
        for j in range(6):
            y = y4 + 2 * j
            Y = dot_nn(wb_ref[...], pair_taps(h1, X, y))
            for d in range(2):
                for k in range(2):
                    z = lane_taps(Y, d, k) + wide_ref[1]
                    m = liq[X + d, pl.ds(y + k, 1), :]
                    act, sig = activate(z)
                    h2[X + d, y + k] = (act * m).astype(BF16)
                    if slot is not None:
                        sbuf[S2 + 12 * (slot + d) + 2 * j + k] = slope_of(z, sig) * m

    planes(2, lambda i: layer2(2 + 6 * i, None))
    planes(2, lambda i: layer2(MID - 1 + 2 * i, 2 * i))

    y2 = gy * 6 + 1

    def layer3(i):
        X = MID - 2 + 2 * i
        for j in range(5):
            y = y2 + 2 * j
            Y = dot_nn(wc_ref[...], pair_taps(h2, X, y))
            for d in range(2):
                for k in range(2):
                    z = lane_taps(Y, d, k) + wide_ref[2]
                    m = liq[X + d, pl.ds(y + k, 1), :]
                    act, sig = activate(z)
                    h3 = (act * m).astype(BF16)
                    score = jnp.sum(wide_ref[3] * h3.astype(F32), axis=0, keepdims=True)
                    pf[X + d, pl.ds(y + k, 1), :] = m * (score + hb_ref[0])
                    sbuf[S3 + 10 * (2 * i + d) + 2 * j + k] = slope_of(z, sig) * m
                    h3o[2 * i + d, 2 * j + k] = h3

    planes(3, layer3)

    def operator(val, X):
        v = val[X, 1 : NY + 1, :]
        s = scl[X, 1 : NY + 1, :]
        q = liq[X, 1 : NY + 1, :]

        def term(nv, ns, nq):
            return 0.5 * (s * nq + ns * q) * (nv - v)

        total = term(val[X + 1, 1 : NY + 1, :], scl[X + 1, 1 : NY + 1, :], liq[X + 1, 1 : NY + 1, :])
        total += term(val[X - 1, 1 : NY + 1, :], scl[X - 1, 1 : NY + 1, :], liq[X - 1, 1 : NY + 1, :])
        total += term(val[X, 2 : NY + 2, :], scl[X, 2 : NY + 2, :], liq[X, 2 : NY + 2, :])
        total += term(val[X, 0:NY, :], scl[X, 0:NY, :], liq[X, 0:NY, :])
        total += term(shift_left(v), shift_left(s), shift_left(q))
        total += term(shift_right(v), shift_right(s), shift_right(q))
        return total

    for X in range(MID - 1, MID + 3):
        rs[X, 1 : NY + 1, :] = operator(pf, X) - liq[X, 1 : NY + 1, :] * f1[X, 1 : NY + 1, :]
    own_y = pl.ds(pl.multiple_of(gy * 8, 8) + 1, 8)
    loss = jnp.zeros((8, NZ), F32)
    for k in range(2):
        p_out[k] = pf[MID + k, own_y, :]
        r = rs[MID + k, own_y, :]
        loss += r * r
    leave = pltpu.make_async_copy(p_out, p_hbm, sems.at[0])
    leave.start()
    sbuf[LOSS, 0:8, :] = loss * (1.0 / cells)
    for X in range(MID - 1, MID + 3):
        rs[X] = rs[X] * (2.0 / cells)
    for k in range(2):
        X = MID + k
        pf[k, 1 : NY + 1, :] = liq[X, 1 : NY + 1, :] * operator(rs, X)
    for k in range(2):
        gs_out[k] = pf[k, own_y, :]

    head = jnp.zeros((HID, NZ), F32)
    for i in range(16):
        X, dy = i // 8, i % 8
        head += pf[X, pl.ds(gy * 8 + 1 + dy, 1), :] * h3o[2 + X, gy * 2 + dy].astype(F32)
    sbuf[HEAD] = head

    f0 = gy * 6

    def copy_out(i):
        for l in range(FRAME):
            r = (l % 4) * 16
            hbuf[X0 + 3 * i + l // 4, r : r + 16, :] = x0s[MID - 1 + i, f0 + l]
            hbuf[H1 + FRAME * i + l] = h1[MID - 1 + i, f0 + l]
            hbuf[H2 + FRAME * i + l] = h2[MID - 1 + i, f0 + l]

    planes(4, copy_out)
    for r in range(36):
        hbuf[WB + r] = tb_ref[r]
        hbuf[WC + r] = tc_ref[r]
    leave.wait()


def stack_gradient(raw, gcat, cols):
    g = raw.astype(F32)
    gcat[0:HID, cols] = shift_left(g).astype(BF16)
    gcat[HID : 2 * HID, cols] = raw
    gcat[2 * HID : 3 * HID, cols] = shift_right(g).astype(BF16)
    return g


def store_weights(W, ref):
    for a in range(3):
        for b in range(3):
            for e in range(3):
                t = 9 * a + 3 * b + e
                k = 3 * a + b
                blk = W[e * HID : (e + 1) * HID, k * HID : (k + 1) * HID]
                ref[t * 32 : (t + 1) * 32, 0:HID] = blk[:32]
                ref[t * 32 : (t + 1) * 32, HID:NZ] = blk[32:]


def early_kernel(score_ref, sbuf, hbuf, wide_ref, gc_ref, bias_ref, cat_ref, gcat, hcat):
    gy = lax.axis_index("gy")
    own = gy * 2 + 1
    bias = jnp.zeros((HID, NZ), F32)
    for i in range(16):
        X, dy = i // 8, i % 8
        y = own + dy
        g = score_ref[X, dy : dy + 1, :]
        raw = (g * wide_ref[3] * sbuf[S3 + 10 * (X + 2) + y - 1]).astype(BF16)
        cols = slice(i * NZ, (i + 1) * NZ)
        bias += stack_gradient(raw, gcat, cols)
        for a in range(3):
            for b in range(3):
                k = 3 * a + b
                row = FRAME * (X + a) + y + b - 1
                hcat[k * HID : (k + 1) * HID, cols] = hbuf[H2 + row]
                cat_ref[k * HID : (k + 1) * HID, cols] = hbuf[H1 + row]
                l = y + b - 1
                q = l // 4
                cat_ref[9 * HID + k * 16 : 9 * HID + (k + 1) * 16, cols] = hbuf[
                    X0 + 3 * (X + a) + q, pl.ds(pl.multiple_of((l - 4 * q) * 16, 16), 16), :
                ]
    bias_ref[...] = bias
    store_weights(dot_nt(gcat[...], hcat[...]), gc_ref)


def backward_kernel(
    gm_ref,
    gmo_ref,
    p2_ref,
    p2o_ref,
    p1_ref,
    p1o_ref,
    sbuf,
    hbuf,
    wide_ref,
    gc_ref,
    bias_ref,
    cat_ref,
    keep_ref,
    send_ref,
    gs,
    g3,
    g2,
    g1,
    gcat,
    acc,
):
    gy = lax.axis_index("gy")
    even = lax.axis_index("gx") % 2 == 0
    own_half = pl.ds(pl.multiple_of(8 * gy, 8), 8)
    far_half = pl.ds(pl.multiple_of(8 - 8 * gy, 8), 8)
    for half, gm, p1, p2 in (
        (own_half, gm_ref, p1_ref, p2_ref),
        (far_half, gmo_ref, p1o_ref, p2o_ref),
    ):
        for k in range(2):
            gs[k, half, :] = jnp.where(even, p2[k], p1[k])
            gs[2 + k, half, :] = gm[k]
            gs[4 + k, half, :] = jnp.where(even, p1[k], p2[k])

    def lhs_at(base):
        tiles = [
            jnp.concatenate([hbuf[base + 6 * t + r] for r in range(6)], axis=0) for t in range(6)
        ]
        return jnp.concatenate(tiles, axis=1)

    for ref in (g3, g2):
        z = jnp.zeros((HID, NZ), BF16)
        for X in range(ref.shape[0]):
            ref[X, 0] = z
            ref[X, FRAME - 1] = z

    def planes(count, body):
        def step(i, c):
            body(i)
            return c

        lax.fori_loop(0, count, step, 0)

    def back3(X):
        for j in range(10):
            g = gs[X, pl.ds(gy * 6 + j, 1), :]
            g3[X, j + 1] = (g * wide_ref[3] * sbuf[S3 + 10 * X + j]).astype(BF16)

    planes(6, back3)

    for X in range(2):
        for r in range(WROWS, ROWS, 8):
            acc[X, r : r + 8, :] = jnp.zeros((8, NZ), F32)
    own = gy * 2 + 1

    def back2(i):
        X = 2 * i
        for j in range(5):
            y = 1 + 2 * j
            Y = dot_nn(lhs_at(WC), pair_taps(g3, X + 1, y))
            for d in range(2):
                for k in range(2):
                    row = gy * 2 + 2 * j + k
                    g2[X + d, y + k] = (
                        lane_taps(Y, d, k) * sbuf[S2 + 12 * (X + d) + row]
                    ).astype(BF16)

    planes(2, back2)
    bias_b = jnp.zeros((HID, NZ), F32)
    for i in range(16):
        cols = slice(i * NZ, (i + 1) * NZ)
        bias_b += stack_gradient(g2[1 + i // 8, own + i % 8], gcat, cols)
    store_weights(dot_nt(gcat[...], cat_ref[0 : 9 * HID, :]), acc.at[0])

    for j in range(4):
        y = own + 2 * j
        Y = dot_nn(lhs_at(WB), pair_taps(g2, 1, y))
        for d in range(2):
            for k in range(2):
                row = gy * 4 + 2 * j + k
                g1[d, 2 * j + k] = (lane_taps(Y, d, k) * sbuf[S1 + 12 * d + row]).astype(BF16)

    bias_a = jnp.zeros((HID, NZ), F32)
    for i in range(16):
        raw = g1[i // 8, i % 8]
        bias_a += raw.astype(F32)
        gcat[0:HID, i * NZ : (i + 1) * NZ] = raw
    A = dot_nt(cat_ref[9 * HID : 9 * HID + 144, :], gcat[0:HID, :])
    for k in range(8):
        blk = A[16 * k : 16 * k + 12]
        which, spot = k // 4, k % 4
        r0 = WROWS + 12 * (spot % 2)
        c0 = HID * (spot // 2)
        acc[which, r0 : r0 + 12, c0 : c0 + HID] = blk
    acc[1, WROWS + 24 : WROWS + 32, 0:HID] = A[128:136]
    acc[1, WROWS + 24 : WROWS + 28, HID:NZ] = A[136:140]
    sums = [
        jnp.sum(v, axis=1, keepdims=True).reshape(1, HID)
        for v in (bias_a, bias_b, bias_ref[...], sbuf[HEAD])
    ]
    total = jnp.sum(jnp.sum(sbuf[LOSS, 0:8, :], axis=0, keepdims=True), axis=1, keepdims=True)
    acc[1, 0:WROWS, :] = gc_ref[...]
    keep_ref[0:ROWS] = acc[gy]
    send_ref[0:ROWS] = acc[1 - gy]
    for ref in (keep_ref, send_ref):
        ref[ROWS : ROWS + 8, :] = jnp.zeros((8, NZ), F32)
        for j in range(2):
            ref[ROWS + j : ROWS + j + 1, :] = jnp.concatenate(
                [sums[2 * j], sums[2 * j + 1]], axis=1
            )
        ref[ROWS + 2 : ROWS + 3, :] = jnp.broadcast_to(total, (1, NZ))


def unpack_half(half, mine_ref, far_ref, stage, gb_hbm, gc_hbm, sems):
    gy = lax.axis_index("gy")
    for ref, which in ((mine_ref, gy), (far_ref, 1 - gy)):
        for j in range(14):
            v = ref[32 * j : 32 * j + 32].astype(F32)
            stage[which, j, 0:32, :] = v[:, :HID]
            stage[which, j, 32:HID, :] = v[:, HID:]
    most = [
        pltpu.make_async_copy(stage.at[i, pl.ds(0, 13)], dst.at[pl.ds(14 * half, 13)], sems.at[i])
        for i, dst in enumerate((gb_hbm, gc_hbm))
    ]
    rest = [
        pltpu.make_async_copy(stage.at[i, 13], dst.at[13], sems.at[2 + i])
        for i, dst in enumerate((gb_hbm, gc_hbm))
    ]
    for copy in most:
        copy.start()

    @pl.when(half == 0)
    def _():
        for copy in rest:
            copy.start()
        for copy in rest:
            copy.wait()

    return most


def near_kernel(mine_ref, far_ref, gb_hbm, gc_hbm, extra_ref, stage, sems):
    half = lax.axis_index("gx") % 2
    most = unpack_half(half, mine_ref, far_ref, stage, gb_hbm, gc_hbm, sems)
    for i in range(2):
        extra_ref[i] = stage[i, 13]
    for copy in most:
        copy.wait()


def finish_kernel(
    mine_ref, far_ref, extra_ref, gb_in, gc_in, gb_hbm, gc_hbm, ga_hbm, stage, first, ga_ref, sems
):
    half = 1 - lax.axis_index("gx") % 2
    most = unpack_half(half, mine_ref, far_ref, stage, gb_hbm, gc_hbm, sems)
    zero, one = [jnp.where(half == 1, stage[i, 13], extra_ref[i]) for i in range(2)]
    first[0:24] = zero[0:24]
    first[24:48] = zero[32:56]
    first[48:72] = one[0:24]
    first[72:96] = one[32:56]
    first[96:104] = one[24:32]
    first[104:108] = one[56:60]
    for ch in range(3):
        ga_ref[ch] = first[pl.ds(ch, 27, stride=4), :]
    last = pltpu.make_async_copy(ga_ref, ga_hbm, sems.at[4])
    last.start()
    last.wait()
    for copy in most:
        copy.wait()


def partner(value, bit, count):
    return lax.ppermute(value, AXES, [(i, i ^ bit) for i in range(count)])


def gather_stage(value, bit, me, count):
    other = partner(value, bit, count)
    upper = (me & bit) != 0
    return jnp.where(upper, jnp.concatenate([other, value]), jnp.concatenate([value, other]))


def two_parts(v):
    high = rounded(v)
    return high, rounded(v - high)


def rounded(v):
    return lax.reduce_precision(v, 8, 7)


def sum_all(keep, send, me, count):
    total = keep + partner(send, 1, count)
    body, tail = total[:ROWS], total[ROWS:]
    half = ROWS // 2
    upper = (me & 2) != 0
    high, low = two_parts(tail)
    away = lax.dynamic_slice_in_dim(body, jnp.where(upper, 0, half), half)
    sent = jnp.concatenate([rounded(away), high, low]).astype(BF16)
    got = partner(sent, 2, count).astype(F32)
    body = lax.dynamic_slice_in_dim(body, jnp.where(upper, half, 0), half) + got[:half]
    tail = tail + got[half : half + 8] + got[half + 8 :]
    bit = 4
    while bit < count:
        high, low = two_parts(tail)
        body = rounded(body)
        sent = jnp.concatenate([body, high, low]).astype(BF16)
        got = partner(sent, bit, count).astype(F32)
        body = body + got[:half]
        tail = (high + low) + (got[half : half + 8] + got[half + 8 :])
        bit *= 2
    body = body.astype(BF16)
    beside = partner(body, 2, count)
    far = partner(body, 1, count)
    return body, far, beside, tail


def on_device(
    loaded_fields,
    brick_home,
    liquid_mask,
    density_class,
    inverse_density,
    conv_a,
    bias_a,
    conv_b,
    bias_b,
    conv_c,
    bias_c,
    head_weight,
    head_bias,
):
    n_slots = lax.axis_size("gx")
    count = n_slots * lax.axis_size("gy")
    gx = lax.axis_index("gx")
    gy = lax.axis_index("gy")
    me = gx * 2 + gy
    cells = 2 * n_slots * NY * NZ
    smem = pl.BlockSpec(memory_space=pltpu.SMEM)
    vmem = pl.BlockSpec(memory_space=pltpu.VMEM)
    params = pltpu.CompilerParams(vmem_limit_bytes=VMEM_LIMIT)

    hbm = pl.BlockSpec(memory_space=pl.ANY)

    def shaped(shape, kind):
        return jax.ShapeDtypeStruct(shape, kind)

    def off_chip(v):
        return pltpu.with_memory_space_constraint(v, pltpu.HBM)

    block = pl.pallas_call(
        payload_kernel,
        out_shape=shaped((2, 8, 4, NZ), BF16),
        in_specs=[hbm] * 3,
        out_specs=vmem,
        scratch_shapes=[
            pltpu.VMEM((2, 2, 8, NZ), BF16),
            pltpu.VMEM((2, 8, NZ), jnp.int32),
            pltpu.VMEM((2, 8, NZ), jnp.int32),
            pltpu.VMEM((2, 8, 4, NZ), F32),
            pltpu.SemaphoreType.DMA((3,)),
        ],
        compiler_params=params,
        name="payload",
    )(*map(off_chip, (loaded_fields, liquid_mask, density_class)))
    lhs = shaped((6 * HID, 12 * HID), BF16)
    turned = shaped((36, HID, NZ), BF16)
    vector = pltpu.VMEM((1, HID), F32)

    def layouts2(args):
        return pl.pallas_call(
            second_lhs_kernel,
            out_shape=(shaped((HID, 144), BF16), lhs, turned),
            in_specs=[hbm] * 2,
            out_specs=(vmem,) * 3,
            scratch_shapes=[
                pltpu.VMEM((27, HID, HID), BF16),
                pltpu.VMEM((3, 27, HID), BF16),
                pltpu.SemaphoreType.DMA((2,)),
            ],
            compiler_params=params,
            name="lhs2",
        )(*map(off_chip, args))

    def layouts3(args):
        return pl.pallas_call(
            third_lhs_kernel,
            out_shape=(
                lhs,
                turned,
                shaped((4, HID, NZ), F32),
                pltpu.SMEM((n_slots,), jnp.int32),
                pltpu.SMEM((4,), F32),
            ),
            in_specs=[hbm] * 7,
            out_specs=(vmem,) * 3 + (smem,) * 2,
            scratch_shapes=[
                pltpu.VMEM((27, HID, HID), BF16),
                vector,
                vector,
                vector,
                pltpu.VMEM((1, HID), BF16),
                pltpu.SemaphoreType.DMA((7,)),
            ],
            compiler_params=params,
            name="lhs3",
        )(*map(off_chip, args))

    jobs = [
        (layouts2, (conv_b, conv_a.transpose(2, 0, 1))),
        (
            layouts3,
            (
                conv_c,
                *(v.reshape(1, HID) for v in (bias_a, bias_b, bias_c, head_weight)),
                brick_home,
                inverse_density,
            ),
        ),
    ]
    made = []
    mine = block[None]
    bit = 2
    while bit < count:
        if bit > 2 and jobs:
            job, args = jobs.pop(0)
            mine, args = lax.optimization_barrier((mine, args))
            results = job(args)
            mine = gather_stage(mine, bit, me, count)
            mine, results = lax.optimization_barrier((mine, results))
            made += results
        else:
            mine = gather_stage(mine, bit, me, count)
        bit *= 2
    for job, args in jobs:
        made += job(args)
    across = partner(mine, 1, count)
    wide = made[5]
    home, table = [pltpu.with_memory_space_constraint(v, pltpu.SMEM) for v in made[6:]]


    pressure, score, sbuf, hbuf = pl.pallas_call(
        functools.partial(forward_kernel, n_slots=n_slots, cells=cells),
        out_shape=(
            shaped((2, 8, NZ), F32),
            shaped((2, 8, NZ), F32),
            shaped((S_BLOCKS, HID, NZ), F32),
            shaped((H_BLOCKS, HID, NZ), BF16),
        ),
        in_specs=[smem] * 3 + [vmem] * 8,
        out_specs=(hbm,) + (vmem,) * 3,
        scratch_shapes=[
            pltpu.VMEM((2, 8, NZ), F32),
            pltpu.SemaphoreType.DMA((1,)),
            pltpu.SMEM((n_slots,), jnp.int32),
            pltpu.VMEM((PLANES, YY, 16, NZ), BF16),
            pltpu.VMEM((PLANES, YY, NZ), F32),
            pltpu.VMEM((PLANES, YY, NZ), F32),
            pltpu.VMEM((PLANES, YY, NZ), F32),
            pltpu.VMEM((PLANES, YY, HID, NZ), BF16),
            pltpu.VMEM((PLANES, YY, HID, NZ), BF16),
            pltpu.VMEM((6, 10, HID, NZ), BF16),
            pltpu.VMEM((PLANES, YY, NZ), F32),
            pltpu.VMEM((PLANES, YY, NZ), F32),
        ],
        compiler_params=params,
        name="forward",
    )(
        home,
        table,
        head_bias,
        mine,
        across,
        *made[:6],
    )

    swap2 = lax.ppermute(score, "gx", [(i, ((i + 1) ^ 1) - 1) for i in range(1, n_slots - 1)])
    swap1 = lax.ppermute(score, "gx", [(i, i ^ 1) for i in range(n_slots)])
    across_score = partner(score, 1, count)
    early = pl.pallas_call(
        early_kernel,
        out_shape=(
            shaped((WROWS, NZ), F32),
            shaped((HID, NZ), F32),
            shaped((9 * HID + 144, 16 * NZ), BF16),
        ),
        in_specs=[vmem] * 4,
        out_specs=(vmem,) * 3,
        scratch_shapes=[
            pltpu.VMEM((3 * HID, 16 * NZ), BF16),
            pltpu.VMEM((9 * HID, 16 * NZ), BF16),
        ],
        compiler_params=params,
        name="early",
    )(score, sbuf, hbuf, wide)
    early, swap2, swap1 = lax.optimization_barrier((early, swap2, swap1))
    scores = [score, across_score]
    for value in (swap2, swap1):
        scores += [value, partner(value, 1, count)]

    keep, send = pl.pallas_call(
        backward_kernel,
        out_shape=(shaped((ROWS + 8, NZ), F32), shaped((ROWS + 8, NZ), F32)),
        in_specs=[vmem] * 12,
        out_specs=(vmem, vmem),
        scratch_shapes=[
            pltpu.VMEM((6, NY, NZ), F32),
            pltpu.VMEM((6, FRAME, HID, NZ), BF16),
            pltpu.VMEM((4, FRAME, HID, NZ), BF16),
            pltpu.VMEM((2, 8, HID, NZ), BF16),
            pltpu.VMEM((3 * HID, 16 * NZ), BF16),
            pltpu.VMEM((2, ROWS, NZ), F32),
        ],
        compiler_params=params,
        name="backward",
    )(
        *scores,
        sbuf,
        hbuf,
        wide,
        *early,
    )

    body, far, beside, tail = sum_all(keep, send, me, count)
    weights = shaped((27, HID, HID), F32)
    stage = pltpu.VMEM((2, 14, HID, HID), F32)
    near = pl.pallas_call(
        near_kernel,
        out_shape=(weights, weights, shaped((2, HID, HID), F32)),
        in_specs=[vmem] * 2,
        out_specs=(hbm, hbm, vmem),
        scratch_shapes=[stage, pltpu.SemaphoreType.DMA((4,))],
        compiler_params=params,
        name="near",
    )(body, far)
    near, beside = lax.optimization_barrier((near, beside))
    half_b, half_c, extra = near
    grad_b, grad_c, grad_a = pl.pallas_call(
        finish_kernel,
        out_shape=(weights, weights, shaped((3, 27, HID), F32)),
        in_specs=[vmem] * 3 + [hbm] * 2,
        out_specs=(hbm, hbm, hbm),
        scratch_shapes=[
            stage,
            pltpu.VMEM((112, HID), F32),
            pltpu.VMEM((3, 27, HID), F32),
            pltpu.SemaphoreType.DMA((5,)),
        ],
        input_output_aliases={3: 0, 4: 1},
        compiler_params=params,
        name="finish",
    )(beside, partner(beside, 1, count), extra, half_b, half_c)
    return (
        pressure,
        tail[2, :1],
        grad_a.transpose(1, 2, 0),
        tail[0, :HID],
        grad_b,
        tail[0, HID:],
        grad_c,
        tail[1, :HID],
        tail[1, HID:],
    )


def solution(mesh):
    grid = P(("grp", "gx"), "gy", None)
    part = P("grp")
    stack = P("grp", None, None)
    return jax.shard_map(
        on_device,
        mesh=mesh,
        in_specs=(P(None, ("grp", "gx"), "gy", None), part, grid, grid) + (P(),) * 9,
        out_specs=(grid, part, stack, part, stack, part, stack, part, part),
        check_vma=False,
    )
```

```python
import functools

import jax
import jax.numpy as jnp
from jax import lax
from jax.experimental import pallas as pl
from jax.experimental.pallas import tpu as pltpu
from jax.sharding import PartitionSpec as P

F32 = jnp.float32
BF16 = jnp.bfloat16
AXES = ("gx", "gy")
HID = 64
NZ = 128
NY = 16
YY = NY + 2
PLANES = 12
MID = 5
FRAME = 12
WROWS = 864
ROWS = 896
SPLIT = 4
VMEM_LIMIT = 24 * 1024 * 1024
S1, S2, S3, HEAD, LOSS, S_BLOCKS = 0, 24, 72, 132, 133, 134
H1, H2, X0, WB, WC, H_BLOCKS = 0, 48, 96, 108, 144, 180


def shift_right(v):
    lane = lax.broadcasted_iota(jnp.int32, v.shape, v.ndim - 1)
    return jnp.where(lane == 0, 0.0, pltpu.roll(v, 1, v.ndim - 1))


def shift_left(v):
    lane = lax.broadcasted_iota(jnp.int32, v.shape, v.ndim - 1)
    return jnp.where(lane == NZ - 1, 0.0, pltpu.roll(v, NZ - 1, v.ndim - 1))


def dot_nn(a, b):
    return jnp.dot(a, b, preferred_element_type=F32)


def dot_nt(a, b):
    return lax.dot_general(a, b, (((1,), (1,)), ((), ())), preferred_element_type=F32)


def taps(src, X, y):
    out = []
    for a in range(3):
        for b in range(3):
            out.append(
                jnp.concatenate([src[X + a - 1, y + b - 1], src[X + a - 1, y + b]], axis=1)
            )
    return jnp.concatenate(out, axis=0)


def pair_taps(src, X, y, n):
    out = []
    for b in range(3):
        for x in range(4):
            rows = [src[X + x - 1, y + b - 1 + k] for k in range(n)]
            out.append(jnp.concatenate(rows, axis=1) if n > 1 else rows[0])
    return jnp.concatenate(out, axis=0)


def row_groups(count):
    return [(j, min(2, count - j)) for j in range(0, count, 2)]


def lane_taps(Y, d, k):
    part = Y[d * 3 * HID : (d + 1) * 3 * HID, k * NZ : (k + 1) * NZ]
    return part[HID : 2 * HID] + shift_right(part[:HID]) + shift_left(part[2 * HID :])


def activate(z):
    sig = 0.5 * jnp.tanh(0.5 * z) + 0.5
    return z * sig, sig


def slope_of(z, sig):
    return sig * (1.0 + z * (1.0 - sig))


def payload_kernel(fields_hbm, liquid_hbm, class_hbm, out_ref, fields, liquid, classes, rows, sems):
    copies = [
        pltpu.make_async_copy(src, dst, sems.at[i])
        for i, (src, dst) in enumerate(
            ((fields_hbm, fields), (liquid_hbm, liquid), (class_hbm, classes))
        )
    ]
    for copy in copies:
        copy.start()
    for copy in copies:
        copy.wait()
    for x in range(2):
        planes = (fields[0, x], fields[1, x], liquid[x], classes[x])
        for p, plane in enumerate(planes):
            plane = plane.astype(F32)
            for y in range(8):
                rows[x, y, p : p + 1, :] = plane[y : y + 1]
    out_ref[...] = rows[...].astype(BF16)


def conv_lhs(w, fwd, bwd):
    zero = jnp.zeros((HID, HID), F32)
    for b in range(3):
        for e in range(3):
            ahead = [w[9 * a + 3 * b + e].astype(F32) for a in range(3)]
            back = [w[26 - (9 * a + 3 * b + e)].astype(F32) for a in range(3)]
            for d in range(2):
                for half in range(2):
                    low, high = 2 * half - d, 2 * half + 1 - d
                    rows = slice((3 * d + e) * HID, (3 * d + e + 1) * HID)
                    tile = 2 * b + half
                    pick = [
                        [v[a] if 0 <= a <= 2 else zero for a in (low, high)] for v in (ahead, back)
                    ]
                    fwd[rows, tile * NZ : (tile + 1) * NZ] = jnp.concatenate(
                        pick[0], axis=1
                    ).astype(BF16)
                    bwd[6 * tile + 3 * d + e] = jnp.concatenate(pick[1], axis=0).T.astype(BF16)


def second_lhs_kernel(wb_hbm, wa_hbm, fa, fb, tb, wb_ref, wa_ref, sems):
    copies = [
        pltpu.make_async_copy(src, dst, sems.at[i])
        for i, (src, dst) in enumerate(((wb_hbm, wb_ref), (wa_hbm, wa_ref)))
    ]
    for copy in copies:
        copy.start()
    for copy in copies:
        copy.wait()
    conv_lhs(wb_ref, fb, tb)
    tap = lax.broadcasted_iota(jnp.int32, (27, 144), 0)
    col = lax.broadcasted_iota(jnp.int32, (27, 144), 1)
    total = jnp.zeros((HID, 144), F32)
    for ch in range(3):
        spot = 16 * (tap // 3) + 4 * (tap - 3 * (tap // 3)) + ch
        pick = jnp.where(col == spot, 1.0, 0.0).astype(BF16)
        total += dot_nn(wa_ref[ch].astype(F32).T.astype(BF16), pick)
    fa[...] = total.astype(BF16)


def third_lhs_kernel(
    wc_hbm,
    ba_hbm,
    bb_hbm,
    bc_hbm,
    hw_hbm,
    home_hbm,
    invd_hbm,
    fc,
    tc,
    wide_ref,
    home_ref,
    invd_ref,
    wc_ref,
    ba_ref,
    bb_ref,
    bc_ref,
    hw_ref,
    sems,
):
    copies = [
        pltpu.make_async_copy(src, dst, sems.at[i])
        for i, (src, dst) in enumerate(
            (
                (wc_hbm, wc_ref),
                (ba_hbm, ba_ref),
                (bb_hbm, bb_ref),
                (bc_hbm, bc_ref),
                (hw_hbm, hw_ref),
                (home_hbm, home_ref),
                (invd_hbm, invd_ref),
            )
        )
    ]
    for copy in copies:
        copy.start()
    for copy in copies:
        copy.wait()
    for i, ref in enumerate((ba_ref, bb_ref, bc_ref, hw_ref)):
        wide_ref[i] = jnp.broadcast_to(ref[...].astype(F32), (NZ, HID)).T
    conv_lhs(wc_ref, fc, tc)


def forward_kernel(
    home_ref,
    invd_ref,
    hb_ref,
    mine_ref,
    other_ref,
    wa_ref,
    wb_ref,
    tb_ref,
    wc_ref,
    tc_ref,
    wide_ref,
    p_hbm,
    gs_out,
    sbuf,
    hbuf,
    p_out,
    sems,
    inv_ref,
    x0s,
    liq,
    scl,
    f1,
    h1,
    h2,
    h3o,
    pf,
    rs,
    *,
    n_slots,
    cells,
):
    gx = lax.axis_index("gx")
    gy = lax.axis_index("gy")
    for ref in (x0s, h1, h2):
        z = jnp.zeros(ref.shape[2:], ref.dtype)
        for X in range(PLANES):
            ref[X, 0] = z
            ref[X, NY + 1] = z
    for ref in (liq, scl, f1, pf, rs):
        for X in range(PLANES):
            ref[X] = jnp.zeros((YY, NZ), F32)
    for s in range(n_slots):
        inv_ref[home_ref[s]] = s

    def load_plane(X, c):
        xg = 2 * gx - MID + X
        ok = jnp.where((xg >= 0) & (xg < 2 * n_slots), 1.0, 0.0).astype(F32)
        xc = jnp.clip(xg, 0, 2 * n_slots - 1)
        home = xc // 2
        half = xc - 2 * home
        slot = inv_ref[home]
        row4 = lax.broadcasted_iota(jnp.int32, (4, NZ), 0)
        for i in range(NY):
            src = (mine_ref, other_ref)[i // 8]
            fb = src[slot, half, i % 8].astype(F32) * ok
            mb = src[home, half, i % 8].astype(F32)
            y = 8 * (gy if i < 8 else 1 - gy) + i % 8
            lq = mb[2:3] * ok
            base = jnp.where(row4 < 2, fb, jnp.where(row4 == 2, mb * ok, 0.0))
            k12 = jnp.concatenate(
                [shift_right(base), base, shift_left(base), jnp.zeros((4, NZ), F32)], axis=0
            )
            x0s[X, y + 1] = k12.astype(BF16)
            liq[X, pl.ds(y + 1, 1), :] = lq
            scl[X, pl.ds(y + 1, 1), :] = mb[3:4]
            f1[X, pl.ds(y + 1, 1), :] = fb[1:2]
        cl = scl[X, 1 : NY + 1, :]
        sc = jnp.zeros((NY, NZ), F32)
        for k in range(4):
            sc = jnp.where(cl == k, invd_ref[k], sc)
        scl[X, 1 : NY + 1, :] = sc * liq[X, 1 : NY + 1, :]
        return c

    lax.fori_loop(0, PLANES, load_plane, 0)

    def planes(count, body):
        def step(i, c):
            body(i)
            return c

        lax.fori_loop(0, count, step, 0)

    y4 = gy * 4 + 1

    def layer1(X, slot):
        for j in range(6):
            y = y4 + 2 * j
            Y = dot_nn(wa_ref[...], taps(x0s, X, y))
            for k in range(2):
                z = Y[:, k * NZ : (k + 1) * NZ] + wide_ref[0]
                m = liq[X, pl.ds(y + k, 1), :]
                act, sig = activate(z)
                h1[X, y + k] = (act * m).astype(BF16)
                if slot is not None:
                    sbuf[S1 + 12 * slot + 2 * j + k] = slope_of(z, sig) * m

    planes(8, lambda i: layer1(1 + i + 2 * (i // 4), None))
    planes(2, lambda i: layer1(MID + i, i))

    y3 = gy * 5 + 1

    def layer2(X, slot):
        for j, n in row_groups(11):
            y = y3 + j
            Y = dot_nn(wb_ref[...], pair_taps(h1, X, y, n))
            for d in range(2):
                for k in range(n):
                    z = lane_taps(Y, d, k) + wide_ref[1]
                    m = liq[X + d, pl.ds(y + k, 1), :]
                    act, sig = activate(z)
                    h2[X + d, y + k] = (act * m).astype(BF16)
                    if slot is not None:
                        sbuf[S2 + 12 * (slot + d) + j + k] = slope_of(z, sig) * m

    planes(2, lambda i: layer2(2 + 6 * i, None))
    planes(2, lambda i: layer2(MID - 1 + 2 * i, 2 * i))

    y2 = gy * 6 + 1

    def layer3(i):
        X = MID - 2 + 2 * i
        for j in range(5):
            y = y2 + 2 * j
            Y = dot_nn(wc_ref[...], pair_taps(h2, X, y, 2))
            for d in range(2):
                for k in range(2):
                    z = lane_taps(Y, d, k) + wide_ref[2]
                    m = liq[X + d, pl.ds(y + k, 1), :]
                    act, sig = activate(z)
                    h3 = (act * m).astype(BF16)
                    score = jnp.sum(wide_ref[3] * h3.astype(F32), axis=0, keepdims=True)
                    pf[X + d, pl.ds(y + k, 1), :] = m * (score + hb_ref[0])
                    sbuf[S3 + 10 * (2 * i + d) + 2 * j + k] = slope_of(z, sig) * m
                    h3o[2 * i + d, 2 * j + k] = h3

    planes(3, layer3)

    def operator(val, X):
        v = val[X, 1 : NY + 1, :]
        s = scl[X, 1 : NY + 1, :]
        q = liq[X, 1 : NY + 1, :]

        def term(nv, ns, nq):
            return 0.5 * (s * nq + ns * q) * (nv - v)

        total = term(val[X + 1, 1 : NY + 1, :], scl[X + 1, 1 : NY + 1, :], liq[X + 1, 1 : NY + 1, :])
        total += term(val[X - 1, 1 : NY + 1, :], scl[X - 1, 1 : NY + 1, :], liq[X - 1, 1 : NY + 1, :])
        total += term(val[X, 2 : NY + 2, :], scl[X, 2 : NY + 2, :], liq[X, 2 : NY + 2, :])
        total += term(val[X, 0:NY, :], scl[X, 0:NY, :], liq[X, 0:NY, :])
        total += term(shift_left(v), shift_left(s), shift_left(q))
        total += term(shift_right(v), shift_right(s), shift_right(q))
        return total

    for X in range(MID - 1, MID + 3):
        rs[X, 1 : NY + 1, :] = operator(pf, X) - liq[X, 1 : NY + 1, :] * f1[X, 1 : NY + 1, :]
    own_y = pl.ds(pl.multiple_of(gy * 8, 8) + 1, 8)
    loss = jnp.zeros((8, NZ), F32)
    for k in range(2):
        p_out[k] = pf[MID + k, own_y, :]
        r = rs[MID + k, own_y, :]
        loss += r * r
    leave = pltpu.make_async_copy(p_out, p_hbm, sems.at[0])
    leave.start()
    sbuf[LOSS, 0:8, :] = loss * (1.0 / cells)
    for X in range(MID - 1, MID + 3):
        rs[X] = rs[X] * (2.0 / cells)
    for k in range(2):
        X = MID + k
        pf[k, 1 : NY + 1, :] = liq[X, 1 : NY + 1, :] * operator(rs, X)
    for k in range(2):
        gs_out[k] = pf[k, own_y, :]

    head = jnp.zeros((HID, NZ), F32)
    for i in range(16):
        X, dy = i // 8, i % 8
        head += pf[X, pl.ds(gy * 8 + 1 + dy, 1), :] * h3o[2 + X, gy * 2 + dy].astype(F32)
    sbuf[HEAD] = head

    f0 = gy * 6

    def copy_out(i):
        for l in range(FRAME):
            r = (l % 4) * 16
            hbuf[X0 + 3 * i + l // 4, r : r + 16, :] = x0s[MID - 1 + i, f0 + l]
            hbuf[H1 + FRAME * i + l] = h1[MID - 1 + i, f0 + l]
            hbuf[H2 + FRAME * i + l] = h2[MID - 1 + i, f0 + l]

    planes(4, copy_out)
    for r in range(36):
        hbuf[WB + r] = tb_ref[r]
        hbuf[WC + r] = tc_ref[r]
    leave.wait()


def stack_gradient(raw, gcat, cols):
    g = raw.astype(F32)
    gcat[0:HID, cols] = shift_left(g).astype(BF16)
    gcat[HID : 2 * HID, cols] = raw
    gcat[2 * HID : 3 * HID, cols] = shift_right(g).astype(BF16)
    return g


def store_weights(W, ref):
    for a in range(3):
        for b in range(3):
            for e in range(3):
                t = 9 * a + 3 * b + e
                k = 3 * a + b
                blk = W[e * HID : (e + 1) * HID, k * HID : (k + 1) * HID]
                ref[t * 32 : (t + 1) * 32, 0:HID] = blk[:32]
                ref[t * 32 : (t + 1) * 32, HID:NZ] = blk[32:]


def channel_sums(first, second):
    rows = [jnp.sum(v, axis=1, keepdims=True).reshape(1, HID) for v in (first, second)]
    return jnp.concatenate(rows, axis=1)


def early_kernel(score_ref, sbuf, hbuf, wide_ref, gc_ref, bias_ref, cat_ref, gcat, hcat):
    gy = lax.axis_index("gy")
    own = gy * 2 + 1
    bias = jnp.zeros((HID, NZ), F32)
    for i in range(16):
        X, dy = i // 8, i % 8
        y = own + dy
        g = score_ref[X, dy : dy + 1, :]
        raw = (g * wide_ref[3] * sbuf[S3 + 10 * (X + 2) + y - 1]).astype(BF16)
        cols = slice(i * NZ, (i + 1) * NZ)
        bias += stack_gradient(raw, gcat, cols)
        for a in range(3):
            for b in range(3):
                k = 3 * a + b
                row = FRAME * (X + a) + y + b - 1
                hcat[k * HID : (k + 1) * HID, cols] = hbuf[H2 + row]
                cat_ref[k * HID : (k + 1) * HID, cols] = hbuf[H1 + row]
                l = y + b - 1
                q = l // 4
                cat_ref[9 * HID + k * 16 : 9 * HID + (k + 1) * 16, cols] = hbuf[
                    X0 + 3 * (X + a) + q, pl.ds(pl.multiple_of((l - 4 * q) * 16, 16), 16), :
                ]
    store_weights(dot_nt(gcat[...], hcat[...]), gc_ref)
    loss = jnp.sum(jnp.sum(sbuf[LOSS, 0:8, :], axis=0, keepdims=True), axis=1, keepdims=True)
    bias_ref[...] = jnp.zeros((8, NZ), F32)
    bias_ref[1:2, :] = channel_sums(bias, sbuf[HEAD])
    bias_ref[2:3, :] = jnp.broadcast_to(loss, (1, NZ))


def backward_kernel(
    gm_ref,
    gmo_ref,
    p2_ref,
    p2o_ref,
    p1_ref,
    p1o_ref,
    sbuf,
    hbuf,
    wide_ref,
    gc_ref,
    bias_ref,
    cat_ref,
    keep_ref,
    send_ref,
    gs,
    g3,
    g2,
    g1,
    gcat,
    acc,
):
    gy = lax.axis_index("gy")
    even = lax.axis_index("gx") % 2 == 0
    own_half = pl.ds(pl.multiple_of(8 * gy, 8), 8)
    far_half = pl.ds(pl.multiple_of(8 - 8 * gy, 8), 8)
    for half, gm, p1, p2 in (
        (own_half, gm_ref, p1_ref, p2_ref),
        (far_half, gmo_ref, p1o_ref, p2o_ref),
    ):
        for k in range(2):
            gs[k, half, :] = jnp.where(even, p2[k], p1[k])
            gs[2 + k, half, :] = gm[k]
            gs[4 + k, half, :] = jnp.where(even, p1[k], p2[k])

    def lhs_at(base):
        tiles = [
            jnp.concatenate([hbuf[base + 6 * t + r] for r in range(6)], axis=0) for t in range(6)
        ]
        return jnp.concatenate(tiles, axis=1)

    for ref in (g3, g2):
        z = jnp.zeros((HID, NZ), BF16)
        for X in range(ref.shape[0]):
            ref[X, 0] = z
            ref[X, FRAME - 1] = z

    def planes(count, body):
        def step(i, c):
            body(i)
            return c

        lax.fori_loop(0, count, step, 0)

    def back3(X):
        for j in range(10):
            g = gs[X, pl.ds(gy * 6 + j, 1), :]
            g3[X, j + 1] = (g * wide_ref[3] * sbuf[S3 + 10 * X + j]).astype(BF16)

    planes(6, back3)

    for X in range(2):
        for r in range(WROWS, ROWS, 8):
            acc[X, r : r + 8, :] = jnp.zeros((8, NZ), F32)
    own = gy * 2 + 1

    def back2(i):
        X = 2 * i
        for j, n in row_groups(9):
            y = 1 + gy + j
            Y = dot_nn(lhs_at(WC), pair_taps(g3, X + 1, y, n))
            for d in range(2):
                for k in range(n):
                    row = 2 * gy + j + k
                    g2[X + d, y + k] = (
                        lane_taps(Y, d, k) * sbuf[S2 + 12 * (X + d) + row]
                    ).astype(BF16)

    planes(2, back2)
    bias_b = jnp.zeros((HID, NZ), F32)
    for i in range(16):
        cols = slice(i * NZ, (i + 1) * NZ)
        bias_b += stack_gradient(g2[1 + i // 8, own + i % 8], gcat, cols)
    store_weights(dot_nt(gcat[...], cat_ref[0 : 9 * HID, :]), acc.at[0])

    for j in range(4):
        y = own + 2 * j
        Y = dot_nn(lhs_at(WB), pair_taps(g2, 1, y, 2))
        for d in range(2):
            for k in range(2):
                row = gy * 4 + 2 * j + k
                g1[d, 2 * j + k] = (lane_taps(Y, d, k) * sbuf[S1 + 12 * d + row]).astype(BF16)

    bias_a = jnp.zeros((HID, NZ), F32)
    for i in range(16):
        raw = g1[i // 8, i % 8]
        bias_a += raw.astype(F32)
        gcat[0:HID, i * NZ : (i + 1) * NZ] = raw
    A = dot_nt(cat_ref[9 * HID : 9 * HID + 144, :], gcat[0:HID, :])
    for k in range(8):
        blk = A[16 * k : 16 * k + 12]
        which, spot = k // 4, k % 4
        r0 = WROWS + 12 * (spot % 2)
        c0 = HID * (spot // 2)
        acc[which, r0 : r0 + 12, c0 : c0 + HID] = blk
    acc[1, WROWS + 24 : WROWS + 32, 0:HID] = A[128:136]
    acc[1, WROWS + 24 : WROWS + 28, HID:NZ] = A[136:140]
    acc[1, 0:WROWS, :] = gc_ref[...]
    keep_ref[0:ROWS] = acc[gy]
    send_ref[0:ROWS] = acc[1 - gy]
    sums = channel_sums(bias_a, bias_b)
    for ref in (keep_ref, send_ref):
        ref[ROWS : ROWS + 8, :] = bias_ref[...]
        ref[ROWS : ROWS + 1, :] = sums


def unpack_half(half, mine_ref, far_ref, stage, gb_hbm, gc_hbm, sems):
    gy = lax.axis_index("gy")
    for ref, which in ((mine_ref, gy), (far_ref, 1 - gy)):
        for j in range(14):
            v = ref[32 * j : 32 * j + 32].astype(F32)
            stage[which, j, 0:32, :] = v[:, :HID]
            stage[which, j, 32:HID, :] = v[:, HID:]
    most = [
        pltpu.make_async_copy(stage.at[i, pl.ds(0, 13)], dst.at[pl.ds(14 * half, 13)], sems.at[i])
        for i, dst in enumerate((gb_hbm, gc_hbm))
    ]
    rest = [
        pltpu.make_async_copy(stage.at[i, 13], dst.at[13], sems.at[2 + i])
        for i, dst in enumerate((gb_hbm, gc_hbm))
    ]
    for copy in most:
        copy.start()

    @pl.when(half == 0)
    def _():
        for copy in rest:
            copy.start()
        for copy in rest:
            copy.wait()

    return most


def near_kernel(mine_ref, far_ref, gb_hbm, gc_hbm, extra_ref, stage, sems):
    half = lax.axis_index("gx") // (SPLIT // 2) % 2
    most = unpack_half(half, mine_ref, far_ref, stage, gb_hbm, gc_hbm, sems)
    for i in range(2):
        extra_ref[i] = stage[i, 13]
    for copy in most:
        copy.wait()


def finish_kernel(
    mine_ref, far_ref, extra_ref, gb_in, gc_in, gb_hbm, gc_hbm, ga_hbm, stage, first, ga_ref, sems
):
    half = 1 - lax.axis_index("gx") // (SPLIT // 2) % 2
    most = unpack_half(half, mine_ref, far_ref, stage, gb_hbm, gc_hbm, sems)
    zero, one = [jnp.where(half == 1, stage[i, 13], extra_ref[i]) for i in range(2)]
    first[0:24] = zero[0:24]
    first[24:48] = zero[32:56]
    first[48:72] = one[0:24]
    first[72:96] = one[32:56]
    first[96:104] = one[24:32]
    first[104:108] = one[56:60]
    for ch in range(3):
        ga_ref[ch] = first[pl.ds(ch, 27, stride=4), :]
    last = pltpu.make_async_copy(ga_ref, ga_hbm, sems.at[4])
    last.start()
    last.wait()
    for copy in most:
        copy.wait()


def partner(value, bit, count):
    return lax.ppermute(value, AXES, [(i, i ^ bit) for i in range(count)])


def gather_stage(value, bit, me, count):
    other = partner(value, bit, count)
    upper = (me & bit) != 0
    return jnp.where(upper, jnp.concatenate([other, value]), jnp.concatenate([value, other]))


def two_parts(v):
    high = rounded(v)
    return high, rounded(v - high)


def rounded(v):
    return lax.reduce_precision(v, 8, 7)


def sum_all(keep, send, me, count):
    total = keep + partner(send, 1, count)
    body, tail = total[:ROWS], total[ROWS:]
    half = ROWS // 2
    upper = (me & SPLIT) != 0
    high, low = two_parts(tail)
    away = lax.dynamic_slice_in_dim(body, jnp.where(upper, 0, half), half)
    sent = jnp.concatenate([rounded(away), high, low]).astype(BF16)
    got = partner(sent, SPLIT, count).astype(F32)
    body = lax.dynamic_slice_in_dim(body, jnp.where(upper, half, 0), half) + got[:half]
    tail = tail + got[half : half + 8] + got[half + 8 :]
    bit = 2
    while bit < count:
        if bit != SPLIT:
            high, low = two_parts(tail)
            body = rounded(body)
            sent = jnp.concatenate([body, high, low]).astype(BF16)
            got = partner(sent, bit, count).astype(F32)
            body = body + got[:half]
            tail = (high + low) + (got[half : half + 8] + got[half + 8 :])
        bit *= 2
    body = body.astype(BF16)
    beside = partner(body, SPLIT, count)
    far = partner(body, 1, count)
    return body, far, beside, tail


def on_device(
    loaded_fields,
    brick_home,
    liquid_mask,
    density_class,
    inverse_density,
    conv_a,
    bias_a,
    conv_b,
    bias_b,
    conv_c,
    bias_c,
    head_weight,
    head_bias,
):
    n_slots = lax.axis_size("gx")
    count = n_slots * lax.axis_size("gy")
    gx = lax.axis_index("gx")
    gy = lax.axis_index("gy")
    me = gx * 2 + gy
    cells = 2 * n_slots * NY * NZ
    smem = pl.BlockSpec(memory_space=pltpu.SMEM)
    vmem = pl.BlockSpec(memory_space=pltpu.VMEM)
    params = pltpu.CompilerParams(vmem_limit_bytes=VMEM_LIMIT)

    hbm = pl.BlockSpec(memory_space=pl.ANY)

    def shaped(shape, kind):
        return jax.ShapeDtypeStruct(shape, kind)

    def off_chip(v):
        return pltpu.with_memory_space_constraint(v, pltpu.HBM)

    block = pl.pallas_call(
        payload_kernel,
        out_shape=shaped((2, 8, 4, NZ), BF16),
        in_specs=[hbm] * 3,
        out_specs=vmem,
        scratch_shapes=[
            pltpu.VMEM((2, 2, 8, NZ), BF16),
            pltpu.VMEM((2, 8, NZ), jnp.int32),
            pltpu.VMEM((2, 8, NZ), jnp.int32),
            pltpu.VMEM((2, 8, 4, NZ), F32),
            pltpu.SemaphoreType.DMA((3,)),
        ],
        compiler_params=params,
        name="payload",
    )(*map(off_chip, (loaded_fields, liquid_mask, density_class)))
    lhs = shaped((6 * HID, 12 * HID), BF16)
    turned = shaped((36, HID, NZ), BF16)
    vector = pltpu.VMEM((1, HID), F32)

    def layouts2(args):
        return pl.pallas_call(
            second_lhs_kernel,
            out_shape=(shaped((HID, 144), BF16), lhs, turned),
            in_specs=[hbm] * 2,
            out_specs=(vmem,) * 3,
            scratch_shapes=[
                pltpu.VMEM((27, HID, HID), BF16),
                pltpu.VMEM((3, 27, HID), BF16),
                pltpu.SemaphoreType.DMA((2,)),
            ],
            compiler_params=params,
            name="lhs2",
        )(*map(off_chip, args))

    def layouts3(args):
        return pl.pallas_call(
            third_lhs_kernel,
            out_shape=(
                lhs,
                turned,
                shaped((4, HID, NZ), F32),
                pltpu.SMEM((n_slots,), jnp.int32),
                pltpu.SMEM((4,), F32),
            ),
            in_specs=[hbm] * 7,
            out_specs=(vmem,) * 3 + (smem,) * 2,
            scratch_shapes=[
                pltpu.VMEM((27, HID, HID), BF16),
                vector,
                vector,
                vector,
                pltpu.VMEM((1, HID), BF16),
                pltpu.SemaphoreType.DMA((7,)),
            ],
            compiler_params=params,
            name="lhs3",
        )(*map(off_chip, args))

    jobs = [
        (layouts2, (conv_b, conv_a.transpose(2, 0, 1))),
        (
            layouts3,
            (
                conv_c,
                *(v.reshape(1, HID) for v in (bias_a, bias_b, bias_c, head_weight)),
                brick_home,
                inverse_density,
            ),
        ),
    ]
    made = []
    mine = block[None]
    bit = 2
    while bit < count:
        if bit > 2 and jobs:
            job, args = jobs.pop(0)
            mine, args = lax.optimization_barrier((mine, args))
            results = job(args)
            mine = gather_stage(mine, bit, me, count)
            mine, results = lax.optimization_barrier((mine, results))
            made += results
        else:
            mine = gather_stage(mine, bit, me, count)
        bit *= 2
    for job, args in jobs:
        made += job(args)
    across = partner(mine, 1, count)
    wide = made[5]
    home, table = [pltpu.with_memory_space_constraint(v, pltpu.SMEM) for v in made[6:]]


    pressure, score, sbuf, hbuf = pl.pallas_call(
        functools.partial(forward_kernel, n_slots=n_slots, cells=cells),
        out_shape=(
            shaped((2, 8, NZ), F32),
            shaped((2, 8, NZ), F32),
            shaped((S_BLOCKS, HID, NZ), F32),
            shaped((H_BLOCKS, HID, NZ), BF16),
        ),
        in_specs=[smem] * 3 + [vmem] * 8,
        out_specs=(hbm,) + (vmem,) * 3,
        scratch_shapes=[
            pltpu.VMEM((2, 8, NZ), F32),
            pltpu.SemaphoreType.DMA((1,)),
            pltpu.SMEM((n_slots,), jnp.int32),
            pltpu.VMEM((PLANES, YY, 16, NZ), BF16),
            pltpu.VMEM((PLANES, YY, NZ), F32),
            pltpu.VMEM((PLANES, YY, NZ), F32),
            pltpu.VMEM((PLANES, YY, NZ), F32),
            pltpu.VMEM((PLANES, YY, HID, NZ), BF16),
            pltpu.VMEM((PLANES, YY, HID, NZ), BF16),
            pltpu.VMEM((6, 10, HID, NZ), BF16),
            pltpu.VMEM((PLANES, YY, NZ), F32),
            pltpu.VMEM((PLANES, YY, NZ), F32),
        ],
        compiler_params=params,
        name="forward",
    )(
        home,
        table,
        head_bias,
        mine,
        across,
        *made[:6],
    )

    swap2 = lax.ppermute(score, "gx", [(i, ((i + 1) ^ 1) - 1) for i in range(1, n_slots - 1)])
    swap1 = lax.ppermute(score, "gx", [(i, i ^ 1) for i in range(n_slots)])
    across_score = partner(score, 1, count)
    early = pl.pallas_call(
        early_kernel,
        out_shape=(
            shaped((WROWS, NZ), F32),
            shaped((8, NZ), F32),
            shaped((9 * HID + 144, 16 * NZ), BF16),
        ),
        in_specs=[vmem] * 4,
        out_specs=(vmem,) * 3,
        scratch_shapes=[
            pltpu.VMEM((3 * HID, 16 * NZ), BF16),
            pltpu.VMEM((9 * HID, 16 * NZ), BF16),
        ],
        compiler_params=params,
        name="early",
    )(score, sbuf, hbuf, wide)
    early, swap2, swap1 = lax.optimization_barrier((early, swap2, swap1))
    scores = [score, across_score]
    for value in (swap2, swap1):
        scores += [value, partner(value, 1, count)]

    keep, send = pl.pallas_call(
        backward_kernel,
        out_shape=(shaped((ROWS + 8, NZ), F32), shaped((ROWS + 8, NZ), F32)),
        in_specs=[vmem] * 12,
        out_specs=(vmem, vmem),
        scratch_shapes=[
            pltpu.VMEM((6, NY, NZ), F32),
            pltpu.VMEM((6, FRAME, HID, NZ), BF16),
            pltpu.VMEM((4, FRAME, HID, NZ), BF16),
            pltpu.VMEM((2, 8, HID, NZ), BF16),
            pltpu.VMEM((3 * HID, 16 * NZ), BF16),
            pltpu.VMEM((2, ROWS, NZ), F32),
        ],
        compiler_params=params,
        name="backward",
    )(
        *scores,
        sbuf,
        hbuf,
        wide,
        *early,
    )

    body, far, beside, tail = sum_all(keep, send, me, count)
    weights = shaped((27, HID, HID), F32)
    stage = pltpu.VMEM((2, 14, HID, HID), F32)
    near = pl.pallas_call(
        near_kernel,
        out_shape=(weights, weights, shaped((2, HID, HID), F32)),
        in_specs=[vmem] * 2,
        out_specs=(hbm, hbm, vmem),
        scratch_shapes=[stage, pltpu.SemaphoreType.DMA((4,))],
        compiler_params=params,
        name="near",
    )(body, far)
    near, beside = lax.optimization_barrier((near, beside))
    half_b, half_c, extra = near
    grad_b, grad_c, grad_a = pl.pallas_call(
        finish_kernel,
        out_shape=(weights, weights, shaped((3, 27, HID), F32)),
        in_specs=[vmem] * 3 + [hbm] * 2,
        out_specs=(hbm, hbm, hbm),
        scratch_shapes=[
            stage,
            pltpu.VMEM((112, HID), F32),
            pltpu.VMEM((3, 27, HID), F32),
            pltpu.SemaphoreType.DMA((5,)),
        ],
        input_output_aliases={3: 0, 4: 1},
        compiler_params=params,
        name="finish",
    )(beside, partner(beside, 1, count), extra, half_b, half_c)
    return (
        pressure,
        tail[2, :1],
        grad_a.transpose(1, 2, 0),
        tail[0, :HID],
        grad_b,
        tail[0, HID:],
        grad_c,
        tail[1, :HID],
        tail[1, HID:],
    )


def solution(mesh):
    grid = P(("grp", "gx"), "gy", None)
    part = P("grp")
    stack = P("grp", None, None)
    return jax.shard_map(
        on_device,
        mesh=mesh,
        in_specs=(P(None, ("grp", "gx"), "gy", None), part, grid, grid) + (P(),) * 9,
        out_specs=(grid, part, stack, part, stack, part, stack, part, part),
        check_vma=False,
    )
```

```python
import functools

import jax
import jax.numpy as jnp
from jax import lax
from jax.experimental import pallas as pl
from jax.experimental.pallas import tpu as pltpu
from jax.sharding import PartitionSpec as P

F32 = jnp.float32
BF16 = jnp.bfloat16
AXES = ("gx", "gy")
HID = 64
NZ = 128
NY = 16
YY = NY + 2
PLANES = 12
MID = 5
FRAME = 12
WROWS = 864
ROWS = 896
SPLIT = 4
VMEM_LIMIT = 24 * 1024 * 1024
S1, S2, S3, HEAD, LOSS, S_BLOCKS = 0, 24, 72, 132, 133, 134
H1, H2, X0, WB, WC, H_BLOCKS = 0, 48, 96, 108, 144, 180


def shift_right(v):
    lane = lax.broadcasted_iota(jnp.int32, v.shape, v.ndim - 1)
    return jnp.where(lane == 0, 0.0, pltpu.roll(v, 1, v.ndim - 1))


def shift_left(v):
    lane = lax.broadcasted_iota(jnp.int32, v.shape, v.ndim - 1)
    return jnp.where(lane == NZ - 1, 0.0, pltpu.roll(v, NZ - 1, v.ndim - 1))


def dot_nn(a, b):
    return jnp.dot(a, b, preferred_element_type=F32)


def dot_nt(a, b):
    return lax.dot_general(a, b, (((1,), (1,)), ((), ())), preferred_element_type=F32)


def taps(src, X, y):
    out = []
    for a in range(3):
        for b in range(3):
            out.append(
                jnp.concatenate([src[X + a - 1, y + b - 1], src[X + a - 1, y + b]], axis=1)
            )
    return jnp.concatenate(out, axis=0)


def pair_taps(src, X, y, n):
    out = []
    for b in range(3):
        for x in range(4):
            rows = [src[X + x - 1, y + b - 1 + k] for k in range(n)]
            out.append(jnp.concatenate(rows, axis=1) if n > 1 else rows[0])
    return jnp.concatenate(out, axis=0)


def row_groups(count):
    return [(j, min(2, count - j)) for j in range(0, count, 2)]


def lane_taps(Y, d, k):
    part = Y[d * 3 * HID : (d + 1) * 3 * HID, k * NZ : (k + 1) * NZ]
    return part[HID : 2 * HID] + shift_right(part[:HID]) + shift_left(part[2 * HID :])


def activate(z):
    sig = 0.5 * jnp.tanh(0.5 * z) + 0.5
    return z * sig, sig


def slope_of(z, sig):
    return sig * (1.0 + z * (1.0 - sig))


def payload_kernel(fields_hbm, liquid_hbm, class_hbm, out_ref, fields, liquid, classes, rows, sems):
    copies = [
        pltpu.make_async_copy(src, dst, sems.at[i])
        for i, (src, dst) in enumerate(
            ((fields_hbm, fields), (liquid_hbm, liquid), (class_hbm, classes))
        )
    ]
    for copy in copies:
        copy.start()
    for copy in copies:
        copy.wait()
    for x in range(2):
        planes = (fields[0, x], fields[1, x], liquid[x], classes[x])
        for p, plane in enumerate(planes):
            plane = plane.astype(F32)
            for y in range(8):
                rows[x, y, p : p + 1, :] = plane[y : y + 1]
    out_ref[...] = rows[...].astype(BF16)


def conv_lhs(w, fwd, bwd):
    zero = jnp.zeros((HID, HID), F32)
    for b in range(3):
        for e in range(3):
            ahead = [w[9 * a + 3 * b + e].astype(F32) for a in range(3)]
            back = [w[26 - (9 * a + 3 * b + e)].astype(F32) for a in range(3)]
            for d in range(2):
                for half in range(2):
                    low, high = 2 * half - d, 2 * half + 1 - d
                    rows = slice((3 * d + e) * HID, (3 * d + e + 1) * HID)
                    tile = 2 * b + half
                    pick = [
                        [v[a] if 0 <= a <= 2 else zero for a in (low, high)] for v in (ahead, back)
                    ]
                    fwd[rows, tile * NZ : (tile + 1) * NZ] = jnp.concatenate(
                        pick[0], axis=1
                    ).astype(BF16)
                    bwd[6 * tile + 3 * d + e] = jnp.concatenate(pick[1], axis=0).T.astype(BF16)


def second_lhs_kernel(wb_hbm, wa_hbm, fa, fb, tb, wb_ref, wa_ref, sems):
    copies = [
        pltpu.make_async_copy(src, dst, sems.at[i])
        for i, (src, dst) in enumerate(((wb_hbm, wb_ref), (wa_hbm, wa_ref)))
    ]
    for copy in copies:
        copy.start()
    for copy in copies:
        copy.wait()
    conv_lhs(wb_ref, fb, tb)
    tap = lax.broadcasted_iota(jnp.int32, (27, 144), 0)
    col = lax.broadcasted_iota(jnp.int32, (27, 144), 1)
    total = jnp.zeros((HID, 144), F32)
    for ch in range(3):
        spot = 16 * (tap // 3) + 4 * (tap - 3 * (tap // 3)) + ch
        pick = jnp.where(col == spot, 1.0, 0.0).astype(BF16)
        total += dot_nn(wa_ref[ch].astype(F32).T.astype(BF16), pick)
    fa[...] = total.astype(BF16)


def third_lhs_kernel(
    wc_hbm,
    ba_hbm,
    bb_hbm,
    bc_hbm,
    hw_hbm,
    home_hbm,
    invd_hbm,
    fc,
    tc,
    wide_ref,
    home_ref,
    invd_ref,
    wc_ref,
    ba_ref,
    bb_ref,
    bc_ref,
    hw_ref,
    sems,
):
    copies = [
        pltpu.make_async_copy(src, dst, sems.at[i])
        for i, (src, dst) in enumerate(
            (
                (wc_hbm, wc_ref),
                (ba_hbm, ba_ref),
                (bb_hbm, bb_ref),
                (bc_hbm, bc_ref),
                (hw_hbm, hw_ref),
                (home_hbm, home_ref),
                (invd_hbm, invd_ref),
            )
        )
    ]
    for copy in copies:
        copy.start()
    for copy in copies:
        copy.wait()
    for i, ref in enumerate((ba_ref, bb_ref, bc_ref, hw_ref)):
        wide_ref[i] = jnp.broadcast_to(ref[...].astype(F32), (NZ, HID)).T
    conv_lhs(wc_ref, fc, tc)


def zero_rims(*refs):
    for ref in refs:
        z = jnp.zeros(ref.shape[2:], ref.dtype)
        for X in range(PLANES):
            ref[X, 0] = z
            ref[X, NY + 1] = z


def load_half(src, y_first, home_ref, inv_ref, x0s, liq, scl, f1, n_slots):
    gx = lax.axis_index("gx")
    for s in range(n_slots):
        inv_ref[home_ref[s]] = s

    def load_plane(X, c):
        xg = 2 * gx - MID + X
        ok = jnp.where((xg >= 0) & (xg < 2 * n_slots), 1.0, 0.0).astype(F32)
        xc = jnp.clip(xg, 0, 2 * n_slots - 1)
        home = xc // 2
        half = xc - 2 * home
        slot = inv_ref[home]
        row4 = lax.broadcasted_iota(jnp.int32, (4, NZ), 0)
        for i in range(8):
            fb = src[slot, half, i].astype(F32) * ok
            mb = src[home, half, i].astype(F32)
            lq = mb[2:3] * ok
            y = y_first + i
            base = jnp.where(row4 < 2, fb, jnp.where(row4 == 2, mb * ok, 0.0))
            k12 = jnp.concatenate(
                [shift_right(base), base, shift_left(base), jnp.zeros((4, NZ), F32)], axis=0
            )
            x0s[X, y + 1] = k12.astype(BF16)
            liq[X, pl.ds(y + 1, 1), :] = lq
            scl[X, pl.ds(y + 1, 1), :] = mb[3:4]
            f1[X, pl.ds(y + 1, 1), :] = fb[1:2]
        return c

    lax.fori_loop(0, PLANES, load_plane, 0)


def prepare_kernel(home_ref, mine_ref, x0s, liq, scl, f1, inv_ref, *, n_slots):
    zero_rims(x0s)
    for ref in (liq, scl, f1):
        for X in range(PLANES):
            ref[X] = jnp.zeros((YY, NZ), F32)
    own = 8 * lax.axis_index("gy")
    load_half(mine_ref, own, home_ref, inv_ref, x0s, liq, scl, f1, n_slots)


def forward_kernel(
    home_ref,
    invd_ref,
    hb_ref,
    other_ref,
    x0s_in,
    liq_in,
    scl_in,
    f1_in,
    wa_ref,
    wb_ref,
    tb_ref,
    wc_ref,
    tc_ref,
    wide_ref,
    p_hbm,
    gs_out,
    sbuf,
    hbuf,
    p_out,
    sems,
    inv_ref,
    x0s,
    liq,
    scl,
    f1,
    h1,
    h2,
    h3o,
    pf,
    rs,
    *,
    n_slots,
    cells,
):
    gx = lax.axis_index("gx")
    gy = lax.axis_index("gy")
    zero_rims(h1, h2)
    for ref in (pf, rs):
        for X in range(PLANES):
            ref[X] = jnp.zeros((YY, NZ), F32)

    for src, dst in ((x0s_in, x0s), (liq_in, liq), (scl_in, scl), (f1_in, f1)):
        for X in range(PLANES):
            dst[X] = src[X]
    load_half(other_ref, 8 - 8 * gy, home_ref, inv_ref, x0s, liq, scl, f1, n_slots)
    for X in range(PLANES):
        cl = scl[X, 1 : NY + 1, :]
        sc = jnp.zeros((NY, NZ), F32)
        for k in range(4):
            sc = jnp.where(cl == k, invd_ref[k], sc)
        scl[X, 1 : NY + 1, :] = sc * liq[X, 1 : NY + 1, :]

    def planes(count, body):
        def step(i, c):
            body(i)
            return c

        lax.fori_loop(0, count, step, 0)

    y4 = gy * 4 + 1

    def layer1(X, slot):
        for j in range(6):
            y = y4 + 2 * j
            Y = dot_nn(wa_ref[...], taps(x0s, X, y))
            for k in range(2):
                z = Y[:, k * NZ : (k + 1) * NZ] + wide_ref[0]
                m = liq[X, pl.ds(y + k, 1), :]
                act, sig = activate(z)
                h1[X, y + k] = (act * m).astype(BF16)
                if slot is not None:
                    sbuf[S1 + 12 * slot + 2 * j + k] = slope_of(z, sig) * m

    planes(8, lambda i: layer1(1 + i + 2 * (i // 4), None))
    planes(2, lambda i: layer1(MID + i, i))

    y3 = gy * 5 + 1

    def layer2(X, slot):
        for j, n in row_groups(11):
            y = y3 + j
            Y = dot_nn(wb_ref[...], pair_taps(h1, X, y, n))
            for d in range(2):
                for k in range(n):
                    z = lane_taps(Y, d, k) + wide_ref[1]
                    m = liq[X + d, pl.ds(y + k, 1), :]
                    act, sig = activate(z)
                    h2[X + d, y + k] = (act * m).astype(BF16)
                    if slot is not None:
                        sbuf[S2 + 12 * (slot + d) + j + k] = slope_of(z, sig) * m

    planes(2, lambda i: layer2(2 + 6 * i, None))
    planes(2, lambda i: layer2(MID - 1 + 2 * i, 2 * i))

    y2 = gy * 6 + 1

    def layer3(i):
        X = MID - 2 + 2 * i
        for j in range(5):
            y = y2 + 2 * j
            Y = dot_nn(wc_ref[...], pair_taps(h2, X, y, 2))
            for d in range(2):
                for k in range(2):
                    z = lane_taps(Y, d, k) + wide_ref[2]
                    m = liq[X + d, pl.ds(y + k, 1), :]
                    act, sig = activate(z)
                    h3 = (act * m).astype(BF16)
                    score = jnp.sum(wide_ref[3] * h3.astype(F32), axis=0, keepdims=True)
                    pf[X + d, pl.ds(y + k, 1), :] = m * (score + hb_ref[0])
                    sbuf[S3 + 10 * (2 * i + d) + 2 * j + k] = slope_of(z, sig) * m
                    h3o[2 * i + d, 2 * j + k] = h3

    planes(3, layer3)

    def operator(val, X):
        v = val[X, 1 : NY + 1, :]
        s = scl[X, 1 : NY + 1, :]
        q = liq[X, 1 : NY + 1, :]

        def term(nv, ns, nq):
            return 0.5 * (s * nq + ns * q) * (nv - v)

        total = term(val[X + 1, 1 : NY + 1, :], scl[X + 1, 1 : NY + 1, :], liq[X + 1, 1 : NY + 1, :])
        total += term(val[X - 1, 1 : NY + 1, :], scl[X - 1, 1 : NY + 1, :], liq[X - 1, 1 : NY + 1, :])
        total += term(val[X, 2 : NY + 2, :], scl[X, 2 : NY + 2, :], liq[X, 2 : NY + 2, :])
        total += term(val[X, 0:NY, :], scl[X, 0:NY, :], liq[X, 0:NY, :])
        total += term(shift_left(v), shift_left(s), shift_left(q))
        total += term(shift_right(v), shift_right(s), shift_right(q))
        return total

    for X in range(MID - 1, MID + 3):
        rs[X, 1 : NY + 1, :] = operator(pf, X) - liq[X, 1 : NY + 1, :] * f1[X, 1 : NY + 1, :]
    own_y = pl.ds(pl.multiple_of(gy * 8, 8) + 1, 8)
    loss = jnp.zeros((8, NZ), F32)
    for k in range(2):
        p_out[k] = pf[MID + k, own_y, :]
        r = rs[MID + k, own_y, :]
        loss += r * r
    leave = pltpu.make_async_copy(p_out, p_hbm, sems.at[0])
    leave.start()
    sbuf[LOSS, 0:8, :] = loss * (1.0 / cells)
    for X in range(MID - 1, MID + 3):
        rs[X] = rs[X] * (2.0 / cells)
    for k in range(2):
        X = MID + k
        pf[k, 1 : NY + 1, :] = liq[X, 1 : NY + 1, :] * operator(rs, X)
    for k in range(2):
        gs_out[k] = pf[k, own_y, :]

    head = jnp.zeros((HID, NZ), F32)
    for i in range(16):
        X, dy = i // 8, i % 8
        head += pf[X, pl.ds(gy * 8 + 1 + dy, 1), :] * h3o[2 + X, gy * 2 + dy].astype(F32)
    sbuf[HEAD] = head

    f0 = gy * 6

    def copy_out(i):
        for l in range(FRAME):
            r = (l % 4) * 16
            hbuf[X0 + 3 * i + l // 4, r : r + 16, :] = x0s[MID - 1 + i, f0 + l]
            hbuf[H1 + FRAME * i + l] = h1[MID - 1 + i, f0 + l]
            hbuf[H2 + FRAME * i + l] = h2[MID - 1 + i, f0 + l]

    planes(4, copy_out)
    for r in range(36):
        hbuf[WB + r] = tb_ref[r]
        hbuf[WC + r] = tc_ref[r]
    leave.wait()


def stack_gradient(raw, gcat, cols):
    g = raw.astype(F32)
    gcat[0:HID, cols] = shift_left(g).astype(BF16)
    gcat[HID : 2 * HID, cols] = raw
    gcat[2 * HID : 3 * HID, cols] = shift_right(g).astype(BF16)
    return g


def store_weights(W, ref):
    for a in range(3):
        for b in range(3):
            for e in range(3):
                t = 9 * a + 3 * b + e
                k = 3 * a + b
                blk = W[e * HID : (e + 1) * HID, k * HID : (k + 1) * HID]
                ref[t * 32 : (t + 1) * 32, 0:HID] = blk[:32]
                ref[t * 32 : (t + 1) * 32, HID:NZ] = blk[32:]


def channel_sums(first, second):
    rows = [jnp.sum(v, axis=1, keepdims=True).reshape(1, HID) for v in (first, second)]
    return jnp.concatenate(rows, axis=1)


def early_kernel(score_ref, sbuf, hbuf, wide_ref, gc_ref, bias_ref, cat_ref, gcat, hcat):
    gy = lax.axis_index("gy")
    own = gy * 2 + 1
    bias = jnp.zeros((HID, NZ), F32)
    for i in range(16):
        X, dy = i // 8, i % 8
        y = own + dy
        g = score_ref[X, dy : dy + 1, :]
        raw = (g * wide_ref[3] * sbuf[S3 + 10 * (X + 2) + y - 1]).astype(BF16)
        cols = slice(i * NZ, (i + 1) * NZ)
        bias += stack_gradient(raw, gcat, cols)
        for a in range(3):
            for b in range(3):
                k = 3 * a + b
                row = FRAME * (X + a) + y + b - 1
                hcat[k * HID : (k + 1) * HID, cols] = hbuf[H2 + row]
                cat_ref[k * HID : (k + 1) * HID, cols] = hbuf[H1 + row]
                l = y + b - 1
                q = l // 4
                cat_ref[9 * HID + k * 16 : 9 * HID + (k + 1) * 16, cols] = hbuf[
                    X0 + 3 * (X + a) + q, pl.ds(pl.multiple_of((l - 4 * q) * 16, 16), 16), :
                ]
    store_weights(dot_nt(gcat[...], hcat[...]), gc_ref)
    loss = jnp.sum(jnp.sum(sbuf[LOSS, 0:8, :], axis=0, keepdims=True), axis=1, keepdims=True)
    bias_ref[...] = jnp.zeros((8, NZ), F32)
    bias_ref[1:2, :] = channel_sums(bias, sbuf[HEAD])
    bias_ref[2:3, :] = jnp.broadcast_to(loss, (1, NZ))


def backward_kernel(
    gm_ref,
    gmo_ref,
    p2_ref,
    p2o_ref,
    p1_ref,
    p1o_ref,
    sbuf,
    hbuf,
    wide_ref,
    gc_ref,
    bias_ref,
    cat_ref,
    keep_ref,
    send_ref,
    gs,
    g3,
    g2,
    g1,
    gcat,
    acc,
):
    gy = lax.axis_index("gy")
    even = lax.axis_index("gx") % 2 == 0
    own_half = pl.ds(pl.multiple_of(8 * gy, 8), 8)
    far_half = pl.ds(pl.multiple_of(8 - 8 * gy, 8), 8)
    for half, gm, p1, p2 in (
        (own_half, gm_ref, p1_ref, p2_ref),
        (far_half, gmo_ref, p1o_ref, p2o_ref),
    ):
        for k in range(2):
            gs[k, half, :] = jnp.where(even, p2[k], p1[k])
            gs[2 + k, half, :] = gm[k]
            gs[4 + k, half, :] = jnp.where(even, p1[k], p2[k])

    def lhs_at(base):
        tiles = [
            jnp.concatenate([hbuf[base + 6 * t + r] for r in range(6)], axis=0) for t in range(6)
        ]
        return jnp.concatenate(tiles, axis=1)

    for ref in (g3, g2):
        z = jnp.zeros((HID, NZ), BF16)
        for X in range(ref.shape[0]):
            ref[X, 0] = z
            ref[X, FRAME - 1] = z

    def planes(count, body):
        def step(i, c):
            body(i)
            return c

        lax.fori_loop(0, count, step, 0)

    def back3(X):
        for j in range(10):
            g = gs[X, pl.ds(gy * 6 + j, 1), :]
            g3[X, j + 1] = (g * wide_ref[3] * sbuf[S3 + 10 * X + j]).astype(BF16)

    planes(6, back3)

    for X in range(2):
        for r in range(WROWS, ROWS, 8):
            acc[X, r : r + 8, :] = jnp.zeros((8, NZ), F32)
    own = gy * 2 + 1

    def back2(i):
        X = 2 * i
        for j, n in row_groups(9):
            y = 1 + gy + j
            Y = dot_nn(lhs_at(WC), pair_taps(g3, X + 1, y, n))
            for d in range(2):
                for k in range(n):
                    row = 2 * gy + j + k
                    g2[X + d, y + k] = (
                        lane_taps(Y, d, k) * sbuf[S2 + 12 * (X + d) + row]
                    ).astype(BF16)

    planes(2, back2)
    bias_b = jnp.zeros((HID, NZ), F32)
    for i in range(16):
        cols = slice(i * NZ, (i + 1) * NZ)
        bias_b += stack_gradient(g2[1 + i // 8, own + i % 8], gcat, cols)
    store_weights(dot_nt(gcat[...], cat_ref[0 : 9 * HID, :]), acc.at[0])

    for j in range(4):
        y = own + 2 * j
        Y = dot_nn(lhs_at(WB), pair_taps(g2, 1, y, 2))
        for d in range(2):
            for k in range(2):
                row = gy * 4 + 2 * j + k
                g1[d, 2 * j + k] = (lane_taps(Y, d, k) * sbuf[S1 + 12 * d + row]).astype(BF16)

    bias_a = jnp.zeros((HID, NZ), F32)
    for i in range(16):
        raw = g1[i // 8, i % 8]
        bias_a += raw.astype(F32)
        gcat[0:HID, i * NZ : (i + 1) * NZ] = raw
    A = dot_nt(cat_ref[9 * HID : 9 * HID + 144, :], gcat[0:HID, :])
    for k in range(8):
        blk = A[16 * k : 16 * k + 12]
        which, spot = k // 4, k % 4
        r0 = WROWS + 12 * (spot % 2)
        c0 = HID * (spot // 2)
        acc[which, r0 : r0 + 12, c0 : c0 + HID] = blk
    acc[1, WROWS + 24 : WROWS + 32, 0:HID] = A[128:136]
    acc[1, WROWS + 24 : WROWS + 28, HID:NZ] = A[136:140]
    acc[1, 0:WROWS, :] = gc_ref[...]
    keep_ref[0:ROWS] = acc[gy]
    send_ref[0:ROWS] = acc[1 - gy]
    sums = channel_sums(bias_a, bias_b)
    for ref in (keep_ref, send_ref):
        ref[ROWS : ROWS + 8, :] = bias_ref[...]
        ref[ROWS : ROWS + 1, :] = sums


def unpack_half(half, mine_ref, far_ref, stage, gb_hbm, gc_hbm, sems):
    gy = lax.axis_index("gy")
    for ref, which in ((mine_ref, gy), (far_ref, 1 - gy)):
        for j in range(14):
            v = ref[32 * j : 32 * j + 32].astype(F32)
            stage[which, j, 0:32, :] = v[:, :HID]
            stage[which, j, 32:HID, :] = v[:, HID:]
    most = [
        pltpu.make_async_copy(stage.at[i, pl.ds(0, 13)], dst.at[pl.ds(14 * half, 13)], sems.at[i])
        for i, dst in enumerate((gb_hbm, gc_hbm))
    ]
    rest = [
        pltpu.make_async_copy(stage.at[i, 13], dst.at[13], sems.at[2 + i])
        for i, dst in enumerate((gb_hbm, gc_hbm))
    ]
    for copy in most:
        copy.start()

    @pl.when(half == 0)
    def _():
        for copy in rest:
            copy.start()

    def finish():
        for copy in most:
            copy.wait()

        @pl.when(half == 0)
        def _():
            for copy in rest:
                copy.wait()

    return finish


def near_kernel(mine_ref, far_ref, gb_hbm, gc_hbm, extra_ref, stage, sems):
    half = lax.axis_index("gx") // (SPLIT // 2) % 2
    wait = unpack_half(half, mine_ref, far_ref, stage, gb_hbm, gc_hbm, sems)
    for i in range(2):
        extra_ref[i] = stage[i, 13]
    wait()


def finish_kernel(
    mine_ref, far_ref, extra_ref, gb_in, gc_in, gb_hbm, gc_hbm, ga_hbm, stage, first, ga_ref, sems
):
    half = 1 - lax.axis_index("gx") // (SPLIT // 2) % 2
    wait = unpack_half(half, mine_ref, far_ref, stage, gb_hbm, gc_hbm, sems)
    zero, one = [jnp.where(half == 1, stage[i, 13], extra_ref[i]) for i in range(2)]
    first[0:24] = zero[0:24]
    first[24:48] = zero[32:56]
    first[48:72] = one[0:24]
    first[72:96] = one[32:56]
    first[96:104] = one[24:32]
    first[104:108] = one[56:60]
    for ch in range(3):
        ga_ref[ch] = first[pl.ds(ch, 27, stride=4), :]
    last = pltpu.make_async_copy(ga_ref, ga_hbm, sems.at[4])
    last.start()
    wait()
    last.wait()


def partner(value, bit, count):
    return lax.ppermute(value, AXES, [(i, i ^ bit) for i in range(count)])


def gather_stage(value, bit, me, count):
    other = partner(value, bit, count)
    upper = (me & bit) != 0
    return jnp.where(upper, jnp.concatenate([other, value]), jnp.concatenate([value, other]))


def two_parts(v):
    high = rounded(v)
    return high, rounded(v - high)


def rounded(v):
    return lax.reduce_precision(v, 8, 7)


def sum_all(keep, send, me, count):
    total = keep + partner(send, 1, count)
    body, tail = total[:ROWS], total[ROWS:]
    half = ROWS // 2
    upper = (me & SPLIT) != 0
    high, low = two_parts(tail)
    away = lax.dynamic_slice_in_dim(body, jnp.where(upper, 0, half), half)
    sent = jnp.concatenate([rounded(away), high, low]).astype(BF16)
    got = partner(sent, SPLIT, count).astype(F32)
    body = lax.dynamic_slice_in_dim(body, jnp.where(upper, half, 0), half) + got[:half]
    tail = tail + got[half : half + 8] + got[half + 8 :]
    bit = 2
    while bit < count:
        if bit != SPLIT:
            high, low = two_parts(tail)
            body = rounded(body)
            sent = jnp.concatenate([body, high, low]).astype(BF16)
            got = partner(sent, bit, count).astype(F32)
            body = body + got[:half]
            tail = (high + low) + (got[half : half + 8] + got[half + 8 :])
        bit *= 2
    body = body.astype(BF16)
    beside = partner(body, SPLIT, count)
    far = partner(body, 1, count)
    return body, far, beside, tail


def on_device(
    loaded_fields,
    brick_home,
    liquid_mask,
    density_class,
    inverse_density,
    conv_a,
    bias_a,
    conv_b,
    bias_b,
    conv_c,
    bias_c,
    head_weight,
    head_bias,
):
    n_slots = lax.axis_size("gx")
    count = n_slots * lax.axis_size("gy")
    gx = lax.axis_index("gx")
    gy = lax.axis_index("gy")
    me = gx * 2 + gy
    cells = 2 * n_slots * NY * NZ
    smem = pl.BlockSpec(memory_space=pltpu.SMEM)
    vmem = pl.BlockSpec(memory_space=pltpu.VMEM)
    params = pltpu.CompilerParams(vmem_limit_bytes=VMEM_LIMIT)

    hbm = pl.BlockSpec(memory_space=pl.ANY)

    def shaped(shape, kind):
        return jax.ShapeDtypeStruct(shape, kind)

    def off_chip(v):
        return pltpu.with_memory_space_constraint(v, pltpu.HBM)

    block = pl.pallas_call(
        payload_kernel,
        out_shape=shaped((2, 8, 4, NZ), BF16),
        in_specs=[hbm] * 3,
        out_specs=vmem,
        scratch_shapes=[
            pltpu.VMEM((2, 2, 8, NZ), BF16),
            pltpu.VMEM((2, 8, NZ), jnp.int32),
            pltpu.VMEM((2, 8, NZ), jnp.int32),
            pltpu.VMEM((2, 8, 4, NZ), F32),
            pltpu.SemaphoreType.DMA((3,)),
        ],
        compiler_params=params,
        name="payload",
    )(*map(off_chip, (loaded_fields, liquid_mask, density_class)))
    lhs = shaped((6 * HID, 12 * HID), BF16)
    turned = shaped((36, HID, NZ), BF16)
    vector = pltpu.VMEM((1, HID), F32)

    def layouts2(args):
        return pl.pallas_call(
            second_lhs_kernel,
            out_shape=(shaped((HID, 144), BF16), lhs, turned),
            in_specs=[hbm] * 2,
            out_specs=(vmem,) * 3,
            scratch_shapes=[
                pltpu.VMEM((27, HID, HID), BF16),
                pltpu.VMEM((3, 27, HID), BF16),
                pltpu.SemaphoreType.DMA((2,)),
            ],
            compiler_params=params,
            name="lhs2",
        )(*map(off_chip, args))

    def layouts3(args):
        return pl.pallas_call(
            third_lhs_kernel,
            out_shape=(
                lhs,
                turned,
                shaped((4, HID, NZ), F32),
                pltpu.SMEM((n_slots,), jnp.int32),
                pltpu.SMEM((4,), F32),
            ),
            in_specs=[hbm] * 7,
            out_specs=(vmem,) * 3 + (smem,) * 2,
            scratch_shapes=[
                pltpu.VMEM((27, HID, HID), BF16),
                vector,
                vector,
                vector,
                pltpu.VMEM((1, HID), BF16),
                pltpu.SemaphoreType.DMA((7,)),
            ],
            compiler_params=params,
            name="lhs3",
        )(*map(off_chip, args))

    jobs = [
        (layouts2, (conv_b, conv_a.transpose(2, 0, 1))),
        (
            layouts3,
            (
                conv_c,
                *(v.reshape(1, HID) for v in (bias_a, bias_b, bias_c, head_weight)),
                brick_home,
                inverse_density,
            ),
        ),
    ]
    made = []
    mine = block[None]
    bit = 2
    while bit < count:
        if bit > 2 and jobs:
            job, args = jobs.pop(0)
            mine, args = lax.optimization_barrier((mine, args))
            results = job(args)
            mine = gather_stage(mine, bit, me, count)
            mine, results = lax.optimization_barrier((mine, results))
            made += results
        else:
            mine = gather_stage(mine, bit, me, count)
        bit *= 2
    for job, args in jobs:
        made += job(args)
    across = partner(mine, 1, count)
    wide = made[5]
    home, table = [pltpu.with_memory_space_constraint(v, pltpu.SMEM) for v in made[6:]]


    plane = shaped((PLANES, YY, NZ), F32)
    inputs = (shaped((PLANES, YY, 16, NZ), BF16), plane, plane, plane)
    prepared = pl.pallas_call(
        functools.partial(prepare_kernel, n_slots=n_slots),
        out_shape=inputs,
        in_specs=[smem, vmem],
        out_specs=(vmem,) * 4,
        scratch_shapes=[pltpu.SMEM((n_slots,), jnp.int32)],
        compiler_params=params,
        name="prepare",
    )(home, mine)

    pressure, score, sbuf, hbuf = pl.pallas_call(
        functools.partial(forward_kernel, n_slots=n_slots, cells=cells),
        out_shape=(
            shaped((2, 8, NZ), F32),
            shaped((2, 8, NZ), F32),
            shaped((S_BLOCKS, HID, NZ), F32),
            shaped((H_BLOCKS, HID, NZ), BF16),
        ),
        in_specs=[smem] * 3 + [vmem] * 11,
        out_specs=(hbm,) + (vmem,) * 3,
        scratch_shapes=[
            pltpu.VMEM((2, 8, NZ), F32),
            pltpu.SemaphoreType.DMA((1,)),
            pltpu.SMEM((n_slots,), jnp.int32),
            pltpu.VMEM((PLANES, YY, 16, NZ), BF16),
            pltpu.VMEM((PLANES, YY, NZ), F32),
            pltpu.VMEM((PLANES, YY, NZ), F32),
            pltpu.VMEM((PLANES, YY, NZ), F32),
            pltpu.VMEM((PLANES, YY, HID, NZ), BF16),
            pltpu.VMEM((PLANES, YY, HID, NZ), BF16),
            pltpu.VMEM((6, 10, HID, NZ), BF16),
            pltpu.VMEM((PLANES, YY, NZ), F32),
            pltpu.VMEM((PLANES, YY, NZ), F32),
        ],
        compiler_params=params,
        name="forward",
    )(
        home,
        table,
        head_bias,
        across,
        *prepared,
        *made[:6],
    )

    swap2 = lax.ppermute(score, "gx", [(i, ((i + 1) ^ 1) - 1) for i in range(1, n_slots - 1)])
    swap1 = lax.ppermute(score, "gx", [(i, i ^ 1) for i in range(n_slots)])
    across_score = partner(score, 1, count)
    early = pl.pallas_call(
        early_kernel,
        out_shape=(
            shaped((WROWS, NZ), F32),
            shaped((8, NZ), F32),
            shaped((9 * HID + 144, 16 * NZ), BF16),
        ),
        in_specs=[vmem] * 4,
        out_specs=(vmem,) * 3,
        scratch_shapes=[
            pltpu.VMEM((3 * HID, 16 * NZ), BF16),
            pltpu.VMEM((9 * HID, 16 * NZ), BF16),
        ],
        compiler_params=params,
        name="early",
    )(score, sbuf, hbuf, wide)
    early, swap2, swap1 = lax.optimization_barrier((early, swap2, swap1))
    scores = [score, across_score]
    for value in (swap2, swap1):
        scores += [value, partner(value, 1, count)]

    keep, send = pl.pallas_call(
        backward_kernel,
        out_shape=(shaped((ROWS + 8, NZ), F32), shaped((ROWS + 8, NZ), F32)),
        in_specs=[vmem] * 12,
        out_specs=(vmem, vmem),
        scratch_shapes=[
            pltpu.VMEM((6, NY, NZ), F32),
            pltpu.VMEM((6, FRAME, HID, NZ), BF16),
            pltpu.VMEM((4, FRAME, HID, NZ), BF16),
            pltpu.VMEM((2, 8, HID, NZ), BF16),
            pltpu.VMEM((3 * HID, 16 * NZ), BF16),
            pltpu.VMEM((2, ROWS, NZ), F32),
        ],
        compiler_params=params,
        name="backward",
    )(
        *scores,
        sbuf,
        hbuf,
        wide,
        *early,
    )

    body, far, beside, tail = sum_all(keep, send, me, count)
    weights = shaped((27, HID, HID), F32)
    stage = pltpu.VMEM((2, 14, HID, HID), F32)
    near = pl.pallas_call(
        near_kernel,
        out_shape=(weights, weights, shaped((2, HID, HID), F32)),
        in_specs=[vmem] * 2,
        out_specs=(hbm, hbm, vmem),
        scratch_shapes=[stage, pltpu.SemaphoreType.DMA((4,))],
        compiler_params=params,
        name="near",
    )(body, far)
    near, beside = lax.optimization_barrier((near, beside))
    half_b, half_c, extra = near
    grad_b, grad_c, grad_a = pl.pallas_call(
        finish_kernel,
        out_shape=(weights, weights, shaped((3, 27, HID), F32)),
        in_specs=[vmem] * 3 + [hbm] * 2,
        out_specs=(hbm, hbm, hbm),
        scratch_shapes=[
            stage,
            pltpu.VMEM((112, HID), F32),
            pltpu.VMEM((3, 27, HID), F32),
            pltpu.SemaphoreType.DMA((5,)),
        ],
        input_output_aliases={3: 0, 4: 1},
        compiler_params=params,
        name="finish",
    )(beside, partner(beside, 1, count), extra, half_b, half_c)
    return (
        pressure,
        tail[2, :1],
        grad_a.transpose(1, 2, 0),
        tail[0, :HID],
        grad_b,
        tail[0, HID:],
        grad_c,
        tail[1, :HID],
        tail[1, HID:],
    )


def solution(mesh):
    grid = P(("grp", "gx"), "gy", None)
    part = P("grp")
    stack = P("grp", None, None)
    return jax.shard_map(
        on_device,
        mesh=mesh,
        in_specs=(P(None, ("grp", "gx"), "gy", None), part, grid, grid) + (P(),) * 9,
        out_specs=(grid, part, stack, part, stack, part, stack, part, part),
        check_vma=False,
    )
```

```python
import functools

import jax
import jax.numpy as jnp
from jax import lax
from jax.experimental import pallas as pl
from jax.experimental.pallas import tpu as pltpu
from jax.sharding import PartitionSpec as P

F32 = jnp.float32
BF16 = jnp.bfloat16
AXES = ("gx", "gy")
HID = 64
NZ = 128
NY = 16
YY = NY + 2
PLANES = 12
MID = 5
FRAME = 12
WROWS = 864
ROWS = 896
SPLIT = 4
VMEM_LIMIT = 24 * 1024 * 1024
S1, S2, S3, HEAD, LOSS, S_BLOCKS = 0, 24, 72, 132, 133, 134
H1, H2, X0, WB, WC, H_BLOCKS = 0, 48, 96, 108, 144, 180


def shift_right(v):
    lane = lax.broadcasted_iota(jnp.int32, v.shape, v.ndim - 1)
    return jnp.where(lane == 0, 0.0, pltpu.roll(v, 1, v.ndim - 1))


def shift_left(v):
    lane = lax.broadcasted_iota(jnp.int32, v.shape, v.ndim - 1)
    return jnp.where(lane == NZ - 1, 0.0, pltpu.roll(v, NZ - 1, v.ndim - 1))


def dot_nn(a, b):
    return jnp.dot(a, b, preferred_element_type=F32)


def dot_nt(a, b):
    return lax.dot_general(a, b, (((1,), (1,)), ((), ())), preferred_element_type=F32)


def taps(src, X, y):
    out = []
    for a in range(3):
        for b in range(3):
            out.append(
                jnp.concatenate([src[X + a - 1, y + b - 1], src[X + a - 1, y + b]], axis=1)
            )
    return jnp.concatenate(out, axis=0)


def pair_taps(src, X, y, n):
    out = []
    for b in range(3):
        for x in range(4):
            rows = [src[X + x - 1, y + b - 1 + k] for k in range(n)]
            out.append(jnp.concatenate(rows, axis=1) if n > 1 else rows[0])
    return jnp.concatenate(out, axis=0)


def row_groups(count):
    return [(j, min(2, count - j)) for j in range(0, count, 2)]


def lane_taps(Y, d, k):
    part = Y[d * 3 * HID : (d + 1) * 3 * HID, k * NZ : (k + 1) * NZ]
    return part[HID : 2 * HID] + shift_right(part[:HID]) + shift_left(part[2 * HID :])


def activate(z):
    sig = 0.5 * jnp.tanh(0.5 * z) + 0.5
    return z * sig, sig


def slope_of(z, sig):
    return sig * (1.0 + z * (1.0 - sig))


def payload_kernel(fields_hbm, liquid_hbm, class_hbm, out_ref, fields, liquid, classes, rows, sems):
    copies = [
        pltpu.make_async_copy(src, dst, sems.at[i])
        for i, (src, dst) in enumerate(
            ((fields_hbm, fields), (liquid_hbm, liquid), (class_hbm, classes))
        )
    ]
    for copy in copies:
        copy.start()
    for copy in copies:
        copy.wait()
    for x in range(2):
        planes = (fields[0, x], fields[1, x], liquid[x], classes[x])
        for p, plane in enumerate(planes):
            plane = plane.astype(F32)
            for y in range(8):
                rows[x, y, p : p + 1, :] = plane[y : y + 1]
    out_ref[...] = rows[...].astype(BF16)


def conv_lhs(w, fwd, bwd):
    zero = jnp.zeros((HID, HID), F32)
    for b in range(3):
        for e in range(3):
            ahead = [w[9 * a + 3 * b + e].astype(F32) for a in range(3)]
            back = [w[26 - (9 * a + 3 * b + e)].astype(F32) for a in range(3)]
            for d in range(2):
                for half in range(2):
                    low, high = 2 * half - d, 2 * half + 1 - d
                    rows = slice((3 * d + e) * HID, (3 * d + e + 1) * HID)
                    tile = 2 * b + half
                    pick = [
                        [v[a] if 0 <= a <= 2 else zero for a in (low, high)] for v in (ahead, back)
                    ]
                    fwd[rows, tile * NZ : (tile + 1) * NZ] = jnp.concatenate(
                        pick[0], axis=1
                    ).astype(BF16)
                    bwd[6 * tile + 3 * d + e] = jnp.concatenate(pick[1], axis=0).T.astype(BF16)


def second_lhs_kernel(wb_hbm, wa_hbm, fa, fb, tb, wb_ref, wa_ref, sems):
    copies = [
        pltpu.make_async_copy(src, dst, sems.at[i])
        for i, (src, dst) in enumerate(((wb_hbm, wb_ref), (wa_hbm, wa_ref)))
    ]
    for copy in copies:
        copy.start()
    for copy in copies:
        copy.wait()
    conv_lhs(wb_ref, fb, tb)
    tap = lax.broadcasted_iota(jnp.int32, (27, 144), 0)
    col = lax.broadcasted_iota(jnp.int32, (27, 144), 1)
    total = jnp.zeros((HID, 144), F32)
    for ch in range(3):
        spot = 16 * (tap // 3) + 4 * (tap - 3 * (tap // 3)) + ch
        pick = jnp.where(col == spot, 1.0, 0.0).astype(BF16)
        total += dot_nn(wa_ref[ch].astype(F32).T.astype(BF16), pick)
    fa[...] = total.astype(BF16)


def third_lhs_kernel(
    wc_hbm,
    ba_hbm,
    bb_hbm,
    bc_hbm,
    hw_hbm,
    home_hbm,
    invd_hbm,
    fc,
    tc,
    wide_ref,
    home_ref,
    invd_ref,
    wc_ref,
    ba_ref,
    bb_ref,
    bc_ref,
    hw_ref,
    sems,
):
    copies = [
        pltpu.make_async_copy(src, dst, sems.at[i])
        for i, (src, dst) in enumerate(
            (
                (wc_hbm, wc_ref),
                (ba_hbm, ba_ref),
                (bb_hbm, bb_ref),
                (bc_hbm, bc_ref),
                (hw_hbm, hw_ref),
                (home_hbm, home_ref),
                (invd_hbm, invd_ref),
            )
        )
    ]
    for copy in copies:
        copy.start()
    for copy in copies:
        copy.wait()
    for i, ref in enumerate((ba_ref, bb_ref, bc_ref, hw_ref)):
        wide_ref[i] = jnp.broadcast_to(ref[...].astype(F32), (NZ, HID)).T
    conv_lhs(wc_ref, fc, tc)


def forward_kernel(
    home_ref,
    invd_ref,
    hb_ref,
    mine_ref,
    other_ref,
    wa_ref,
    wb_ref,
    tb_ref,
    wc_ref,
    tc_ref,
    wide_ref,
    p_hbm,
    gs_out,
    sbuf,
    hbuf,
    p_out,
    sems,
    inv_ref,
    x0s,
    liq,
    scl,
    f1,
    h1,
    h2,
    h3o,
    pf,
    rs,
    *,
    n_slots,
    cells,
):
    gx = lax.axis_index("gx")
    gy = lax.axis_index("gy")
    for ref in (x0s, h1, h2):
        z = jnp.zeros(ref.shape[2:], ref.dtype)
        for X in range(PLANES):
            ref[X, 0] = z
            ref[X, NY + 1] = z
    for ref in (liq, scl, f1, pf, rs):
        for X in range(PLANES):
            ref[X] = jnp.zeros((YY, NZ), F32)
    for s in range(n_slots):
        inv_ref[home_ref[s]] = s

    def load_plane(X):
        xg = 2 * gx - MID + X
        ok = jnp.where((xg >= 0) & (xg < 2 * n_slots), 1.0, 0.0).astype(F32)
        xc = jnp.clip(xg, 0, 2 * n_slots - 1)
        home = xc // 2
        half = xc - 2 * home
        slot = inv_ref[home]
        row4 = lax.broadcasted_iota(jnp.int32, (4, NZ), 0)
        for i in range(NY):
            src = (mine_ref, other_ref)[i // 8]
            fb = src[slot, half, i % 8].astype(F32) * ok
            mb = src[home, half, i % 8].astype(F32)
            y = 8 * (gy if i < 8 else 1 - gy) + i % 8
            lq = mb[2:3] * ok
            base = jnp.where(row4 < 2, fb, jnp.where(row4 == 2, mb * ok, 0.0))
            k12 = jnp.concatenate(
                [shift_right(base), base, shift_left(base), jnp.zeros((4, NZ), F32)], axis=0
            )
            x0s[X, y + 1] = k12.astype(BF16)
            liq[X, pl.ds(y + 1, 1), :] = lq
            scl[X, pl.ds(y + 1, 1), :] = mb[3:4]
            f1[X, pl.ds(y + 1, 1), :] = fb[1:2]
        cl = scl[X, 1 : NY + 1, :]
        sc = jnp.zeros((NY, NZ), F32)
        for k in range(4):
            sc = jnp.where(cl == k, invd_ref[k], sc)
        scl[X, 1 : NY + 1, :] = sc * liq[X, 1 : NY + 1, :]

    def load_planes(i, c):
        for k in range(3):
            load_plane(3 * i + k)
        return c

    lax.fori_loop(0, PLANES // 3, load_planes, 0)

    def planes(count, body):
        def step(i, c):
            body(i)
            return c

        lax.fori_loop(0, count, step, 0)

    y4 = gy * 4 + 1

    def layer1(X, slot):
        for j in range(6):
            y = y4 + 2 * j
            Y = dot_nn(wa_ref[...], taps(x0s, X, y))
            for k in range(2):
                z = Y[:, k * NZ : (k + 1) * NZ] + wide_ref[0]
                m = liq[X, pl.ds(y + k, 1), :]
                act, sig = activate(z)
                h1[X, y + k] = (act * m).astype(BF16)
                if slot is not None:
                    sbuf[S1 + 12 * slot + 2 * j + k] = slope_of(z, sig) * m

    def layer1_pair(i):
        X = 1 + 2 * i + 2 * (i // 2)
        layer1(X, None)
        layer1(X + 1, None)

    planes(4, layer1_pair)
    layer1(MID, 0)
    layer1(MID + 1, 1)

    y3 = gy * 5 + 1

    def layer2(X, slot):
        for j, n in row_groups(11):
            y = y3 + j
            Y = dot_nn(wb_ref[...], pair_taps(h1, X, y, n))
            for d in range(2):
                for k in range(n):
                    z = lane_taps(Y, d, k) + wide_ref[1]
                    m = liq[X + d, pl.ds(y + k, 1), :]
                    act, sig = activate(z)
                    h2[X + d, y + k] = (act * m).astype(BF16)
                    if slot is not None:
                        sbuf[S2 + 12 * (slot + d) + j + k] = slope_of(z, sig) * m

    planes(2, lambda i: layer2(2 + 6 * i, None))
    planes(2, lambda i: layer2(MID - 1 + 2 * i, 2 * i))

    y2 = gy * 6 + 1

    def layer3(i):
        X = MID - 2 + 2 * i
        for j in range(5):
            y = y2 + 2 * j
            Y = dot_nn(wc_ref[...], pair_taps(h2, X, y, 2))
            for d in range(2):
                for k in range(2):
                    z = lane_taps(Y, d, k) + wide_ref[2]
                    m = liq[X + d, pl.ds(y + k, 1), :]
                    act, sig = activate(z)
                    h3 = (act * m).astype(BF16)
                    score = jnp.sum(wide_ref[3] * h3.astype(F32), axis=0, keepdims=True)
                    pf[X + d, pl.ds(y + k, 1), :] = m * (score + hb_ref[0])
                    sbuf[S3 + 10 * (2 * i + d) + 2 * j + k] = slope_of(z, sig) * m
                    h3o[2 * i + d, 2 * j + k] = h3

    planes(3, layer3)

    def operator(val, X):
        v = val[X, 1 : NY + 1, :]
        s = scl[X, 1 : NY + 1, :]
        q = liq[X, 1 : NY + 1, :]

        def term(nv, ns, nq):
            return 0.5 * (s * nq + ns * q) * (nv - v)

        total = term(val[X + 1, 1 : NY + 1, :], scl[X + 1, 1 : NY + 1, :], liq[X + 1, 1 : NY + 1, :])
        total += term(val[X - 1, 1 : NY + 1, :], scl[X - 1, 1 : NY + 1, :], liq[X - 1, 1 : NY + 1, :])
        total += term(val[X, 2 : NY + 2, :], scl[X, 2 : NY + 2, :], liq[X, 2 : NY + 2, :])
        total += term(val[X, 0:NY, :], scl[X, 0:NY, :], liq[X, 0:NY, :])
        total += term(shift_left(v), shift_left(s), shift_left(q))
        total += term(shift_right(v), shift_right(s), shift_right(q))
        return total

    for X in range(MID - 1, MID + 3):
        rs[X, 1 : NY + 1, :] = operator(pf, X) - liq[X, 1 : NY + 1, :] * f1[X, 1 : NY + 1, :]
    own_y = pl.ds(pl.multiple_of(gy * 8, 8) + 1, 8)
    loss = jnp.zeros((8, NZ), F32)
    for k in range(2):
        p_out[k] = pf[MID + k, own_y, :]
        r = rs[MID + k, own_y, :]
        loss += r * r
    leave = pltpu.make_async_copy(p_out, p_hbm, sems.at[0])
    leave.start()
    sbuf[LOSS, 0:8, :] = loss * (1.0 / cells)
    for X in range(MID - 1, MID + 3):
        rs[X] = rs[X] * (2.0 / cells)
    for k in range(2):
        X = MID + k
        pf[k, 1 : NY + 1, :] = liq[X, 1 : NY + 1, :] * operator(rs, X)
    for k in range(2):
        gs_out[k] = pf[k, own_y, :]

    head = jnp.zeros((HID, NZ), F32)
    for i in range(16):
        X, dy = i // 8, i % 8
        head += pf[X, pl.ds(gy * 8 + 1 + dy, 1), :] * h3o[2 + X, gy * 2 + dy].astype(F32)
    sbuf[HEAD] = head

    f0 = gy * 6

    def copy_out(i):
        for l in range(FRAME):
            r = (l % 4) * 16
            hbuf[X0 + 3 * i + l // 4, r : r + 16, :] = x0s[MID - 1 + i, f0 + l]
            hbuf[H1 + FRAME * i + l] = h1[MID - 1 + i, f0 + l]
            hbuf[H2 + FRAME * i + l] = h2[MID - 1 + i, f0 + l]

    planes(4, copy_out)
    for r in range(36):
        hbuf[WB + r] = tb_ref[r]
        hbuf[WC + r] = tc_ref[r]
    leave.wait()


def stack_gradient(raw, gcat, cols):
    g = raw.astype(F32)
    gcat[0:HID, cols] = shift_left(g).astype(BF16)
    gcat[HID : 2 * HID, cols] = raw
    gcat[2 * HID : 3 * HID, cols] = shift_right(g).astype(BF16)
    return g


def store_weights(W, ref):
    for a in range(3):
        for b in range(3):
            for e in range(3):
                t = 9 * a + 3 * b + e
                k = 3 * a + b
                blk = W[e * HID : (e + 1) * HID, k * HID : (k + 1) * HID]
                ref[t * 32 : (t + 1) * 32, 0:HID] = blk[:32]
                ref[t * 32 : (t + 1) * 32, HID:NZ] = blk[32:]


def channel_sums(first, second):
    rows = [jnp.sum(v, axis=1, keepdims=True).reshape(1, HID) for v in (first, second)]
    return jnp.concatenate(rows, axis=1)


def early_kernel(score_ref, sbuf, hbuf, wide_ref, gc_ref, bias_ref, cat_ref, gcat, hcat):
    gy = lax.axis_index("gy")
    own = gy * 2 + 1
    bias = jnp.zeros((HID, NZ), F32)
    for i in range(16):
        X, dy = i // 8, i % 8
        y = own + dy
        g = score_ref[X, dy : dy + 1, :]
        raw = (g * wide_ref[3] * sbuf[S3 + 10 * (X + 2) + y - 1]).astype(BF16)
        cols = slice(i * NZ, (i + 1) * NZ)
        bias += stack_gradient(raw, gcat, cols)
        for a in range(3):
            for b in range(3):
                k = 3 * a + b
                row = FRAME * (X + a) + y + b - 1
                hcat[k * HID : (k + 1) * HID, cols] = hbuf[H2 + row]
                cat_ref[k * HID : (k + 1) * HID, cols] = hbuf[H1 + row]
                l = y + b - 1
                q = l // 4
                cat_ref[9 * HID + k * 16 : 9 * HID + (k + 1) * 16, cols] = hbuf[
                    X0 + 3 * (X + a) + q, pl.ds(pl.multiple_of((l - 4 * q) * 16, 16), 16), :
                ]
    store_weights(dot_nt(gcat[...], hcat[...]), gc_ref)
    loss = jnp.sum(jnp.sum(sbuf[LOSS, 0:8, :], axis=0, keepdims=True), axis=1, keepdims=True)
    bias_ref[...] = jnp.zeros((8, NZ), F32)
    bias_ref[1:2, :] = channel_sums(bias, sbuf[HEAD])
    bias_ref[2:3, :] = jnp.broadcast_to(loss, (1, NZ))


def backward_kernel(
    gm_ref,
    gmo_ref,
    p2_ref,
    p2o_ref,
    p1_ref,
    p1o_ref,
    sbuf,
    hbuf,
    wide_ref,
    gc_ref,
    bias_ref,
    cat_ref,
    keep_ref,
    send_ref,
    gs,
    g3,
    g2,
    g1,
    gcat,
    acc,
):
    gy = lax.axis_index("gy")
    even = lax.axis_index("gx") % 2 == 0
    own_half = pl.ds(pl.multiple_of(8 * gy, 8), 8)
    far_half = pl.ds(pl.multiple_of(8 - 8 * gy, 8), 8)
    for half, gm, p1, p2 in (
        (own_half, gm_ref, p1_ref, p2_ref),
        (far_half, gmo_ref, p1o_ref, p2o_ref),
    ):
        for k in range(2):
            gs[k, half, :] = jnp.where(even, p2[k], p1[k])
            gs[2 + k, half, :] = gm[k]
            gs[4 + k, half, :] = jnp.where(even, p1[k], p2[k])

    def lhs_at(base):
        tiles = [
            jnp.concatenate([hbuf[base + 6 * t + r] for r in range(6)], axis=0) for t in range(6)
        ]
        return jnp.concatenate(tiles, axis=1)

    for ref in (g3, g2):
        z = jnp.zeros((HID, NZ), BF16)
        for X in range(ref.shape[0]):
            ref[X, 0] = z
            ref[X, FRAME - 1] = z

    def planes(count, body):
        def step(i, c):
            body(i)
            return c

        lax.fori_loop(0, count, step, 0)

    def back3(X):
        for j in range(10):
            g = gs[X, pl.ds(gy * 6 + j, 1), :]
            g3[X, j + 1] = (g * wide_ref[3] * sbuf[S3 + 10 * X + j]).astype(BF16)

    planes(6, back3)

    for X in range(2):
        for r in range(WROWS, ROWS, 8):
            acc[X, r : r + 8, :] = jnp.zeros((8, NZ), F32)
    own = gy * 2 + 1

    def back2(i):
        X = 2 * i
        for j, n in row_groups(9):
            y = 1 + gy + j
            Y = dot_nn(lhs_at(WC), pair_taps(g3, X + 1, y, n))
            for d in range(2):
                for k in range(n):
                    row = 2 * gy + j + k
                    g2[X + d, y + k] = (
                        lane_taps(Y, d, k) * sbuf[S2 + 12 * (X + d) + row]
                    ).astype(BF16)

    planes(2, back2)
    bias_b = jnp.zeros((HID, NZ), F32)
    for i in range(16):
        cols = slice(i * NZ, (i + 1) * NZ)
        bias_b += stack_gradient(g2[1 + i // 8, own + i % 8], gcat, cols)
    store_weights(dot_nt(gcat[...], cat_ref[0 : 9 * HID, :]), acc.at[0])

    for j in range(4):
        y = own + 2 * j
        Y = dot_nn(lhs_at(WB), pair_taps(g2, 1, y, 2))
        for d in range(2):
            for k in range(2):
                row = gy * 4 + 2 * j + k
                g1[d, 2 * j + k] = (lane_taps(Y, d, k) * sbuf[S1 + 12 * d + row]).astype(BF16)

    bias_a = jnp.zeros((HID, NZ), F32)
    for i in range(16):
        raw = g1[i // 8, i % 8]
        bias_a += raw.astype(F32)
        gcat[0:HID, i * NZ : (i + 1) * NZ] = raw
    A = dot_nt(cat_ref[9 * HID : 9 * HID + 144, :], gcat[0:HID, :])
    for k in range(8):
        blk = A[16 * k : 16 * k + 12]
        which, spot = k // 4, k % 4
        r0 = WROWS + 12 * (spot % 2)
        c0 = HID * (spot // 2)
        acc[which, r0 : r0 + 12, c0 : c0 + HID] = blk
    acc[1, WROWS + 24 : WROWS + 32, 0:HID] = A[128:136]
    acc[1, WROWS + 24 : WROWS + 28, HID:NZ] = A[136:140]
    acc[1, 0:WROWS, :] = gc_ref[...]
    keep_ref[0:ROWS] = acc[gy]
    send_ref[0:ROWS] = acc[1 - gy]
    sums = channel_sums(bias_a, bias_b)
    for ref in (keep_ref, send_ref):
        ref[ROWS : ROWS + 8, :] = bias_ref[...]
        ref[ROWS : ROWS + 1, :] = sums


def unpack_half(half, mine_ref, far_ref, stage, gb_hbm, gc_hbm, sems):
    gy = lax.axis_index("gy")
    for ref, which in ((mine_ref, gy), (far_ref, 1 - gy)):
        for j in range(14):
            v = ref[32 * j : 32 * j + 32].astype(F32)
            stage[which, j, 0:32, :] = v[:, :HID]
            stage[which, j, 32:HID, :] = v[:, HID:]
    most = [
        pltpu.make_async_copy(stage.at[i, pl.ds(0, 13)], dst.at[pl.ds(14 * half, 13)], sems.at[i])
        for i, dst in enumerate((gb_hbm, gc_hbm))
    ]
    rest = [
        pltpu.make_async_copy(stage.at[i, 13], dst.at[13], sems.at[2 + i])
        for i, dst in enumerate((gb_hbm, gc_hbm))
    ]
    for copy in most:
        copy.start()

    @pl.when(half == 0)
    def _():
        for copy in rest:
            copy.start()

    def finish():
        for copy in most:
            copy.wait()

        @pl.when(half == 0)
        def _():
            for copy in rest:
                copy.wait()

    return finish


def near_kernel(mine_ref, far_ref, gb_hbm, gc_hbm, extra_ref, stage, sems):
    half = lax.axis_index("gx") // (SPLIT // 2) % 2
    wait = unpack_half(half, mine_ref, far_ref, stage, gb_hbm, gc_hbm, sems)
    for i in range(2):
        extra_ref[i] = stage[i, 13]
    wait()


def finish_kernel(
    mine_ref, far_ref, extra_ref, gb_in, gc_in, gb_hbm, gc_hbm, ga_hbm, stage, first, ga_ref, sems
):
    half = 1 - lax.axis_index("gx") // (SPLIT // 2) % 2
    wait = unpack_half(half, mine_ref, far_ref, stage, gb_hbm, gc_hbm, sems)
    zero, one = [jnp.where(half == 1, stage[i, 13], extra_ref[i]) for i in range(2)]
    first[0:24] = zero[0:24]
    first[24:48] = zero[32:56]
    first[48:72] = one[0:24]
    first[72:96] = one[32:56]
    first[96:104] = one[24:32]
    first[104:108] = one[56:60]
    for ch in range(3):
        ga_ref[ch] = first[pl.ds(ch, 27, stride=4), :]
    last = pltpu.make_async_copy(ga_ref, ga_hbm, sems.at[4])
    last.start()
    wait()
    last.wait()


def partner(value, bit, count):
    return lax.ppermute(value, AXES, [(i, i ^ bit) for i in range(count)])


def gather_stage(value, bit, me, count):
    other = partner(value, bit, count)
    upper = (me & bit) != 0
    return jnp.where(upper, jnp.concatenate([other, value]), jnp.concatenate([value, other]))


def two_parts(v):
    high = rounded(v)
    return high, rounded(v - high)


def rounded(v):
    return lax.reduce_precision(v, 8, 7)


def sum_all(keep, send, me, count):
    total = keep + partner(send, 1, count)
    body, tail = total[:ROWS], total[ROWS:]
    half = ROWS // 2
    upper = (me & SPLIT) != 0
    high, low = two_parts(tail)
    away = lax.dynamic_slice_in_dim(body, jnp.where(upper, 0, half), half)
    sent = jnp.concatenate([rounded(away), high, low]).astype(BF16)
    got = partner(sent, SPLIT, count).astype(F32)
    body = lax.dynamic_slice_in_dim(body, jnp.where(upper, half, 0), half) + got[:half]
    tail = tail + got[half : half + 8] + got[half + 8 :]
    bit = 2
    while bit < count:
        if bit != SPLIT:
            high, low = two_parts(tail)
            body = rounded(body)
            sent = jnp.concatenate([body, high, low]).astype(BF16)
            got = partner(sent, bit, count).astype(F32)
            body = body + got[:half]
            tail = (high + low) + (got[half : half + 8] + got[half + 8 :])
        bit *= 2
    body = body.astype(BF16)
    beside = partner(body, SPLIT, count)
    far = partner(body, 1, count)
    return body, far, beside, tail


def on_device(
    loaded_fields,
    brick_home,
    liquid_mask,
    density_class,
    inverse_density,
    conv_a,
    bias_a,
    conv_b,
    bias_b,
    conv_c,
    bias_c,
    head_weight,
    head_bias,
):
    n_slots = lax.axis_size("gx")
    count = n_slots * lax.axis_size("gy")
    gx = lax.axis_index("gx")
    gy = lax.axis_index("gy")
    me = gx * 2 + gy
    cells = 2 * n_slots * NY * NZ
    smem = pl.BlockSpec(memory_space=pltpu.SMEM)
    vmem = pl.BlockSpec(memory_space=pltpu.VMEM)
    params = pltpu.CompilerParams(vmem_limit_bytes=VMEM_LIMIT)

    hbm = pl.BlockSpec(memory_space=pl.ANY)

    def shaped(shape, kind):
        return jax.ShapeDtypeStruct(shape, kind)

    def off_chip(v):
        return pltpu.with_memory_space_constraint(v, pltpu.HBM)

    block = pl.pallas_call(
        payload_kernel,
        out_shape=shaped((2, 8, 4, NZ), BF16),
        in_specs=[hbm] * 3,
        out_specs=vmem,
        scratch_shapes=[
            pltpu.VMEM((2, 2, 8, NZ), BF16),
            pltpu.VMEM((2, 8, NZ), jnp.int32),
            pltpu.VMEM((2, 8, NZ), jnp.int32),
            pltpu.VMEM((2, 8, 4, NZ), F32),
            pltpu.SemaphoreType.DMA((3,)),
        ],
        compiler_params=params,
        name="payload",
    )(*map(off_chip, (loaded_fields, liquid_mask, density_class)))
    lhs = shaped((6 * HID, 12 * HID), BF16)
    turned = shaped((36, HID, NZ), BF16)
    vector = pltpu.VMEM((1, HID), F32)

    def layouts2(args):
        return pl.pallas_call(
            second_lhs_kernel,
            out_shape=(shaped((HID, 144), BF16), lhs, turned),
            in_specs=[hbm] * 2,
            out_specs=(vmem,) * 3,
            scratch_shapes=[
                pltpu.VMEM((27, HID, HID), BF16),
                pltpu.VMEM((3, 27, HID), BF16),
                pltpu.SemaphoreType.DMA((2,)),
            ],
            compiler_params=params,
            name="lhs2",
        )(*map(off_chip, args))

    def layouts3(args):
        return pl.pallas_call(
            third_lhs_kernel,
            out_shape=(
                lhs,
                turned,
                shaped((4, HID, NZ), F32),
                pltpu.SMEM((n_slots,), jnp.int32),
                pltpu.SMEM((4,), F32),
            ),
            in_specs=[hbm] * 7,
            out_specs=(vmem,) * 3 + (smem,) * 2,
            scratch_shapes=[
                pltpu.VMEM((27, HID, HID), BF16),
                vector,
                vector,
                vector,
                pltpu.VMEM((1, HID), BF16),
                pltpu.SemaphoreType.DMA((7,)),
            ],
            compiler_params=params,
            name="lhs3",
        )(*map(off_chip, args))

    jobs = [
        (layouts2, (conv_b, conv_a.transpose(2, 0, 1))),
        (
            layouts3,
            (
                conv_c,
                *(v.reshape(1, HID) for v in (bias_a, bias_b, bias_c, head_weight)),
                brick_home,
                inverse_density,
            ),
        ),
    ]
    made = []
    mine = block[None]
    bit = 2
    while bit < count:
        if bit > 2 and jobs:
            job, args = jobs.pop(0)
            mine, args = lax.optimization_barrier((mine, args))
            results = job(args)
            mine = gather_stage(mine, bit, me, count)
            mine, results = lax.optimization_barrier((mine, results))
            made += results
        else:
            mine = gather_stage(mine, bit, me, count)
        bit *= 2
    for job, args in jobs:
        made += job(args)
    across = partner(mine, 1, count)
    wide = made[5]
    home, table = [pltpu.with_memory_space_constraint(v, pltpu.SMEM) for v in made[6:]]


    pressure, score, sbuf, hbuf = pl.pallas_call(
        functools.partial(forward_kernel, n_slots=n_slots, cells=cells),
        out_shape=(
            shaped((2, 8, NZ), F32),
            shaped((2, 8, NZ), F32),
            shaped((S_BLOCKS, HID, NZ), F32),
            shaped((H_BLOCKS, HID, NZ), BF16),
        ),
        in_specs=[smem] * 3 + [vmem] * 8,
        out_specs=(hbm,) + (vmem,) * 3,
        scratch_shapes=[
            pltpu.VMEM((2, 8, NZ), F32),
            pltpu.SemaphoreType.DMA((1,)),
            pltpu.SMEM((n_slots,), jnp.int32),
            pltpu.VMEM((PLANES, YY, 16, NZ), BF16),
            pltpu.VMEM((PLANES, YY, NZ), F32),
            pltpu.VMEM((PLANES, YY, NZ), F32),
            pltpu.VMEM((PLANES, YY, NZ), F32),
            pltpu.VMEM((PLANES, YY, HID, NZ), BF16),
            pltpu.VMEM((PLANES, YY, HID, NZ), BF16),
            pltpu.VMEM((6, 10, HID, NZ), BF16),
            pltpu.VMEM((PLANES, YY, NZ), F32),
            pltpu.VMEM((PLANES, YY, NZ), F32),
        ],
        compiler_params=params,
        name="forward",
    )(
        home,
        table,
        head_bias,
        mine,
        across,
        *made[:6],
    )

    swap2 = lax.ppermute(score, "gx", [(i, ((i + 1) ^ 1) - 1) for i in range(1, n_slots - 1)])
    swap1 = lax.ppermute(score, "gx", [(i, i ^ 1) for i in range(n_slots)])
    across_score = partner(score, 1, count)
    early = pl.pallas_call(
        early_kernel,
        out_shape=(
            shaped((WROWS, NZ), F32),
            shaped((8, NZ), F32),
            shaped((9 * HID + 144, 16 * NZ), BF16),
        ),
        in_specs=[vmem] * 4,
        out_specs=(vmem,) * 3,
        scratch_shapes=[
            pltpu.VMEM((3 * HID, 16 * NZ), BF16),
            pltpu.VMEM((9 * HID, 16 * NZ), BF16),
        ],
        compiler_params=params,
        name="early",
    )(score, sbuf, hbuf, wide)
    early, swap2, swap1 = lax.optimization_barrier((early, swap2, swap1))
    scores = [score, across_score]
    for value in (swap2, swap1):
        scores += [value, partner(value, 1, count)]

    keep, send = pl.pallas_call(
        backward_kernel,
        out_shape=(shaped((ROWS + 8, NZ), F32), shaped((ROWS + 8, NZ), F32)),
        in_specs=[vmem] * 12,
        out_specs=(vmem, vmem),
        scratch_shapes=[
            pltpu.VMEM((6, NY, NZ), F32),
            pltpu.VMEM((6, FRAME, HID, NZ), BF16),
            pltpu.VMEM((4, FRAME, HID, NZ), BF16),
            pltpu.VMEM((2, 8, HID, NZ), BF16),
            pltpu.VMEM((3 * HID, 16 * NZ), BF16),
            pltpu.VMEM((2, ROWS, NZ), F32),
        ],
        compiler_params=params,
        name="backward",
    )(
        *scores,
        sbuf,
        hbuf,
        wide,
        *early,
    )

    body, far, beside, tail = sum_all(keep, send, me, count)
    weights = shaped((27, HID, HID), F32)
    stage = pltpu.VMEM((2, 14, HID, HID), F32)
    near = pl.pallas_call(
        near_kernel,
        out_shape=(weights, weights, shaped((2, HID, HID), F32)),
        in_specs=[vmem] * 2,
        out_specs=(hbm, hbm, vmem),
        scratch_shapes=[stage, pltpu.SemaphoreType.DMA((4,))],
        compiler_params=params,
        name="near",
    )(body, far)
    near, beside = lax.optimization_barrier((near, beside))
    half_b, half_c, extra = near
    grad_b, grad_c, grad_a = pl.pallas_call(
        finish_kernel,
        out_shape=(weights, weights, shaped((3, 27, HID), F32)),
        in_specs=[vmem] * 3 + [hbm] * 2,
        out_specs=(hbm, hbm, hbm),
        scratch_shapes=[
            stage,
            pltpu.VMEM((112, HID), F32),
            pltpu.VMEM((3, 27, HID), F32),
            pltpu.SemaphoreType.DMA((5,)),
        ],
        input_output_aliases={3: 0, 4: 1},
        compiler_params=params,
        name="finish",
    )(beside, partner(beside, 1, count), extra, half_b, half_c)
    return (
        pressure,
        tail[2, :1],
        grad_a.transpose(1, 2, 0),
        tail[0, :HID],
        grad_b,
        tail[0, HID:],
        grad_c,
        tail[1, :HID],
        tail[1, HID:],
    )


def solution(mesh):
    grid = P(("grp", "gx"), "gy", None)
    part = P("grp")
    stack = P("grp", None, None)
    return jax.shard_map(
        on_device,
        mesh=mesh,
        in_specs=(P(None, ("grp", "gx"), "gy", None), part, grid, grid) + (P(),) * 9,
        out_specs=(grid, part, stack, part, stack, part, stack, part, part),
        check_vma=False,
    )
```

```python
import functools

import jax
import jax.numpy as jnp
from jax import lax
from jax.experimental import pallas as pl
from jax.experimental.pallas import tpu as pltpu
from jax.sharding import PartitionSpec as P

F32 = jnp.float32
BF16 = jnp.bfloat16
AXES = ("gx", "gy")
HID = 64
NZ = 128
NY = 16
YY = NY + 2
PLANES = 12
MID = 5
FRAME = 12
WROWS = 864
ROWS = 896
SPLIT = 4
VMEM_LIMIT = 24 * 1024 * 1024
S1, S2, S3, HEAD, LOSS, S_BLOCKS = 0, 24, 72, 132, 133, 134
H1, H2, X0, WB, WC, H_BLOCKS = 0, 48, 96, 108, 144, 180


def shift_right(v):
    lane = lax.broadcasted_iota(jnp.int32, v.shape, v.ndim - 1)
    return jnp.where(lane == 0, 0.0, pltpu.roll(v, 1, v.ndim - 1))


def shift_left(v):
    lane = lax.broadcasted_iota(jnp.int32, v.shape, v.ndim - 1)
    return jnp.where(lane == NZ - 1, 0.0, pltpu.roll(v, NZ - 1, v.ndim - 1))


def dot_nn(a, b):
    return jnp.dot(a, b, preferred_element_type=F32)


def dot_nt(a, b):
    return lax.dot_general(a, b, (((1,), (1,)), ((), ())), preferred_element_type=F32)


def taps(src, X, y):
    out = []
    for a in range(3):
        for b in range(3):
            out.append(
                jnp.concatenate([src[X + a - 1, y + b - 1], src[X + a - 1, y + b]], axis=1)
            )
    return jnp.concatenate(out, axis=0)


def pair_taps(src, X, y, n):
    out = []
    for b in range(3):
        for x in range(4):
            rows = [src[X + x - 1, y + b - 1 + k] for k in range(n)]
            out.append(jnp.concatenate(rows, axis=1) if n > 1 else rows[0])
    return jnp.concatenate(out, axis=0)


def row_groups(count):
    return [(j, min(2, count - j)) for j in range(0, count, 2)]


def lane_taps(Y, d, k):
    part = Y[d * 3 * HID : (d + 1) * 3 * HID, k * NZ : (k + 1) * NZ]
    return part[HID : 2 * HID] + shift_right(part[:HID]) + shift_left(part[2 * HID :])


def activate(z):
    sig = 0.5 * jnp.tanh(0.5 * z) + 0.5
    return z * sig, sig


def slope_of(z, sig):
    return sig * (1.0 + z * (1.0 - sig))


def payload_kernel(fields_hbm, liquid_hbm, class_hbm, out_ref, fields, liquid, classes, rows, sems):
    copies = [
        pltpu.make_async_copy(src, dst, sems.at[i])
        for i, (src, dst) in enumerate(
            ((fields_hbm, fields), (liquid_hbm, liquid), (class_hbm, classes))
        )
    ]
    for copy in copies:
        copy.start()
    for copy in copies:
        copy.wait()
    for x in range(2):
        planes = (fields[0, x], fields[1, x], liquid[x], classes[x])
        for p, plane in enumerate(planes):
            plane = plane.astype(F32)
            for y in range(8):
                rows[x, y, p : p + 1, :] = plane[y : y + 1]
    out_ref[...] = rows[...].astype(BF16)


def conv_lhs(w, fwd, bwd):
    zero = jnp.zeros((HID, HID), F32)
    for b in range(3):
        for e in range(3):
            ahead = [w[9 * a + 3 * b + e].astype(F32) for a in range(3)]
            back = [w[26 - (9 * a + 3 * b + e)].astype(F32) for a in range(3)]
            for d in range(2):
                for half in range(2):
                    low, high = 2 * half - d, 2 * half + 1 - d
                    rows = slice((3 * d + e) * HID, (3 * d + e + 1) * HID)
                    tile = 2 * b + half
                    pick = [
                        [v[a] if 0 <= a <= 2 else zero for a in (low, high)] for v in (ahead, back)
                    ]
                    fwd[rows, tile * NZ : (tile + 1) * NZ] = jnp.concatenate(
                        pick[0], axis=1
                    ).astype(BF16)
                    bwd[6 * tile + 3 * d + e] = jnp.concatenate(pick[1], axis=0).T.astype(BF16)


def second_lhs_kernel(wb_hbm, wa_hbm, fa, fb, tb, wb_ref, wa_ref, sems):
    copies = [
        pltpu.make_async_copy(src, dst, sems.at[i])
        for i, (src, dst) in enumerate(((wb_hbm, wb_ref), (wa_hbm, wa_ref)))
    ]
    for copy in copies:
        copy.start()
    for copy in copies:
        copy.wait()
    conv_lhs(wb_ref, fb, tb)
    tap = lax.broadcasted_iota(jnp.int32, (27, 144), 0)
    col = lax.broadcasted_iota(jnp.int32, (27, 144), 1)
    total = jnp.zeros((HID, 144), F32)
    for ch in range(3):
        spot = 16 * (tap // 3) + 4 * (tap - 3 * (tap // 3)) + ch
        pick = jnp.where(col == spot, 1.0, 0.0).astype(BF16)
        total += dot_nn(wa_ref[ch].astype(F32).T.astype(BF16), pick)
    fa[...] = total.astype(BF16)


def third_lhs_kernel(
    wc_hbm,
    ba_hbm,
    bb_hbm,
    bc_hbm,
    hw_hbm,
    home_hbm,
    invd_hbm,
    fc,
    tc,
    wide_ref,
    home_ref,
    invd_ref,
    wc_ref,
    ba_ref,
    bb_ref,
    bc_ref,
    hw_ref,
    sems,
):
    copies = [
        pltpu.make_async_copy(src, dst, sems.at[i])
        for i, (src, dst) in enumerate(
            (
                (wc_hbm, wc_ref),
                (ba_hbm, ba_ref),
                (bb_hbm, bb_ref),
                (bc_hbm, bc_ref),
                (hw_hbm, hw_ref),
                (home_hbm, home_ref),
                (invd_hbm, invd_ref),
            )
        )
    ]
    for copy in copies:
        copy.start()
    for copy in copies:
        copy.wait()
    for i, ref in enumerate((ba_ref, bb_ref, bc_ref, hw_ref)):
        wide_ref[i] = jnp.broadcast_to(ref[...].astype(F32), (NZ, HID)).T
    conv_lhs(wc_ref, fc, tc)


def forward_kernel(
    home_ref,
    invd_ref,
    hb_ref,
    mine_ref,
    other_ref,
    wa_ref,
    wb_ref,
    tb_ref,
    wc_ref,
    tc_ref,
    wide_ref,
    p_hbm,
    gs_out,
    sbuf,
    hbuf,
    p_out,
    sems,
    inv_ref,
    x0s,
    liq,
    scl,
    f1,
    h1,
    h2,
    h3o,
    pf,
    rs,
    *,
    n_slots,
    cells,
):
    gx = lax.axis_index("gx")
    gy = lax.axis_index("gy")
    for ref in (x0s, h1, h2):
        z = jnp.zeros(ref.shape[2:], ref.dtype)
        for X in range(PLANES):
            ref[X, 0] = z
            ref[X, NY + 1] = z
    for ref in (liq, scl, f1, pf, rs):
        for X in range(PLANES):
            ref[X] = jnp.zeros((YY, NZ), F32)
    for s in range(n_slots):
        inv_ref[home_ref[s]] = s

    def load_plane(X):
        xg = 2 * gx - MID + X
        ok = jnp.where((xg >= 0) & (xg < 2 * n_slots), 1.0, 0.0).astype(F32)
        xc = jnp.clip(xg, 0, 2 * n_slots - 1)
        home = xc // 2
        half = xc - 2 * home
        slot = inv_ref[home]
        row4 = lax.broadcasted_iota(jnp.int32, (4, NZ), 0)
        for i in range(NY):
            src = (mine_ref, other_ref)[i // 8]
            fb = src[slot, half, i % 8].astype(F32) * ok
            mb = src[home, half, i % 8].astype(F32)
            y = 8 * (gy if i < 8 else 1 - gy) + i % 8
            lq = mb[2:3] * ok
            base = jnp.where(row4 < 2, fb, jnp.where(row4 == 2, mb * ok, 0.0))
            k12 = jnp.concatenate(
                [shift_right(base), base, shift_left(base), jnp.zeros((4, NZ), F32)], axis=0
            )
            x0s[X, y + 1] = k12.astype(BF16)
            liq[X, pl.ds(y + 1, 1), :] = lq
            scl[X, pl.ds(y + 1, 1), :] = mb[3:4]
            f1[X, pl.ds(y + 1, 1), :] = fb[1:2]
        cl = scl[X, 1 : NY + 1, :]
        sc = jnp.zeros((NY, NZ), F32)
        for k in range(4):
            sc = jnp.where(cl == k, invd_ref[k], sc)
        scl[X, 1 : NY + 1, :] = sc * liq[X, 1 : NY + 1, :]

    def load_planes(i, c):
        for k in range(6):
            load_plane(6 * i + k)
        return c

    lax.fori_loop(0, PLANES // 6, load_planes, 0)

    def planes(count, body):
        def step(i, c):
            body(i)
            return c

        lax.fori_loop(0, count, step, 0)

    y4 = gy * 4 + 1

    def layer1(X, slot):
        for j in range(6):
            y = y4 + 2 * j
            Y = dot_nn(wa_ref[...], taps(x0s, X, y))
            for k in range(2):
                z = Y[:, k * NZ : (k + 1) * NZ] + wide_ref[0]
                m = liq[X, pl.ds(y + k, 1), :]
                act, sig = activate(z)
                h1[X, y + k] = (act * m).astype(BF16)
                if slot is not None:
                    sbuf[S1 + 12 * slot + 2 * j + k] = slope_of(z, sig) * m

    def layer1_side(i):
        for k in range(4):
            layer1(1 + 6 * i + k, None)

    planes(2, layer1_side)
    layer1(MID, 0)
    layer1(MID + 1, 1)

    y3 = gy * 5 + 1

    def layer2(X, slot):
        for j, n in row_groups(11):
            y = y3 + j
            Y = dot_nn(wb_ref[...], pair_taps(h1, X, y, n))
            for d in range(2):
                for k in range(n):
                    z = lane_taps(Y, d, k) + wide_ref[1]
                    m = liq[X + d, pl.ds(y + k, 1), :]
                    act, sig = activate(z)
                    h2[X + d, y + k] = (act * m).astype(BF16)
                    if slot is not None:
                        sbuf[S2 + 12 * (slot + d) + j + k] = slope_of(z, sig) * m

    for i in range(2):
        layer2(2 + 6 * i, None)
    for i in range(2):
        layer2(MID - 1 + 2 * i, 2 * i)

    y2 = gy * 6 + 1

    def layer3(i):
        X = MID - 2 + 2 * i
        for j in range(5):
            y = y2 + 2 * j
            Y = dot_nn(wc_ref[...], pair_taps(h2, X, y, 2))
            for d in range(2):
                for k in range(2):
                    z = lane_taps(Y, d, k) + wide_ref[2]
                    m = liq[X + d, pl.ds(y + k, 1), :]
                    act, sig = activate(z)
                    h3 = (act * m).astype(BF16)
                    score = jnp.sum(wide_ref[3] * h3.astype(F32), axis=0, keepdims=True)
                    pf[X + d, pl.ds(y + k, 1), :] = m * (score + hb_ref[0])
                    sbuf[S3 + 10 * (2 * i + d) + 2 * j + k] = slope_of(z, sig) * m
                    h3o[2 * i + d, 2 * j + k] = h3

    for i in range(3):
        layer3(i)

    def operator(val, X):
        v = val[X, 1 : NY + 1, :]
        s = scl[X, 1 : NY + 1, :]
        q = liq[X, 1 : NY + 1, :]

        def term(nv, ns, nq):
            return 0.5 * (s * nq + ns * q) * (nv - v)

        total = term(val[X + 1, 1 : NY + 1, :], scl[X + 1, 1 : NY + 1, :], liq[X + 1, 1 : NY + 1, :])
        total += term(val[X - 1, 1 : NY + 1, :], scl[X - 1, 1 : NY + 1, :], liq[X - 1, 1 : NY + 1, :])
        total += term(val[X, 2 : NY + 2, :], scl[X, 2 : NY + 2, :], liq[X, 2 : NY + 2, :])
        total += term(val[X, 0:NY, :], scl[X, 0:NY, :], liq[X, 0:NY, :])
        total += term(shift_left(v), shift_left(s), shift_left(q))
        total += term(shift_right(v), shift_right(s), shift_right(q))
        return total

    for X in range(MID - 1, MID + 3):
        rs[X, 1 : NY + 1, :] = operator(pf, X) - liq[X, 1 : NY + 1, :] * f1[X, 1 : NY + 1, :]
    own_y = pl.ds(pl.multiple_of(gy * 8, 8) + 1, 8)
    loss = jnp.zeros((8, NZ), F32)
    for k in range(2):
        p_out[k] = pf[MID + k, own_y, :]
        r = rs[MID + k, own_y, :]
        loss += r * r
    leave = pltpu.make_async_copy(p_out, p_hbm, sems.at[0])
    leave.start()
    sbuf[LOSS, 0:8, :] = loss * (1.0 / cells)
    for X in range(MID - 1, MID + 3):
        rs[X] = rs[X] * (2.0 / cells)
    for k in range(2):
        X = MID + k
        pf[k, 1 : NY + 1, :] = liq[X, 1 : NY + 1, :] * operator(rs, X)
    for k in range(2):
        gs_out[k] = pf[k, own_y, :]

    head = jnp.zeros((HID, NZ), F32)
    for i in range(16):
        X, dy = i // 8, i % 8
        head += pf[X, pl.ds(gy * 8 + 1 + dy, 1), :] * h3o[2 + X, gy * 2 + dy].astype(F32)
    sbuf[HEAD] = head

    f0 = gy * 6

    def copy_out(i):
        for l in range(FRAME):
            r = (l % 4) * 16
            hbuf[X0 + 3 * i + l // 4, r : r + 16, :] = x0s[MID - 1 + i, f0 + l]
            hbuf[H1 + FRAME * i + l] = h1[MID - 1 + i, f0 + l]
            hbuf[H2 + FRAME * i + l] = h2[MID - 1 + i, f0 + l]

    for i in range(4):
        copy_out(i)
    for r in range(36):
        hbuf[WB + r] = tb_ref[r]
        hbuf[WC + r] = tc_ref[r]
    leave.wait()


def stack_gradient(raw, gcat, cols):
    g = raw.astype(F32)
    gcat[0:HID, cols] = shift_left(g).astype(BF16)
    gcat[HID : 2 * HID, cols] = raw
    gcat[2 * HID : 3 * HID, cols] = shift_right(g).astype(BF16)
    return g


def store_weights(W, ref):
    for a in range(3):
        for b in range(3):
            for e in range(3):
                t = 9 * a + 3 * b + e
                k = 3 * a + b
                blk = W[e * HID : (e + 1) * HID, k * HID : (k + 1) * HID]
                ref[t * 32 : (t + 1) * 32, 0:HID] = blk[:32]
                ref[t * 32 : (t + 1) * 32, HID:NZ] = blk[32:]


def channel_sums(first, second):
    rows = [jnp.sum(v, axis=1, keepdims=True).reshape(1, HID) for v in (first, second)]
    return jnp.concatenate(rows, axis=1)


def early_kernel(score_ref, sbuf, hbuf, wide_ref, gc_ref, bias_ref, cat_ref, gcat, hcat):
    gy = lax.axis_index("gy")
    own = gy * 2 + 1
    bias = jnp.zeros((HID, NZ), F32)
    for i in range(16):
        X, dy = i // 8, i % 8
        y = own + dy
        g = score_ref[X, dy : dy + 1, :]
        raw = (g * wide_ref[3] * sbuf[S3 + 10 * (X + 2) + y - 1]).astype(BF16)
        cols = slice(i * NZ, (i + 1) * NZ)
        bias += stack_gradient(raw, gcat, cols)
        for a in range(3):
            for b in range(3):
                k = 3 * a + b
                row = FRAME * (X + a) + y + b - 1
                hcat[k * HID : (k + 1) * HID, cols] = hbuf[H2 + row]
                cat_ref[k * HID : (k + 1) * HID, cols] = hbuf[H1 + row]
                l = y + b - 1
                q = l // 4
                cat_ref[9 * HID + k * 16 : 9 * HID + (k + 1) * 16, cols] = hbuf[
                    X0 + 3 * (X + a) + q, pl.ds(pl.multiple_of((l - 4 * q) * 16, 16), 16), :
                ]
    store_weights(dot_nt(gcat[...], hcat[...]), gc_ref)
    loss = jnp.sum(jnp.sum(sbuf[LOSS, 0:8, :], axis=0, keepdims=True), axis=1, keepdims=True)
    bias_ref[...] = jnp.zeros((8, NZ), F32)
    bias_ref[1:2, :] = channel_sums(bias, sbuf[HEAD])
    bias_ref[2:3, :] = jnp.broadcast_to(loss, (1, NZ))


def backward_kernel(
    gm_ref,
    gmo_ref,
    p2_ref,
    p2o_ref,
    p1_ref,
    p1o_ref,
    sbuf,
    hbuf,
    wide_ref,
    gc_ref,
    bias_ref,
    cat_ref,
    keep_ref,
    send_ref,
    gs,
    g3,
    g2,
    g1,
    gcat,
    acc,
):
    gy = lax.axis_index("gy")
    even = lax.axis_index("gx") % 2 == 0
    own_half = pl.ds(pl.multiple_of(8 * gy, 8), 8)
    far_half = pl.ds(pl.multiple_of(8 - 8 * gy, 8), 8)
    for half, gm, p1, p2 in (
        (own_half, gm_ref, p1_ref, p2_ref),
        (far_half, gmo_ref, p1o_ref, p2o_ref),
    ):
        for k in range(2):
            gs[k, half, :] = jnp.where(even, p2[k], p1[k])
            gs[2 + k, half, :] = gm[k]
            gs[4 + k, half, :] = jnp.where(even, p1[k], p2[k])

    def lhs_at(base):
        tiles = [
            jnp.concatenate([hbuf[base + 6 * t + r] for r in range(6)], axis=0) for t in range(6)
        ]
        return jnp.concatenate(tiles, axis=1)

    for ref in (g3, g2):
        z = jnp.zeros((HID, NZ), BF16)
        for X in range(ref.shape[0]):
            ref[X, 0] = z
            ref[X, FRAME - 1] = z

    def back3(X):
        for j in range(10):
            g = gs[X, pl.ds(gy * 6 + j, 1), :]
            g3[X, j + 1] = (g * wide_ref[3] * sbuf[S3 + 10 * X + j]).astype(BF16)

    for X in range(6):
        back3(X)

    for X in range(2):
        for r in range(WROWS, ROWS, 8):
            acc[X, r : r + 8, :] = jnp.zeros((8, NZ), F32)
    own = gy * 2 + 1

    def back2(i):
        X = 2 * i
        for j, n in row_groups(9):
            y = 1 + gy + j
            Y = dot_nn(lhs_at(WC), pair_taps(g3, X + 1, y, n))
            for d in range(2):
                for k in range(n):
                    row = 2 * gy + j + k
                    g2[X + d, y + k] = (
                        lane_taps(Y, d, k) * sbuf[S2 + 12 * (X + d) + row]
                    ).astype(BF16)

    for i in range(2):
        back2(i)
    bias_b = jnp.zeros((HID, NZ), F32)
    for i in range(16):
        cols = slice(i * NZ, (i + 1) * NZ)
        bias_b += stack_gradient(g2[1 + i // 8, own + i % 8], gcat, cols)
    store_weights(dot_nt(gcat[...], cat_ref[0 : 9 * HID, :]), acc.at[0])

    for j in range(4):
        y = own + 2 * j
        Y = dot_nn(lhs_at(WB), pair_taps(g2, 1, y, 2))
        for d in range(2):
            for k in range(2):
                row = gy * 4 + 2 * j + k
                g1[d, 2 * j + k] = (lane_taps(Y, d, k) * sbuf[S1 + 12 * d + row]).astype(BF16)

    bias_a = jnp.zeros((HID, NZ), F32)
    for i in range(16):
        raw = g1[i // 8, i % 8]
        bias_a += raw.astype(F32)
        gcat[0:HID, i * NZ : (i + 1) * NZ] = raw
    A = dot_nt(cat_ref[9 * HID : 9 * HID + 144, :], gcat[0:HID, :])
    for k in range(8):
        blk = A[16 * k : 16 * k + 12]
        which, spot = k // 4, k % 4
        r0 = WROWS + 12 * (spot % 2)
        c0 = HID * (spot // 2)
        acc[which, r0 : r0 + 12, c0 : c0 + HID] = blk
    acc[1, WROWS + 24 : WROWS + 32, 0:HID] = A[128:136]
    acc[1, WROWS + 24 : WROWS + 28, HID:NZ] = A[136:140]
    acc[1, 0:WROWS, :] = gc_ref[...]
    keep_ref[0:ROWS] = acc[gy]
    send_ref[0:ROWS] = acc[1 - gy]
    sums = channel_sums(bias_a, bias_b)
    for ref in (keep_ref, send_ref):
        ref[ROWS : ROWS + 8, :] = bias_ref[...]
        ref[ROWS : ROWS + 1, :] = sums


def unpack_half(half, mine_ref, far_ref, stage, gb_hbm, gc_hbm, sems):
    gy = lax.axis_index("gy")
    for ref, which in ((mine_ref, gy), (far_ref, 1 - gy)):
        for j in range(14):
            v = ref[32 * j : 32 * j + 32].astype(F32)
            stage[which, j, 0:32, :] = v[:, :HID]
            stage[which, j, 32:HID, :] = v[:, HID:]
    most = [
        pltpu.make_async_copy(stage.at[i, pl.ds(0, 13)], dst.at[pl.ds(14 * half, 13)], sems.at[i])
        for i, dst in enumerate((gb_hbm, gc_hbm))
    ]
    rest = [
        pltpu.make_async_copy(stage.at[i, 13], dst.at[13], sems.at[2 + i])
        for i, dst in enumerate((gb_hbm, gc_hbm))
    ]
    for copy in most:
        copy.start()

    @pl.when(half == 0)
    def _():
        for copy in rest:
            copy.start()

    def finish():
        for copy in most:
            copy.wait()

        @pl.when(half == 0)
        def _():
            for copy in rest:
                copy.wait()

    return finish


def near_kernel(mine_ref, far_ref, gb_hbm, gc_hbm, extra_ref, stage, sems):
    half = lax.axis_index("gx") // (SPLIT // 2) % 2
    wait = unpack_half(half, mine_ref, far_ref, stage, gb_hbm, gc_hbm, sems)
    for i in range(2):
        extra_ref[i] = stage[i, 13]
    wait()


def finish_kernel(
    mine_ref, far_ref, extra_ref, gb_in, gc_in, gb_hbm, gc_hbm, ga_hbm, stage, first, ga_ref, sems
):
    half = 1 - lax.axis_index("gx") // (SPLIT // 2) % 2
    wait = unpack_half(half, mine_ref, far_ref, stage, gb_hbm, gc_hbm, sems)
    zero, one = [jnp.where(half == 1, stage[i, 13], extra_ref[i]) for i in range(2)]
    first[0:24] = zero[0:24]
    first[24:48] = zero[32:56]
    first[48:72] = one[0:24]
    first[72:96] = one[32:56]
    first[96:104] = one[24:32]
    first[104:108] = one[56:60]
    for ch in range(3):
        ga_ref[ch] = first[pl.ds(ch, 27, stride=4), :]
    last = pltpu.make_async_copy(ga_ref, ga_hbm, sems.at[4])
    last.start()
    wait()
    last.wait()


def partner(value, bit, count):
    return lax.ppermute(value, AXES, [(i, i ^ bit) for i in range(count)])


def gather_stage(value, bit, me, count):
    other = partner(value, bit, count)
    upper = (me & bit) != 0
    return jnp.where(upper, jnp.concatenate([other, value]), jnp.concatenate([value, other]))


def two_parts(v):
    high = rounded(v)
    return high, rounded(v - high)


def rounded(v):
    return lax.reduce_precision(v, 8, 7)


def sum_all(keep, send, me, count):
    total = keep + partner(send, 1, count)
    body, tail = total[:ROWS], total[ROWS:]
    half = ROWS // 2
    upper = (me & SPLIT) != 0
    high, low = two_parts(tail)
    away = lax.dynamic_slice_in_dim(body, jnp.where(upper, 0, half), half)
    sent = jnp.concatenate([rounded(away), high, low]).astype(BF16)
    got = partner(sent, SPLIT, count).astype(F32)
    body = lax.dynamic_slice_in_dim(body, jnp.where(upper, half, 0), half) + got[:half]
    tail = tail + got[half : half + 8] + got[half + 8 :]
    bit = 2
    while bit < count:
        if bit != SPLIT:
            high, low = two_parts(tail)
            body = rounded(body)
            sent = jnp.concatenate([body, high, low]).astype(BF16)
            got = partner(sent, bit, count).astype(F32)
            body = body + got[:half]
            tail = (high + low) + (got[half : half + 8] + got[half + 8 :])
        bit *= 2
    body = body.astype(BF16)
    beside = partner(body, SPLIT, count)
    far = partner(body, 1, count)
    return body, far, beside, tail


def on_device(
    loaded_fields,
    brick_home,
    liquid_mask,
    density_class,
    inverse_density,
    conv_a,
    bias_a,
    conv_b,
    bias_b,
    conv_c,
    bias_c,
    head_weight,
    head_bias,
):
    n_slots = lax.axis_size("gx")
    count = n_slots * lax.axis_size("gy")
    gx = lax.axis_index("gx")
    gy = lax.axis_index("gy")
    me = gx * 2 + gy
    cells = 2 * n_slots * NY * NZ
    smem = pl.BlockSpec(memory_space=pltpu.SMEM)
    vmem = pl.BlockSpec(memory_space=pltpu.VMEM)
    params = pltpu.CompilerParams(vmem_limit_bytes=VMEM_LIMIT)

    hbm = pl.BlockSpec(memory_space=pl.ANY)

    def shaped(shape, kind):
        return jax.ShapeDtypeStruct(shape, kind)

    def off_chip(v):
        return pltpu.with_memory_space_constraint(v, pltpu.HBM)

    block = pl.pallas_call(
        payload_kernel,
        out_shape=shaped((2, 8, 4, NZ), BF16),
        in_specs=[hbm] * 3,
        out_specs=vmem,
        scratch_shapes=[
            pltpu.VMEM((2, 2, 8, NZ), BF16),
            pltpu.VMEM((2, 8, NZ), jnp.int32),
            pltpu.VMEM((2, 8, NZ), jnp.int32),
            pltpu.VMEM((2, 8, 4, NZ), F32),
            pltpu.SemaphoreType.DMA((3,)),
        ],
        compiler_params=params,
        name="payload",
    )(*map(off_chip, (loaded_fields, liquid_mask, density_class)))
    lhs = shaped((6 * HID, 12 * HID), BF16)
    turned = shaped((36, HID, NZ), BF16)
    vector = pltpu.VMEM((1, HID), F32)

    def layouts2(args):
        return pl.pallas_call(
            second_lhs_kernel,
            out_shape=(shaped((HID, 144), BF16), lhs, turned),
            in_specs=[hbm] * 2,
            out_specs=(vmem,) * 3,
            scratch_shapes=[
                pltpu.VMEM((27, HID, HID), BF16),
                pltpu.VMEM((3, 27, HID), BF16),
                pltpu.SemaphoreType.DMA((2,)),
            ],
            compiler_params=params,
            name="lhs2",
        )(*map(off_chip, args))

    def layouts3(args):
        return pl.pallas_call(
            third_lhs_kernel,
            out_shape=(
                lhs,
                turned,
                shaped((4, HID, NZ), F32),
                pltpu.SMEM((n_slots,), jnp.int32),
                pltpu.SMEM((4,), F32),
            ),
            in_specs=[hbm] * 7,
            out_specs=(vmem,) * 3 + (smem,) * 2,
            scratch_shapes=[
                pltpu.VMEM((27, HID, HID), BF16),
                vector,
                vector,
                vector,
                pltpu.VMEM((1, HID), BF16),
                pltpu.SemaphoreType.DMA((7,)),
            ],
            compiler_params=params,
            name="lhs3",
        )(*map(off_chip, args))

    jobs = [
        (layouts2, (conv_b, conv_a.transpose(2, 0, 1))),
        (
            layouts3,
            (
                conv_c,
                *(v.reshape(1, HID) for v in (bias_a, bias_b, bias_c, head_weight)),
                brick_home,
                inverse_density,
            ),
        ),
    ]
    made = []
    mine = block[None]
    bit = 2
    while bit < count:
        if bit > 2 and jobs:
            job, args = jobs.pop(0)
            mine, args = lax.optimization_barrier((mine, args))
            results = job(args)
            mine = gather_stage(mine, bit, me, count)
            mine, results = lax.optimization_barrier((mine, results))
            made += results
        else:
            mine = gather_stage(mine, bit, me, count)
        bit *= 2
    for job, args in jobs:
        made += job(args)
    across = partner(mine, 1, count)
    wide = made[5]
    home, table = [pltpu.with_memory_space_constraint(v, pltpu.SMEM) for v in made[6:]]


    pressure, score, sbuf, hbuf = pl.pallas_call(
        functools.partial(forward_kernel, n_slots=n_slots, cells=cells),
        out_shape=(
            shaped((2, 8, NZ), F32),
            shaped((2, 8, NZ), F32),
            shaped((S_BLOCKS, HID, NZ), F32),
            shaped((H_BLOCKS, HID, NZ), BF16),
        ),
        in_specs=[smem] * 3 + [vmem] * 8,
        out_specs=(hbm,) + (vmem,) * 3,
        scratch_shapes=[
            pltpu.VMEM((2, 8, NZ), F32),
            pltpu.SemaphoreType.DMA((1,)),
            pltpu.SMEM((n_slots,), jnp.int32),
            pltpu.VMEM((PLANES, YY, 16, NZ), BF16),
            pltpu.VMEM((PLANES, YY, NZ), F32),
            pltpu.VMEM((PLANES, YY, NZ), F32),
            pltpu.VMEM((PLANES, YY, NZ), F32),
            pltpu.VMEM((PLANES, YY, HID, NZ), BF16),
            pltpu.VMEM((PLANES, YY, HID, NZ), BF16),
            pltpu.VMEM((6, 10, HID, NZ), BF16),
            pltpu.VMEM((PLANES, YY, NZ), F32),
            pltpu.VMEM((PLANES, YY, NZ), F32),
        ],
        compiler_params=params,
        name="forward",
    )(
        home,
        table,
        head_bias,
        mine,
        across,
        *made[:6],
    )

    swap2 = lax.ppermute(score, "gx", [(i, ((i + 1) ^ 1) - 1) for i in range(1, n_slots - 1)])
    swap1 = lax.ppermute(score, "gx", [(i, i ^ 1) for i in range(n_slots)])
    across_score = partner(score, 1, count)
    early = pl.pallas_call(
        early_kernel,
        out_shape=(
            shaped((WROWS, NZ), F32),
            shaped((8, NZ), F32),
            shaped((9 * HID + 144, 16 * NZ), BF16),
        ),
        in_specs=[vmem] * 4,
        out_specs=(vmem,) * 3,
        scratch_shapes=[
            pltpu.VMEM((3 * HID, 16 * NZ), BF16),
            pltpu.VMEM((9 * HID, 16 * NZ), BF16),
        ],
        compiler_params=params,
        name="early",
    )(score, sbuf, hbuf, wide)
    early, swap2, swap1 = lax.optimization_barrier((early, swap2, swap1))
    scores = [score, across_score]
    for value in (swap2, swap1):
        scores += [value, partner(value, 1, count)]

    keep, send = pl.pallas_call(
        backward_kernel,
        out_shape=(shaped((ROWS + 8, NZ), F32), shaped((ROWS + 8, NZ), F32)),
        in_specs=[vmem] * 12,
        out_specs=(vmem, vmem),
        scratch_shapes=[
            pltpu.VMEM((6, NY, NZ), F32),
            pltpu.VMEM((6, FRAME, HID, NZ), BF16),
            pltpu.VMEM((4, FRAME, HID, NZ), BF16),
            pltpu.VMEM((2, 8, HID, NZ), BF16),
            pltpu.VMEM((3 * HID, 16 * NZ), BF16),
            pltpu.VMEM((2, ROWS, NZ), F32),
        ],
        compiler_params=params,
        name="backward",
    )(
        *scores,
        sbuf,
        hbuf,
        wide,
        *early,
    )

    body, far, beside, tail = sum_all(keep, send, me, count)
    weights = shaped((27, HID, HID), F32)
    stage = pltpu.VMEM((2, 14, HID, HID), F32)
    near = pl.pallas_call(
        near_kernel,
        out_shape=(weights, weights, shaped((2, HID, HID), F32)),
        in_specs=[vmem] * 2,
        out_specs=(hbm, hbm, vmem),
        scratch_shapes=[stage, pltpu.SemaphoreType.DMA((4,))],
        compiler_params=params,
        name="near",
    )(body, far)
    near, beside = lax.optimization_barrier((near, beside))
    half_b, half_c, extra = near
    grad_b, grad_c, grad_a = pl.pallas_call(
        finish_kernel,
        out_shape=(weights, weights, shaped((3, 27, HID), F32)),
        in_specs=[vmem] * 3 + [hbm] * 2,
        out_specs=(hbm, hbm, hbm),
        scratch_shapes=[
            stage,
            pltpu.VMEM((112, HID), F32),
            pltpu.VMEM((3, 27, HID), F32),
            pltpu.SemaphoreType.DMA((5,)),
        ],
        input_output_aliases={3: 0, 4: 1},
        compiler_params=params,
        name="finish",
    )(beside, partner(beside, 1, count), extra, half_b, half_c)
    return (
        pressure,
        tail[2, :1],
        grad_a.transpose(1, 2, 0),
        tail[0, :HID],
        grad_b,
        tail[0, HID:],
        grad_c,
        tail[1, :HID],
        tail[1, HID:],
    )


def solution(mesh):
    grid = P(("grp", "gx"), "gy", None)
    part = P("grp")
    stack = P("grp", None, None)
    return jax.shard_map(
        on_device,
        mesh=mesh,
        in_specs=(P(None, ("grp", "gx"), "gy", None), part, grid, grid) + (P(),) * 9,
        out_specs=(grid, part, stack, part, stack, part, stack, part, part),
        check_vma=False,
    )
```

```python
import functools

import jax
import jax.numpy as jnp
from jax import lax
from jax.experimental import pallas as pl
from jax.experimental.pallas import tpu as pltpu
from jax.sharding import PartitionSpec as P

F32 = jnp.float32
BF16 = jnp.bfloat16
AXES = ("gx", "gy")
HID = 64
NZ = 128
NY = 16
YY = NY + 2
PLANES = 12
MID = 5
FRAME = 12
WROWS = 864
ROWS = 896
SPLIT = 4
VMEM_LIMIT = 24 * 1024 * 1024
S1, S2, S3, HEAD, LOSS, S_BLOCKS = 0, 24, 72, 132, 133, 134
H1, H2, X0, WB, WC, H_BLOCKS = 0, 48, 96, 108, 144, 180


def shift_right(v):
    lane = lax.broadcasted_iota(jnp.int32, v.shape, v.ndim - 1)
    return jnp.where(lane == 0, 0.0, pltpu.roll(v, 1, v.ndim - 1))


def shift_left(v):
    lane = lax.broadcasted_iota(jnp.int32, v.shape, v.ndim - 1)
    return jnp.where(lane == NZ - 1, 0.0, pltpu.roll(v, NZ - 1, v.ndim - 1))


def dot_nn(a, b):
    return jnp.dot(a, b, preferred_element_type=F32)


def dot_nt(a, b):
    return lax.dot_general(a, b, (((1,), (1,)), ((), ())), preferred_element_type=F32)


def taps(src, X, y):
    out = []
    for a in range(3):
        for b in range(3):
            out.append(
                jnp.concatenate([src[X + a - 1, y + b - 1], src[X + a - 1, y + b]], axis=1)
            )
    return jnp.concatenate(out, axis=0)


def pair_taps(src, X, y, n):
    out = []
    for b in range(3):
        for x in range(4):
            rows = [src[X + x - 1, y + b - 1 + k] for k in range(n)]
            out.append(jnp.concatenate(rows, axis=1) if n > 1 else rows[0])
    return jnp.concatenate(out, axis=0)


def row_groups(count):
    return [(j, min(2, count - j)) for j in range(0, count, 2)]


def lane_taps(Y, d, k):
    part = Y[d * 3 * HID : (d + 1) * 3 * HID, k * NZ : (k + 1) * NZ]
    return part[HID : 2 * HID] + shift_right(part[:HID]) + shift_left(part[2 * HID :])


def activate(z):
    sig = 0.5 * jnp.tanh(0.5 * z) + 0.5
    return z * sig, sig


def slope_of(z, sig):
    return sig * (1.0 + z * (1.0 - sig))


def payload_kernel(fields_hbm, liquid_hbm, class_hbm, out_ref, fields, liquid, classes, rows, sems):
    copies = [
        pltpu.make_async_copy(src, dst, sems.at[i])
        for i, (src, dst) in enumerate(
            ((fields_hbm, fields), (liquid_hbm, liquid), (class_hbm, classes))
        )
    ]
    for copy in copies:
        copy.start()
    for copy in copies:
        copy.wait()
    for x in range(2):
        planes = (fields[0, x], fields[1, x], liquid[x], classes[x])
        for p, plane in enumerate(planes):
            plane = plane.astype(F32)
            for y in range(8):
                rows[x, y, p : p + 1, :] = plane[y : y + 1]
    out_ref[...] = rows[...].astype(BF16)


def conv_lhs(w, fwd, bwd):
    zero = jnp.zeros((HID, HID), F32)
    for b in range(3):
        for e in range(3):
            ahead = [w[9 * a + 3 * b + e].astype(F32) for a in range(3)]
            back = [w[26 - (9 * a + 3 * b + e)].astype(F32) for a in range(3)]
            for d in range(2):
                for half in range(2):
                    low, high = 2 * half - d, 2 * half + 1 - d
                    rows = slice((3 * d + e) * HID, (3 * d + e + 1) * HID)
                    tile = 2 * b + half
                    pick = [
                        [v[a] if 0 <= a <= 2 else zero for a in (low, high)] for v in (ahead, back)
                    ]
                    fwd[rows, tile * NZ : (tile + 1) * NZ] = jnp.concatenate(
                        pick[0], axis=1
                    ).astype(BF16)
                    bwd[6 * tile + 3 * d + e] = jnp.concatenate(pick[1], axis=0).T.astype(BF16)


def second_lhs_kernel(wb_hbm, wa_hbm, fa, fb, tb, wb_ref, wa_ref, sems):
    copies = [
        pltpu.make_async_copy(src, dst, sems.at[i])
        for i, (src, dst) in enumerate(((wb_hbm, wb_ref), (wa_hbm, wa_ref)))
    ]
    for copy in copies:
        copy.start()
    for copy in copies:
        copy.wait()
    conv_lhs(wb_ref, fb, tb)
    tap = lax.broadcasted_iota(jnp.int32, (27, 144), 0)
    col = lax.broadcasted_iota(jnp.int32, (27, 144), 1)
    total = jnp.zeros((HID, 144), F32)
    for ch in range(3):
        spot = 16 * (tap // 3) + 4 * (tap - 3 * (tap // 3)) + ch
        pick = jnp.where(col == spot, 1.0, 0.0).astype(BF16)
        total += dot_nn(wa_ref[ch].astype(F32).T.astype(BF16), pick)
    fa[...] = total.astype(BF16)


def third_lhs_kernel(
    wc_hbm,
    ba_hbm,
    bb_hbm,
    bc_hbm,
    hw_hbm,
    home_hbm,
    invd_hbm,
    fc,
    tc,
    wide_ref,
    home_ref,
    invd_ref,
    wc_ref,
    ba_ref,
    bb_ref,
    bc_ref,
    hw_ref,
    sems,
):
    copies = [
        pltpu.make_async_copy(src, dst, sems.at[i])
        for i, (src, dst) in enumerate(
            (
                (wc_hbm, wc_ref),
                (ba_hbm, ba_ref),
                (bb_hbm, bb_ref),
                (bc_hbm, bc_ref),
                (hw_hbm, hw_ref),
                (home_hbm, home_ref),
                (invd_hbm, invd_ref),
            )
        )
    ]
    for copy in copies:
        copy.start()
    for copy in copies:
        copy.wait()
    for i, ref in enumerate((ba_ref, bb_ref, bc_ref, hw_ref)):
        wide_ref[i] = jnp.broadcast_to(ref[...].astype(F32), (NZ, HID)).T
    conv_lhs(wc_ref, fc, tc)


def forward_kernel(
    home_ref,
    invd_ref,
    hb_ref,
    mine_ref,
    other_ref,
    wa_ref,
    wb_ref,
    tb_ref,
    wc_ref,
    tc_ref,
    wide_ref,
    p_hbm,
    gs_out,
    sbuf,
    hbuf,
    p_out,
    sems,
    inv_ref,
    x0s,
    liq,
    scl,
    f1,
    h1,
    h2,
    h3o,
    pf,
    rs,
    *,
    n_slots,
    cells,
):
    gx = lax.axis_index("gx")
    gy = lax.axis_index("gy")
    for ref in (x0s, h1, h2):
        z = jnp.zeros(ref.shape[2:], ref.dtype)
        for X in range(PLANES):
            ref[X, 0] = z
            ref[X, NY + 1] = z
    for ref in (liq, scl, f1, pf, rs):
        for X in range(PLANES):
            ref[X] = jnp.zeros((YY, NZ), F32)
    for s in range(n_slots):
        inv_ref[home_ref[s]] = s

    def load_plane(X):
        xg = 2 * gx - MID + X
        ok = jnp.where((xg >= 0) & (xg < 2 * n_slots), 1.0, 0.0).astype(F32)
        xc = jnp.clip(xg, 0, 2 * n_slots - 1)
        home = xc // 2
        half = xc - 2 * home
        slot = inv_ref[home]
        row4 = lax.broadcasted_iota(jnp.int32, (4, NZ), 0)
        for i in range(NY):
            src = (mine_ref, other_ref)[i // 8]
            fb = src[slot, half, i % 8].astype(F32) * ok
            mb = src[home, half, i % 8].astype(F32)
            y = 8 * (gy if i < 8 else 1 - gy) + i % 8
            lq = mb[2:3] * ok
            base = jnp.where(row4 < 2, fb, jnp.where(row4 == 2, mb * ok, 0.0))
            k12 = jnp.concatenate(
                [shift_right(base), base, shift_left(base), jnp.zeros((4, NZ), F32)], axis=0
            )
            x0s[X, y + 1] = k12.astype(BF16)
            liq[X, pl.ds(y + 1, 1), :] = lq
            scl[X, pl.ds(y + 1, 1), :] = mb[3:4]
            f1[X, pl.ds(y + 1, 1), :] = fb[1:2]
        cl = scl[X, 1 : NY + 1, :]
        sc = jnp.zeros((NY, NZ), F32)
        for k in range(4):
            sc = jnp.where(cl == k, invd_ref[k], sc)
        scl[X, 1 : NY + 1, :] = sc * liq[X, 1 : NY + 1, :]

    def load_planes(i, c):
        for k in range(6):
            load_plane(6 * i + k)
        return c

    lax.fori_loop(0, PLANES // 6, load_planes, 0)

    def planes(count, body):
        def step(i, c):
            body(i)
            return c

        lax.fori_loop(0, count, step, 0)

    y4 = gy * 4 + 1

    def layer1(X, slot):
        for j in range(6):
            y = y4 + 2 * j
            Y = dot_nn(wa_ref[...], taps(x0s, X, y))
            for k in range(2):
                z = Y[:, k * NZ : (k + 1) * NZ] + wide_ref[0]
                m = liq[X, pl.ds(y + k, 1), :]
                act, sig = activate(z)
                h1[X, y + k] = (act * m).astype(BF16)
                if slot is not None:
                    sbuf[S1 + 12 * slot + 2 * j + k] = slope_of(z, sig) * m

    def layer1_side(i):
        for k in range(4):
            layer1(1 + 6 * i + k, None)

    for i in range(2):
        layer1_side(i)
    layer1(MID, 0)
    layer1(MID + 1, 1)

    y3 = gy * 5 + 1

    def layer2(X, slot):
        for j, n in row_groups(11):
            y = y3 + j
            Y = dot_nn(wb_ref[...], pair_taps(h1, X, y, n))
            for d in range(2):
                for k in range(n):
                    z = lane_taps(Y, d, k) + wide_ref[1]
                    m = liq[X + d, pl.ds(y + k, 1), :]
                    act, sig = activate(z)
                    h2[X + d, y + k] = (act * m).astype(BF16)
                    if slot is not None:
                        sbuf[S2 + 12 * (slot + d) + j + k] = slope_of(z, sig) * m

    for i in range(2):
        layer2(2 + 6 * i, None)
    for i in range(2):
        layer2(MID - 1 + 2 * i, 2 * i)

    y2 = gy * 6 + 1

    def layer3(i):
        X = MID - 2 + 2 * i
        for j in range(5):
            y = y2 + 2 * j
            Y = dot_nn(wc_ref[...], pair_taps(h2, X, y, 2))
            for d in range(2):
                for k in range(2):
                    z = lane_taps(Y, d, k) + wide_ref[2]
                    m = liq[X + d, pl.ds(y + k, 1), :]
                    act, sig = activate(z)
                    h3 = (act * m).astype(BF16)
                    score = jnp.sum(wide_ref[3] * h3.astype(F32), axis=0, keepdims=True)
                    pf[X + d, pl.ds(y + k, 1), :] = m * (score + hb_ref[0])
                    sbuf[S3 + 10 * (2 * i + d) + 2 * j + k] = slope_of(z, sig) * m
                    h3o[2 * i + d, 2 * j + k] = h3

    for i in range(3):
        layer3(i)

    def operator(val, X):
        v = val[X, 1 : NY + 1, :]
        s = scl[X, 1 : NY + 1, :]
        q = liq[X, 1 : NY + 1, :]

        def term(nv, ns, nq):
            return 0.5 * (s * nq + ns * q) * (nv - v)

        total = term(val[X + 1, 1 : NY + 1, :], scl[X + 1, 1 : NY + 1, :], liq[X + 1, 1 : NY + 1, :])
        total += term(val[X - 1, 1 : NY + 1, :], scl[X - 1, 1 : NY + 1, :], liq[X - 1, 1 : NY + 1, :])
        total += term(val[X, 2 : NY + 2, :], scl[X, 2 : NY + 2, :], liq[X, 2 : NY + 2, :])
        total += term(val[X, 0:NY, :], scl[X, 0:NY, :], liq[X, 0:NY, :])
        total += term(shift_left(v), shift_left(s), shift_left(q))
        total += term(shift_right(v), shift_right(s), shift_right(q))
        return total

    for X in range(MID - 1, MID + 3):
        rs[X, 1 : NY + 1, :] = operator(pf, X) - liq[X, 1 : NY + 1, :] * f1[X, 1 : NY + 1, :]
    own_y = pl.ds(pl.multiple_of(gy * 8, 8) + 1, 8)
    loss = jnp.zeros((8, NZ), F32)
    for k in range(2):
        p_out[k] = pf[MID + k, own_y, :]
        r = rs[MID + k, own_y, :]
        loss += r * r
    leave = pltpu.make_async_copy(p_out, p_hbm, sems.at[0])
    leave.start()
    sbuf[LOSS, 0:8, :] = loss * (1.0 / cells)
    for X in range(MID - 1, MID + 3):
        rs[X] = rs[X] * (2.0 / cells)
    for k in range(2):
        X = MID + k
        pf[k, 1 : NY + 1, :] = liq[X, 1 : NY + 1, :] * operator(rs, X)
    for k in range(2):
        gs_out[k] = pf[k, own_y, :]

    head = jnp.zeros((HID, NZ), F32)
    for i in range(16):
        X, dy = i // 8, i % 8
        head += pf[X, pl.ds(gy * 8 + 1 + dy, 1), :] * h3o[2 + X, gy * 2 + dy].astype(F32)
    sbuf[HEAD] = head

    f0 = gy * 6

    def copy_out(i):
        for l in range(FRAME):
            r = (l % 4) * 16
            hbuf[X0 + 3 * i + l // 4, r : r + 16, :] = x0s[MID - 1 + i, f0 + l]
            hbuf[H1 + FRAME * i + l] = h1[MID - 1 + i, f0 + l]
            hbuf[H2 + FRAME * i + l] = h2[MID - 1 + i, f0 + l]

    for i in range(4):
        copy_out(i)
    for r in range(36):
        hbuf[WB + r] = tb_ref[r]
        hbuf[WC + r] = tc_ref[r]
    leave.wait()


def stack_gradient(raw, gcat, cols):
    g = raw.astype(F32)
    gcat[0:HID, cols] = shift_left(g).astype(BF16)
    gcat[HID : 2 * HID, cols] = raw
    gcat[2 * HID : 3 * HID, cols] = shift_right(g).astype(BF16)
    return g


def store_weights(W, ref):
    for a in range(3):
        for b in range(3):
            for e in range(3):
                t = 9 * a + 3 * b + e
                k = 3 * a + b
                blk = W[e * HID : (e + 1) * HID, k * HID : (k + 1) * HID]
                ref[t * 32 : (t + 1) * 32, 0:HID] = blk[:32]
                ref[t * 32 : (t + 1) * 32, HID:NZ] = blk[32:]


def channel_sums(first, second):
    rows = [jnp.sum(v, axis=1, keepdims=True).reshape(1, HID) for v in (first, second)]
    return jnp.concatenate(rows, axis=1)


def early_kernel(score_ref, sbuf, hbuf, wide_ref, gc_ref, bias_ref, cat_ref, gcat, hcat):
    gy = lax.axis_index("gy")
    own = gy * 2 + 1
    bias = jnp.zeros((HID, NZ), F32)
    for i in range(16):
        X, dy = i // 8, i % 8
        y = own + dy
        g = score_ref[X, dy : dy + 1, :]
        raw = (g * wide_ref[3] * sbuf[S3 + 10 * (X + 2) + y - 1]).astype(BF16)
        cols = slice(i * NZ, (i + 1) * NZ)
        bias += stack_gradient(raw, gcat, cols)
        for a in range(3):
            for b in range(3):
                k = 3 * a + b
                row = FRAME * (X + a) + y + b - 1
                hcat[k * HID : (k + 1) * HID, cols] = hbuf[H2 + row]
                cat_ref[k * HID : (k + 1) * HID, cols] = hbuf[H1 + row]
                l = y + b - 1
                q = l // 4
                cat_ref[9 * HID + k * 16 : 9 * HID + (k + 1) * 16, cols] = hbuf[
                    X0 + 3 * (X + a) + q, pl.ds(pl.multiple_of((l - 4 * q) * 16, 16), 16), :
                ]
    store_weights(dot_nt(gcat[...], hcat[...]), gc_ref)
    loss = jnp.sum(jnp.sum(sbuf[LOSS, 0:8, :], axis=0, keepdims=True), axis=1, keepdims=True)
    bias_ref[...] = jnp.zeros((8, NZ), F32)
    bias_ref[1:2, :] = channel_sums(bias, sbuf[HEAD])
    bias_ref[2:3, :] = jnp.broadcast_to(loss, (1, NZ))


def backward_kernel(
    gm_ref,
    gmo_ref,
    p2_ref,
    p2o_ref,
    p1_ref,
    p1o_ref,
    sbuf,
    hbuf,
    wide_ref,
    gc_ref,
    bias_ref,
    cat_ref,
    keep_ref,
    send_ref,
    gs,
    g3,
    g2,
    g1,
    gcat,
    acc,
):
    gy = lax.axis_index("gy")
    even = lax.axis_index("gx") % 2 == 0
    own_half = pl.ds(pl.multiple_of(8 * gy, 8), 8)
    far_half = pl.ds(pl.multiple_of(8 - 8 * gy, 8), 8)
    for half, gm, p1, p2 in (
        (own_half, gm_ref, p1_ref, p2_ref),
        (far_half, gmo_ref, p1o_ref, p2o_ref),
    ):
        for k in range(2):
            gs[k, half, :] = jnp.where(even, p2[k], p1[k])
            gs[2 + k, half, :] = gm[k]
            gs[4 + k, half, :] = jnp.where(even, p1[k], p2[k])

    def lhs_at(base):
        tiles = [
            jnp.concatenate([hbuf[base + 6 * t + r] for r in range(6)], axis=0) for t in range(6)
        ]
        return jnp.concatenate(tiles, axis=1)

    for ref in (g3, g2):
        z = jnp.zeros((HID, NZ), BF16)
        for X in range(ref.shape[0]):
            ref[X, 0] = z
            ref[X, FRAME - 1] = z

    def back3(X):
        for j in range(10):
            g = gs[X, pl.ds(gy * 6 + j, 1), :]
            g3[X, j + 1] = (g * wide_ref[3] * sbuf[S3 + 10 * X + j]).astype(BF16)

    for X in range(6):
        back3(X)

    for X in range(2):
        for r in range(WROWS, ROWS, 8):
            acc[X, r : r + 8, :] = jnp.zeros((8, NZ), F32)
    own = gy * 2 + 1

    def back2(i):
        X = 2 * i
        for j, n in row_groups(9):
            y = 1 + gy + j
            Y = dot_nn(lhs_at(WC), pair_taps(g3, X + 1, y, n))
            for d in range(2):
                for k in range(n):
                    row = 2 * gy + j + k
                    g2[X + d, y + k] = (
                        lane_taps(Y, d, k) * sbuf[S2 + 12 * (X + d) + row]
                    ).astype(BF16)

    for i in range(2):
        back2(i)
    bias_b = jnp.zeros((HID, NZ), F32)
    for i in range(16):
        cols = slice(i * NZ, (i + 1) * NZ)
        bias_b += stack_gradient(g2[1 + i // 8, own + i % 8], gcat, cols)
    store_weights(dot_nt(gcat[...], cat_ref[0 : 9 * HID, :]), acc.at[0])

    for j in range(4):
        y = own + 2 * j
        Y = dot_nn(lhs_at(WB), pair_taps(g2, 1, y, 2))
        for d in range(2):
            for k in range(2):
                row = gy * 4 + 2 * j + k
                g1[d, 2 * j + k] = (lane_taps(Y, d, k) * sbuf[S1 + 12 * d + row]).astype(BF16)

    bias_a = jnp.zeros((HID, NZ), F32)
    for i in range(16):
        raw = g1[i // 8, i % 8]
        bias_a += raw.astype(F32)
        gcat[0:HID, i * NZ : (i + 1) * NZ] = raw
    A = dot_nt(cat_ref[9 * HID : 9 * HID + 144, :], gcat[0:HID, :])
    for k in range(8):
        blk = A[16 * k : 16 * k + 12]
        which, spot = k // 4, k % 4
        r0 = WROWS + 12 * (spot % 2)
        c0 = HID * (spot // 2)
        acc[which, r0 : r0 + 12, c0 : c0 + HID] = blk
    acc[1, WROWS + 24 : WROWS + 32, 0:HID] = A[128:136]
    acc[1, WROWS + 24 : WROWS + 28, HID:NZ] = A[136:140]
    acc[1, 0:WROWS, :] = gc_ref[...]
    keep_ref[0:ROWS] = acc[gy]
    send_ref[0:ROWS] = acc[1 - gy]
    sums = channel_sums(bias_a, bias_b)
    for ref in (keep_ref, send_ref):
        ref[ROWS : ROWS + 8, :] = bias_ref[...]
        ref[ROWS : ROWS + 1, :] = sums


def unpack_half(half, mine_ref, far_ref, stage, gb_hbm, gc_hbm, sems):
    gy = lax.axis_index("gy")
    for ref, which in ((mine_ref, gy), (far_ref, 1 - gy)):
        for j in range(14):
            v = ref[32 * j : 32 * j + 32].astype(F32)
            stage[which, j, 0:32, :] = v[:, :HID]
            stage[which, j, 32:HID, :] = v[:, HID:]
    most = [
        pltpu.make_async_copy(stage.at[i, pl.ds(0, 13)], dst.at[pl.ds(14 * half, 13)], sems.at[i])
        for i, dst in enumerate((gb_hbm, gc_hbm))
    ]
    rest = [
        pltpu.make_async_copy(stage.at[i, 13], dst.at[13], sems.at[2 + i])
        for i, dst in enumerate((gb_hbm, gc_hbm))
    ]
    for copy in most:
        copy.start()

    @pl.when(half == 0)
    def _():
        for copy in rest:
            copy.start()

    def finish():
        for copy in most:
            copy.wait()

        @pl.when(half == 0)
        def _():
            for copy in rest:
                copy.wait()

    return finish


def near_kernel(mine_ref, far_ref, gb_hbm, gc_hbm, extra_ref, stage, sems):
    half = lax.axis_index("gx") // (SPLIT // 2) % 2
    wait = unpack_half(half, mine_ref, far_ref, stage, gb_hbm, gc_hbm, sems)
    for i in range(2):
        extra_ref[i] = stage[i, 13]
    wait()


def finish_kernel(
    mine_ref, far_ref, extra_ref, gb_in, gc_in, gb_hbm, gc_hbm, ga_hbm, stage, first, ga_ref, sems
):
    half = 1 - lax.axis_index("gx") // (SPLIT // 2) % 2
    wait = unpack_half(half, mine_ref, far_ref, stage, gb_hbm, gc_hbm, sems)
    zero, one = [jnp.where(half == 1, stage[i, 13], extra_ref[i]) for i in range(2)]
    first[0:24] = zero[0:24]
    first[24:48] = zero[32:56]
    first[48:72] = one[0:24]
    first[72:96] = one[32:56]
    first[96:104] = one[24:32]
    first[104:108] = one[56:60]
    for ch in range(3):
        ga_ref[ch] = first[pl.ds(ch, 27, stride=4), :]
    last = pltpu.make_async_copy(ga_ref, ga_hbm, sems.at[4])
    last.start()
    wait()
    last.wait()


def partner(value, bit, count):
    return lax.ppermute(value, AXES, [(i, i ^ bit) for i in range(count)])


def gather_stage(value, bit, me, count):
    other = partner(value, bit, count)
    upper = (me & bit) != 0
    return jnp.where(upper, jnp.concatenate([other, value]), jnp.concatenate([value, other]))


def two_parts(v):
    high = rounded(v)
    return high, rounded(v - high)


def rounded(v):
    return lax.reduce_precision(v, 8, 7)


def sum_all(keep, send, me, count):
    total = keep + partner(send, 1, count)
    body, tail = total[:ROWS], total[ROWS:]
    half = ROWS // 2
    upper = (me & SPLIT) != 0
    high, low = two_parts(tail)
    away = lax.dynamic_slice_in_dim(body, jnp.where(upper, 0, half), half)
    sent = jnp.concatenate([rounded(away), high, low]).astype(BF16)
    got = partner(sent, SPLIT, count).astype(F32)
    body = lax.dynamic_slice_in_dim(body, jnp.where(upper, half, 0), half) + got[:half]
    tail = tail + got[half : half + 8] + got[half + 8 :]
    bit = 2
    while bit < count:
        if bit != SPLIT:
            high, low = two_parts(tail)
            body = rounded(body)
            sent = jnp.concatenate([body, high, low]).astype(BF16)
            got = partner(sent, bit, count).astype(F32)
            body = body + got[:half]
            tail = (high + low) + (got[half : half + 8] + got[half + 8 :])
        bit *= 2
    body = body.astype(BF16)
    beside = partner(body, SPLIT, count)
    far = partner(body, 1, count)
    return body, far, beside, tail


def on_device(
    loaded_fields,
    brick_home,
    liquid_mask,
    density_class,
    inverse_density,
    conv_a,
    bias_a,
    conv_b,
    bias_b,
    conv_c,
    bias_c,
    head_weight,
    head_bias,
):
    n_slots = lax.axis_size("gx")
    count = n_slots * lax.axis_size("gy")
    gx = lax.axis_index("gx")
    gy = lax.axis_index("gy")
    me = gx * 2 + gy
    cells = 2 * n_slots * NY * NZ
    smem = pl.BlockSpec(memory_space=pltpu.SMEM)
    vmem = pl.BlockSpec(memory_space=pltpu.VMEM)
    params = pltpu.CompilerParams(vmem_limit_bytes=VMEM_LIMIT)

    hbm = pl.BlockSpec(memory_space=pl.ANY)

    def shaped(shape, kind):
        return jax.ShapeDtypeStruct(shape, kind)

    def off_chip(v):
        return pltpu.with_memory_space_constraint(v, pltpu.HBM)

    block = pl.pallas_call(
        payload_kernel,
        out_shape=shaped((2, 8, 4, NZ), BF16),
        in_specs=[hbm] * 3,
        out_specs=vmem,
        scratch_shapes=[
            pltpu.VMEM((2, 2, 8, NZ), BF16),
            pltpu.VMEM((2, 8, NZ), jnp.int32),
            pltpu.VMEM((2, 8, NZ), jnp.int32),
            pltpu.VMEM((2, 8, 4, NZ), F32),
            pltpu.SemaphoreType.DMA((3,)),
        ],
        compiler_params=params,
        name="payload",
    )(*map(off_chip, (loaded_fields, liquid_mask, density_class)))
    lhs = shaped((6 * HID, 12 * HID), BF16)
    turned = shaped((36, HID, NZ), BF16)
    vector = pltpu.VMEM((1, HID), F32)

    def layouts2(args):
        return pl.pallas_call(
            second_lhs_kernel,
            out_shape=(shaped((HID, 144), BF16), lhs, turned),
            in_specs=[hbm] * 2,
            out_specs=(vmem,) * 3,
            scratch_shapes=[
                pltpu.VMEM((27, HID, HID), BF16),
                pltpu.VMEM((3, 27, HID), BF16),
                pltpu.SemaphoreType.DMA((2,)),
            ],
            compiler_params=params,
            name="lhs2",
        )(*map(off_chip, args))

    def layouts3(args):
        return pl.pallas_call(
            third_lhs_kernel,
            out_shape=(
                lhs,
                turned,
                shaped((4, HID, NZ), F32),
                pltpu.SMEM((n_slots,), jnp.int32),
                pltpu.SMEM((4,), F32),
            ),
            in_specs=[hbm] * 7,
            out_specs=(vmem,) * 3 + (smem,) * 2,
            scratch_shapes=[
                pltpu.VMEM((27, HID, HID), BF16),
                vector,
                vector,
                vector,
                pltpu.VMEM((1, HID), BF16),
                pltpu.SemaphoreType.DMA((7,)),
            ],
            compiler_params=params,
            name="lhs3",
        )(*map(off_chip, args))

    jobs = [
        (layouts2, (conv_b, conv_a.transpose(2, 0, 1))),
        (
            layouts3,
            (
                conv_c,
                *(v.reshape(1, HID) for v in (bias_a, bias_b, bias_c, head_weight)),
                brick_home,
                inverse_density,
            ),
        ),
    ]
    made = []
    mine = block[None]
    bit = 2
    while bit < count:
        if bit > 2 and jobs:
            job, args = jobs.pop(0)
            mine, args = lax.optimization_barrier((mine, args))
            results = job(args)
            mine = gather_stage(mine, bit, me, count)
            mine, results = lax.optimization_barrier((mine, results))
            made += results
        else:
            mine = gather_stage(mine, bit, me, count)
        bit *= 2
    for job, args in jobs:
        made += job(args)
    across = partner(mine, 1, count)
    wide = made[5]
    home, table = [pltpu.with_memory_space_constraint(v, pltpu.SMEM) for v in made[6:]]


    pressure, score, sbuf, hbuf = pl.pallas_call(
        functools.partial(forward_kernel, n_slots=n_slots, cells=cells),
        out_shape=(
            shaped((2, 8, NZ), F32),
            shaped((2, 8, NZ), F32),
            shaped((S_BLOCKS, HID, NZ), F32),
            shaped((H_BLOCKS, HID, NZ), BF16),
        ),
        in_specs=[smem] * 3 + [vmem] * 8,
        out_specs=(hbm,) + (vmem,) * 3,
        scratch_shapes=[
            pltpu.VMEM((2, 8, NZ), F32),
            pltpu.SemaphoreType.DMA((1,)),
            pltpu.SMEM((n_slots,), jnp.int32),
            pltpu.VMEM((PLANES, YY, 16, NZ), BF16),
            pltpu.VMEM((PLANES, YY, NZ), F32),
            pltpu.VMEM((PLANES, YY, NZ), F32),
            pltpu.VMEM((PLANES, YY, NZ), F32),
            pltpu.VMEM((PLANES, YY, HID, NZ), BF16),
            pltpu.VMEM((PLANES, YY, HID, NZ), BF16),
            pltpu.VMEM((6, 10, HID, NZ), BF16),
            pltpu.VMEM((PLANES, YY, NZ), F32),
            pltpu.VMEM((PLANES, YY, NZ), F32),
        ],
        compiler_params=params,
        name="forward",
    )(
        home,
        table,
        head_bias,
        mine,
        across,
        *made[:6],
    )

    swap2 = lax.ppermute(score, "gx", [(i, ((i + 1) ^ 1) - 1) for i in range(1, n_slots - 1)])
    swap1 = lax.ppermute(score, "gx", [(i, i ^ 1) for i in range(n_slots)])
    across_score = partner(score, 1, count)
    early = pl.pallas_call(
        early_kernel,
        out_shape=(
            shaped((WROWS, NZ), F32),
            shaped((8, NZ), F32),
            shaped((9 * HID + 144, 16 * NZ), BF16),
        ),
        in_specs=[vmem] * 4,
        out_specs=(vmem,) * 3,
        scratch_shapes=[
            pltpu.VMEM((3 * HID, 16 * NZ), BF16),
            pltpu.VMEM((9 * HID, 16 * NZ), BF16),
        ],
        compiler_params=params,
        name="early",
    )(score, sbuf, hbuf, wide)
    early, swap2, swap1 = lax.optimization_barrier((early, swap2, swap1))
    scores = [score, across_score]
    for value in (swap2, swap1):
        scores += [value, partner(value, 1, count)]

    keep, send = pl.pallas_call(
        backward_kernel,
        out_shape=(shaped((ROWS + 8, NZ), F32), shaped((ROWS + 8, NZ), F32)),
        in_specs=[vmem] * 12,
        out_specs=(vmem, vmem),
        scratch_shapes=[
            pltpu.VMEM((6, NY, NZ), F32),
            pltpu.VMEM((6, FRAME, HID, NZ), BF16),
            pltpu.VMEM((4, FRAME, HID, NZ), BF16),
            pltpu.VMEM((2, 8, HID, NZ), BF16),
            pltpu.VMEM((3 * HID, 16 * NZ), BF16),
            pltpu.VMEM((2, ROWS, NZ), F32),
        ],
        compiler_params=params,
        name="backward",
    )(
        *scores,
        sbuf,
        hbuf,
        wide,
        *early,
    )

    body, far, beside, tail = sum_all(keep, send, me, count)
    weights = shaped((27, HID, HID), F32)
    stage = pltpu.VMEM((2, 14, HID, HID), F32)
    near = pl.pallas_call(
        near_kernel,
        out_shape=(weights, weights, shaped((2, HID, HID), F32)),
        in_specs=[vmem] * 2,
        out_specs=(hbm, hbm, vmem),
        scratch_shapes=[stage, pltpu.SemaphoreType.DMA((4,))],
        compiler_params=params,
        name="near",
    )(body, far)
    near, beside = lax.optimization_barrier((near, beside))
    half_b, half_c, extra = near
    grad_b, grad_c, grad_a = pl.pallas_call(
        finish_kernel,
        out_shape=(weights, weights, shaped((3, 27, HID), F32)),
        in_specs=[vmem] * 3 + [hbm] * 2,
        out_specs=(hbm, hbm, hbm),
        scratch_shapes=[
            stage,
            pltpu.VMEM((112, HID), F32),
            pltpu.VMEM((3, 27, HID), F32),
            pltpu.SemaphoreType.DMA((5,)),
        ],
        input_output_aliases={3: 0, 4: 1},
        compiler_params=params,
        name="finish",
    )(beside, partner(beside, 1, count), extra, half_b, half_c)
    return (
        pressure,
        tail[2, :1],
        grad_a.transpose(1, 2, 0),
        tail[0, :HID],
        grad_b,
        tail[0, HID:],
        grad_c,
        tail[1, :HID],
        tail[1, HID:],
    )


def solution(mesh):
    grid = P(("grp", "gx"), "gy", None)
    part = P("grp")
    stack = P("grp", None, None)
    return jax.shard_map(
        on_device,
        mesh=mesh,
        in_specs=(P(None, ("grp", "gx"), "gy", None), part, grid, grid) + (P(),) * 9,
        out_specs=(grid, part, stack, part, stack, part, stack, part, part),
        check_vma=False,
    )
```
